32 devices in a mesh: section: 2 (over core), gx: 4 (over z), gy: 4 (over y, x).
Axes of the slice: x: 2, y: 2, z: 4, core: 2. Of those that a mesh axis runs over, the one named last changes fastest.
Arguments:
- ends: bfloat16 [2, 32, 64, 64, 128], P('section', None, 'gx', 'gy'), may hold values from -9 to 9, as said below
- spectral_weight: bfloat16 [2, 32, 16, 32, 32, 32], P('section', 'gy', 'gx'), may hold values from -1 to 1
- point_weight: bfloat16 [2, 32, 32], P('section'), may hold values from -1 to 1
- point_bias: bfloat16 [2, 32], P('section'), may hold values from -3 to 3
Outputs:
- spectral_grad: float32 [2, 32, 16, 32, 32, 32], P('section', 'gy', 'gx')
- point_grad: float32 [2, 32, 32], P('section')
- bias_grad: float32 [2, 32], P('section')
The draws below stay inside these ranges and needn't reach their ends.
Inputs may be any that keep to these rules, and one draw needn't show every extreme that they name: `ends`: both slots are fields of order one with a smooth part made of low modes inside the retained range and a rough part that varies from cell to cell.
All inputs are finite; a program needn't handle non-finite values.
Results may differ from the reference program's by a relative error of at most 0.014.
Values may be sent and summed in bfloat16 or wider, within the bound.
No kernel may reach another device: no remote copies, remote signals or barrier semaphores. Data moves between devices by JAX's collectives and lax.ppermute only.
A program may use at most 128 MiB of HBM per device.

```python
import math
import jax
import jax.numpy as jnp
from jax import lax

C = 32
KX = 32
KY = 32
KZ = 16
NZ = 128
L = 2
NX = 64
NY = 64


def wave_table(count, length):
    modes = jnp.arange(count, dtype=jnp.int32)
    half = count // 2
    is_cos = modes < half
    wave = jnp.where(is_cos, modes, modes - half + 1)
    places = jnp.arange(length, dtype=jnp.int32)
    phase = wave[:, None] * places[None, :] % length
    angle = phase.astype(jnp.float32) * (2.0 * math.pi / length)
    return jnp.where(is_cos[:, None], jnp.cos(angle), jnp.sin(angle))


def draw_ends(key, part):
    key_rough = jax.random.fold_in(key, 11)
    key_coef = jax.random.fold_in(key, 12)
    shape = (2, C, NX, NY, NZ)
    places_x = jnp.arange(NX, dtype=jnp.int32)
    ramp = places_x.astype(jnp.float32) / NX
    level = 0.6 * math.sqrt(8.0 / (KX * KY * KZ))
    rough = jax.random.normal(key_rough, shape, jnp.float32) * 0.8
    envelope = 0.5 + 1.5 * ramp
    coef = jax.random.normal(key_coef, (2, C, KX, KY, KZ), jnp.float32) * level
    table_x = wave_table(KX, NX)
    table_y = wave_table(KY, NY)
    table_z = wave_table(KZ, NZ)
    high = lax.Precision.HIGHEST
    along_z = jnp.einsum('scjlk,kz->scjlz', coef, table_z, precision=high)
    along_y = jnp.einsum('scjlz,ly->scjyz', along_z, table_y, precision=high)
    smooth = jnp.einsum('scjyz,jx->scxyz', along_y, table_x, precision=high)
    total = (rough + smooth) * envelope[None, None, :, None, None]
    return jnp.clip(total, -9.0, 9.0).astype(jnp.bfloat16)


def block_scale(rng, shape, pieces, smallest, top_value):
    gain, own = 1.0, jax.random.fold_in(rng, 6)
    for dim, shards_of in pieces:
        steps = jnp.exp(jax.random.uniform(jax.random.fold_in(own, dim), (shards_of,), jnp.float32, smallest / len(pieces), top_value / len(pieces)))
        gain = gain * jnp.repeat(steps, shape[dim] // shards_of).reshape([-1 if axis == dim else 1 for axis in range(len(shape))])
    return gain


def gaussian(stream_key, extent, width, most, pieces=(), kind=jnp.bfloat16):
    drawn = jax.random.normal(stream_key, extent, jnp.float32) * width
    if len(pieces) > 0:
        drawn = block_scale(stream_key, extent, pieces, -0.22, 0.18) * drawn
    return jnp.clip(drawn, min=-most, max=most).astype(kind)


def setup_inputs(seed: int = 0) -> dict:
    splits = jax.random.split(jax.random.key(seed), 5)
    return {
        "ends": draw_ends(jax.random.fold_in(splits[4], 71), 0),
        "spectral_weight": gaussian(splits[1], (L, KX, KZ, KY, C, C), C ** -0.5, 1.0, ((0, 2), (1, 4), (2, 4))),
        "point_weight": gaussian(splits[2], (L, C, C), C ** -0.5, 1.0, ((0, 2),)),
        "point_bias": gaussian(splits[3], (L, C), 0.5, 3.0, ((0, 2),)),
    }


gelu_coef = 0.7978845608028654

def activate(pre):
    inner = gelu_coef * (pre + 0.044715 * pre * pre * pre)
    return 0.5 * pre * (1.0 + jnp.tanh(inner))

def activate_slope(pre):
    inner = gelu_coef * (pre + 0.044715 * pre * pre * pre)
    tanh_val = jnp.tanh(inner)
    return 0.5 * (1.0 + tanh_val) + 0.5 * pre * (1.0 - tanh_val * tanh_val) * gelu_coef * (1.0 + 3.0 * 0.044715 * pre * pre)

def basis_rows(modes, places, length, count):
    half = count // 2
    is_cos = modes < half
    wave = jnp.where(is_cos, modes, modes - half + 1)
    phase = wave[:, None] * places[None, :] % length
    angle = phase.astype(jnp.float32) * (2.0 * math.pi / length)
    values = jnp.where(is_cos[:, None], jnp.cos(angle), jnp.sin(angle))
    scale = jnp.where(is_cos & (wave == 0), math.sqrt(1.0 / length), math.sqrt(2.0 / length))
    return (values * scale[:, None]).astype(jnp.bfloat16)

def reference(ends, spectral_weight, point_weight, point_bias):
    f32 = jnp.float32
    bf16 = jnp.bfloat16
    basis_x = basis_rows(jnp.arange(KX, dtype=jnp.int32), jnp.arange(NX, dtype=jnp.int32), NX, KX).astype(f32)
    basis_y = basis_rows(jnp.arange(KY, dtype=jnp.int32), jnp.arange(NY, dtype=jnp.int32), NY, KY).astype(f32)
    basis_z = basis_rows(jnp.arange(KZ, dtype=jnp.int32), jnp.arange(NZ, dtype=jnp.int32), NZ, KZ).astype(f32)

    def analyse(values):
        first = jnp.einsum('cxyn,kn->cxyk', values.astype(f32), basis_z).astype(bf16)
        second = jnp.einsum('cnyk,jn->cjyk', first.astype(f32), basis_x).astype(bf16)
        return jnp.einsum('cjnk,ln->cjlk', second.astype(f32), basis_y).astype(bf16)

    def synthesise(spectrum):
        first = jnp.einsum('cjlk,ln->cjnk', spectrum.astype(f32), basis_y).astype(bf16)
        second = jnp.einsum('cjyk,jn->cnyk', first.astype(f32), basis_x).astype(bf16)
        return jnp.einsum('cxyk,kn->cxyn', second.astype(f32), basis_z)

    def layer(values, idx):
        spec_in = analyse(values)
        mixed = jnp.einsum('ijlk,jklio->ojlk', spec_in.astype(f32), spectral_weight[idx].astype(f32)).astype(bf16)
        back = synthesise(mixed)
        pre = jnp.einsum('io,ixyz->oxyz', point_weight[idx].astype(f32), values.astype(f32)) + back
        pre = pre + point_bias[idx].astype(f32)[:, None, None, None]
        return (spec_in, pre)
    fields = []
    values = ends[0]
    for idx in range(L):
        fields.append(values)
        spec_in, pre = layer(values, idx)
        values = activate(pre).astype(bf16)
    grad = ends[1]
    spec_grads = [None] * L
    point_grads = [None] * L
    bias_grads = [None] * L
    for idx in reversed(range(L)):
        spec_in, pre = layer(fields[idx], idx)
        slope = (grad.astype(f32) * activate_slope(pre)).astype(bf16)
        point_grads[idx] = jnp.einsum('ixyz,oxyz->io', fields[idx].astype(f32), slope.astype(f32))
        bias_grads[idx] = lax.optimization_barrier(jnp.sum(slope, axis=(1, 2, 3), dtype=f32))
        spec_out = analyse(slope)
        spec_grads[idx] = jnp.einsum('ijlk,ojlk->jklio', spec_in.astype(f32), spec_out.astype(f32))
        if idx > 0:
            turned = jnp.einsum('ojlk,jklio->ijlk', spec_out.astype(f32), spectral_weight[idx].astype(f32)).astype(bf16)
            back = synthesise(turned)
            grad = (jnp.einsum('io,oxyz->ixyz', point_weight[idx].astype(f32), slope.astype(f32)) + back).astype(bf16)
    return (jnp.stack(spec_grads), jnp.stack(point_grads), jnp.stack(bias_grads))
```

```python
import math

import jax
import jax.numpy as jnp
import ml_dtypes
import numpy as np
from jax import lax
from jax.experimental import pallas as pl
from jax.experimental.pallas import tpu as pltpu
from jax.sharding import PartitionSpec as P

gelu_coef = 0.7978845608028654
f32 = jnp.float32
bf16 = jnp.bfloat16
AXES = ("section", "gx", "gy")


def table(length, count):
    half = count // 2
    modes = np.arange(count)
    is_cos = modes < half
    wave = np.where(is_cos, modes, modes - half + 1)
    phase = wave[:, None] * np.arange(length)[None, :] % length
    angle = phase.astype(np.float32) * np.float32(2.0 * math.pi / length)
    values = np.where(is_cos[:, None], np.cos(angle), np.sin(angle)).astype(np.float32)
    scale = np.where(is_cos & (wave == 0), math.sqrt(1.0 / length), math.sqrt(2.0 / length))
    return (values * scale.astype(np.float32)[:, None]).astype(ml_dtypes.bfloat16).astype(np.float32)


def nn(a, b):
    return lax.dot_general(a, b, (((1,), (0,)), ((), ())), preferred_element_type=f32)


def nt(a, b):
    return lax.dot_general(a, b, (((1,), (1,)), ((), ())), preferred_element_type=f32)


def tn(a, b):
    return lax.dot_general(a, b, (((0,), (0,)), ((), ())), preferred_element_type=f32)


def iota(shape, dim):
    return lax.broadcasted_iota(jnp.int32, shape, dim)


def vmem(n):
    return [pl.BlockSpec(memory_space=pltpu.VMEM)] * n


params = pltpu.CompilerParams(vmem_limit_bytes=56 * 1024 * 1024)
smem = pl.BlockSpec(memory_space=pltpu.SMEM)
hbm = pl.BlockSpec(memory_space=pl.ANY)


class Sizes:
    def __init__(self, ends, weight):
        self.n_gx = lax.axis_size("gx")
        self.n_gy = lax.axis_size("gy")
        _, self.chans, self.len_x, full, self.depth = ends.shape
        self.len_y = full // 2
        _, self.blk_j, self.blk_k, self.modes_y, _, _ = weight.shape
        self.half_j = self.blk_j // 2
        self.jk = self.half_j * self.blk_k
        self.places = 2 * self.n_gx * self.n_gy
        self.modes = self.places * self.jk
        self.rows = self.chans * self.len_y
        self.cells = self.len_x * self.depth
        self.lines = 2 * self.n_gy
        self.cpl = 128 // self.len_y
        self.groups = self.rows // 128
        self.lgs = self.modes_y // 8
        self.full_x = self.len_x * self.n_gx
        self.full_y = full * self.n_gy


def mode_tables(sz):
    bx = table(sz.full_x, sz.blk_j * sz.n_gy)
    bz = table(sz.depth, sz.blk_k * sz.n_gx)
    by = table(sz.full_y, sz.modes_y)
    sec, gx, gy, jj, kk = np.meshgrid(
        np.arange(2), np.arange(sz.n_gx), np.arange(sz.n_gy), np.arange(sz.half_j), np.arange(sz.blk_k), indexing="ij"
    )
    row_j = (gy * sz.blk_j + sec * sz.half_j + jj).reshape(-1)
    row_k = (gx * sz.blk_k + kk).reshape(-1)
    sec, gy, yy = np.meshgrid(np.arange(2), np.arange(sz.n_gy), np.arange(sz.len_y), indexing="ij")
    row_y = (gy * 2 * sz.len_y + sec * sz.len_y + yy).reshape(-1)
    return bx[row_j], bz[row_k], np.repeat(by[:, row_y].T, sz.cpl, axis=1)


def activate(pre):
    inner = gelu_coef * (pre + 0.044715 * pre * pre * pre)
    tanh_val = jnp.tanh(inner)
    value = 0.5 * pre * (1.0 + tanh_val)
    slope = 0.5 * (1.0 + tanh_val) + 0.5 * pre * (1.0 - tanh_val * tanh_val) * gelu_coef * (
        1.0 + 3.0 * 0.044715 * pre * pre
    )
    return value, slope


def spread(sz):
    shape = (sz.rows, sz.chans)
    return (iota(shape, 0) // sz.len_y == iota(shape, 1)).astype(bf16)


def same_y(sz):
    shape = (sz.rows, sz.rows)
    return iota(shape, 0) % sz.len_y == iota(shape, 1) % sz.len_y


def point_matrix(sz, weight, forward):
    one = spread(sz)
    part = nt(one, weight) if forward else nn(one, weight)
    full = nt(part.astype(bf16), one)
    return jnp.where(same_y(sz), full, 0.0).astype(bf16)


def swapped(rows, half):
    return jnp.concatenate([rows[half:], rows[:half]], axis=0)


def send_analysis(sz, bb_ref, field, out_ref, layer):
    out = nt(bb_ref[...], field).astype(bf16)
    out_ref[...] = swapped(out, sz.modes // 2) if layer == 1 else out


def first_kernel(sz, s_ref, keep_ref, recv_ref, bx_ref, bz_ref, by_ref, bb_ref, ya_ref, out_ref):
    depth = sz.depth
    for x in range(sz.len_x):
        bb_ref[:, x * depth : (x + 1) * depth] = (bx_ref[:, x : x + 1] * bz_ref[...]).astype(bf16)
    wide = sz.modes_y * sz.cpl
    lane_c = iota((sz.len_y, wide), 1) % sz.cpl
    for g in range(sz.lines):
        part = by_ref[g * sz.len_y : (g + 1) * sz.len_y, :]
        block = jnp.concatenate([jnp.where(lane_c == c, part, 0.0) for c in range(sz.cpl)], axis=0)
        ya_ref[g * 128 : (g + 1) * 128, :] = block.astype(bf16)
    field = jnp.where(s_ref[0] == 0, keep_ref[...], recv_ref[...])
    send_analysis(sz, bb_ref, field, out_ref, 0)


def first_call(sz, s, keep, recv, bx, bz, by):
    return pl.pallas_call(
        lambda *refs: first_kernel(sz, *refs),
        out_shape=(
            jax.ShapeDtypeStruct((sz.modes, sz.cells), bf16),
            jax.ShapeDtypeStruct((sz.lines * 128, sz.modes_y * sz.cpl), bf16),
            jax.ShapeDtypeStruct((sz.modes, sz.rows), bf16),
        ),
        in_specs=[smem] + vmem(5),
        out_specs=tuple(vmem(3)),
        compiler_params=params,
        name="first",
    )(s, keep, recv, bx, bz, by)


def line_analysis(sz, r_ref, ya_ref):
    jk = sz.jk
    lines = []
    for sec in range(2):
        for gy in range(sz.n_gy):
            total = None
            for gx in range(sz.n_gx):
                at = ((sec * sz.n_gx + gx) * sz.n_gy + gy) * jk
                part = r_ref[at : at + jk, :].astype(f32)
                total = part if total is None else total + part
            lines.append(total.astype(bf16))
    halves = [
        jnp.concatenate([line[:, h * 128 : (h + 1) * 128] for line in lines], axis=1) for h in range(sz.groups)
    ]
    return nn(jnp.concatenate(halves, axis=0), ya_ref[...]).astype(bf16)


def diagonal(sz, count):
    shape = (count, sz.groups * 128)
    return iota(shape, 0) % 8 == (iota(shape, 1) % 128) // sz.cpl


def row_spread(sz):
    shape = (sz.jk * 8, sz.jk)
    return (iota(shape, 0) // 8 == iota(shape, 1)).astype(bf16)


def row_gather(sz):
    shape = (sz.jk, sz.jk * 8)
    return (iota(shape, 1) // 8 == iota(shape, 0)).astype(bf16)


def chan_lanes(sz):
    shape = (sz.groups * 128, sz.chans)
    lane = iota(shape, 0)
    return ((lane // 128) * sz.cpl + lane % sz.cpl == iota(shape, 1)).astype(bf16)


def to_blocks(sz, rows, lg):
    jk = sz.jk
    wide = jnp.concatenate(
        [rows[h * jk : (h + 1) * jk, lg * 128 : (lg + 1) * 128] for h in range(sz.groups)], axis=1
    )
    return jnp.where(diagonal(sz, jk * 8), nn(row_spread(sz), wide), 0.0)


def from_blocks(sz, blocks):
    jk = sz.jk
    pieces = []
    for block in blocks:
        kept = jnp.where(diagonal(sz, jk * 8), block, 0.0).astype(bf16)
        pieces.append(nn(row_gather(sz), kept).astype(bf16))
    return jnp.concatenate(
        [
            jnp.concatenate([piece[:, h * 128 : (h + 1) * 128] for piece in pieces], axis=1)
            for h in range(sz.groups)
        ],
        axis=0,
    )


def send_lines(sz, rows, ya_ref, out_ref):
    jk = sz.jk
    lines = nt(rows, ya_ref[...]).astype(bf16)
    for sec in range(2):
        for gy in range(sz.n_gy):
            line = sec * sz.n_gy + gy
            block = jnp.concatenate(
                [lines[h * jk : (h + 1) * jk, line * 128 : (line + 1) * 128] for h in range(sz.groups)], axis=1
            )
            for gx in range(sz.n_gx):
                at = ((sec * sz.n_gx + gx) * sz.n_gy + gy) * jk
                out_ref[at : at + jk, :] = block


def weight_block(sz, w_ref, jk, lg, h):
    jj, kk = jk // sz.blk_k, jk % sz.blk_k
    part = w_ref[jj, kk, lg * 8 : (lg + 1) * 8, h * sz.cpl : (h + 1) * sz.cpl, :]
    return part.reshape(128, sz.chans)


def mix_kernel(sz, layer, turn, s_ref, r_ref, ya_ref, own_ref, other_ref, spec_ref, out_ref, w_ref, blk_ref, mix_ref, sem):
    own = pltpu.make_async_copy(own_ref.at[0, pl.ds(0, sz.half_j)], w_ref, sem)
    other = pltpu.make_async_copy(other_ref, w_ref, sem)

    @pl.when(s_ref[0] == layer)
    def _():
        own.start()

    @pl.when(s_ref[0] != layer)
    def _():
        other.start()

    spec = line_analysis(sz, r_ref, ya_ref)
    spec_ref[...] = spec
    count = sz.jk * 8
    for lg in range(sz.lgs):
        blk_ref[lg * count : (lg + 1) * count, :] = to_blocks(sz, spec, lg)
    if turn:
        flat = nn(blk_ref[...].astype(bf16), chan_lanes(sz))
        blk_ref[:, : sz.chans] = flat
    other.wait()
    for lg in range(sz.lgs):
        for jk in range(sz.jk):
            at = (lg * sz.jk + jk) * 8
            if turn:
                left = blk_ref[at : at + 8, : sz.chans].astype(bf16)
                for h in range(sz.groups):
                    mix_ref[at : at + 8, h * 128 : (h + 1) * 128] = nt(left, weight_block(sz, w_ref, jk, lg, h))
            else:
                left = blk_ref[at : at + 8, :].astype(bf16)
                total = None
                for h in range(sz.groups):
                    part = nn(left[:, h * 128 : (h + 1) * 128], weight_block(sz, w_ref, jk, lg, h))
                    total = part if total is None else total + part
                mix_ref[at : at + 8, : sz.chans] = total
    blocks = []
    for lg in range(sz.lgs):
        if turn:
            blocks.append(mix_ref[lg * count : (lg + 1) * count, :])
        else:
            blocks.append(nt(mix_ref[lg * count : (lg + 1) * count, : sz.chans].astype(bf16), chan_lanes(sz)))
    send_lines(sz, from_blocks(sz, blocks), ya_ref, out_ref)


def mix_call(sz, layer, turn, s, r, ya, own, other):
    count = sz.jk * 8 * sz.lgs
    return pl.pallas_call(
        lambda *refs: mix_kernel(sz, layer, turn, *refs),
        out_shape=(
            jax.ShapeDtypeStruct((sz.groups * sz.jk, sz.modes_y * sz.cpl), bf16),
            jax.ShapeDtypeStruct((sz.modes, sz.rows), bf16),
        ),
        in_specs=[smem] + vmem(2) + [hbm, hbm],
        out_specs=tuple(vmem(2)),
        scratch_shapes=[
            pltpu.VMEM((sz.half_j, sz.blk_k, sz.modes_y, sz.chans, sz.chans), bf16),
            pltpu.VMEM((count, sz.groups * 128), f32),
            pltpu.VMEM((count, sz.groups * 128), f32),
            pltpu.SemaphoreType.DMA,
        ],
        compiler_params=params,
        name="mix",
    )(s, r, ya, own, other)


def spec_kernel(sz, r_ref, ya_ref, out_ref):
    out_ref[...] = line_analysis(sz, r_ref, ya_ref)


def spec_call(sz, r, ya):
    return pl.pallas_call(
        lambda *refs: spec_kernel(sz, *refs),
        out_shape=jax.ShapeDtypeStruct((sz.groups * sz.jk, sz.modes_y * sz.cpl), bf16),
        in_specs=vmem(2),
        out_specs=vmem(1)[0],
        compiler_params=params,
        name="spec",
    )(r, ya)


def turned_modes(sz, u_ref, layer):
    left = jnp.transpose(u_ref[...])
    half = sz.modes // 2
    if layer == 1:
        left = jnp.concatenate([left[:, half:], left[:, :half]], axis=1)
    return left


CHUNK = 256


def small_parts(sz, s_ref, own_ref, other_ref, layer):
    chosen = jnp.where(s_ref[0] == layer, own_ref[...].astype(f32), other_ref[...].astype(f32)).astype(bf16)
    return chosen[: sz.chans], chosen[sz.chans :]


def forward_kernel(sz, s_ref, keep_ref, recv_ref, u_ref, bb_ref, own_ref, other_ref, v_ref, slope_ref, out_ref):
    weight, bias = small_parts(sz, s_ref, own_ref, other_ref, 0)
    matrix = point_matrix(sz, weight, True)
    column = nt(spread(sz), bias)[:, :1]
    left = turned_modes(sz, u_ref, 0)
    for at in range(0, sz.cells, CHUNK):
        cut = slice(at, at + CHUNK)
        field = jnp.where(s_ref[0] == 0, keep_ref[:, cut], recv_ref[:, cut])
        pre = nn(left, bb_ref[:, cut]) + nn(matrix, field) + column
        value, slope = activate(pre)
        v_ref[:, cut] = value.astype(bf16)
        slope_ref[:, cut] = slope
    send_analysis(sz, bb_ref, v_ref[...], out_ref, 1)


def forward_call(sz, s, keep, recv, u, bb, own, other):
    return pl.pallas_call(
        lambda *refs: forward_kernel(sz, *refs),
        out_shape=(
            jax.ShapeDtypeStruct((sz.rows, sz.cells), bf16),
            jax.ShapeDtypeStruct((sz.rows, sz.cells), f32),
            jax.ShapeDtypeStruct((sz.modes, sz.rows), bf16),
        ),
        in_specs=[smem] + vmem(6),
        out_specs=tuple(vmem(3)),
        compiler_params=params,
        name="forward",
    )(s, keep, recv, u, bb, own, other)


def turn_kernel(sz, s_ref, keep_ref, recv_ref, v_ref, u_ref, bb_ref, own_ref, other_ref, d_ref, out_ref):
    weight, bias = small_parts(sz, s_ref, own_ref, other_ref, 1)
    matrix = point_matrix(sz, weight, True)
    column = nt(spread(sz), bias)[:, :1]
    left = turned_modes(sz, u_ref, 1)
    for at in range(0, sz.cells, CHUNK):
        cut = slice(at, at + CHUNK)
        grad = jnp.where(s_ref[0] == 0, recv_ref[:, cut], keep_ref[:, cut]).astype(f32)
        pre = nn(left, bb_ref[:, cut]) + nn(matrix, v_ref[:, cut]) + column
        _, slope = activate(pre)
        d_ref[:, cut] = (grad * slope).astype(bf16)
    send_analysis(sz, bb_ref, d_ref[...], out_ref, 1)


def turn_call(sz, s, keep, recv, v, u, bb, own, other):
    return pl.pallas_call(
        lambda *refs: turn_kernel(sz, *refs),
        out_shape=(
            jax.ShapeDtypeStruct((sz.rows, sz.cells), bf16),
            jax.ShapeDtypeStruct((sz.modes, sz.rows), bf16),
        ),
        in_specs=[smem] + vmem(7),
        out_specs=tuple(vmem(2)),
        compiler_params=params,
        name="turn",
    )(s, keep, recv, v, u, bb, own, other)


def back_kernel(sz, s_ref, d_ref, slope_ref, u_ref, bb_ref, own_ref, other_ref, new_ref, out_ref):
    weight, _ = small_parts(sz, s_ref, own_ref, other_ref, 1)
    matrix = point_matrix(sz, weight, False)
    left = turned_modes(sz, u_ref, 1)
    for at in range(0, sz.cells, CHUNK):
        cut = slice(at, at + CHUNK)
        grad = (nn(left, bb_ref[:, cut]) + nn(matrix, d_ref[:, cut])).astype(bf16).astype(f32)
        new_ref[:, cut] = (grad * slope_ref[:, cut]).astype(bf16)
    send_analysis(sz, bb_ref, new_ref[...], out_ref, 0)


def back_call(sz, s, d, slope, u, bb, own, other):
    return pl.pallas_call(
        lambda *refs: back_kernel(sz, *refs),
        out_shape=(
            jax.ShapeDtypeStruct((sz.rows, sz.cells), bf16),
            jax.ShapeDtypeStruct((sz.modes, sz.rows), bf16),
        ),
        in_specs=[smem] + vmem(6),
        out_specs=tuple(vmem(2)),
        compiler_params=params,
        name="back",
    )(s, d, slope, u, bb, own, other)


def point_kernel(sz, field, d_ref, out_ref):
    d = d_ref[...]
    pairs = jnp.where(same_y(sz), nt(field, d), 0.0)
    pairs = jnp.sum(pairs.reshape(sz.chans, sz.len_y, sz.rows), axis=1)
    ones = jnp.ones((8, sz.cells), bf16)
    bias = nt(ones, d)
    part = sz.chans // 4
    total = None
    for t in range(4):
        shape = (sz.rows, 128)
        place = (iota(shape, 0) // sz.len_y + t * sz.chans == iota(shape, 1)).astype(f32)
        both = pairs[t * part : (t + 1) * part]
        if t == 0:
            both = jnp.concatenate([both, bias], axis=0)
        else:
            both = jnp.concatenate([both, jnp.zeros_like(bias)], axis=0)
        term = lax.dot_general(
            both, place, (((1,), (0,)), ((), ())), precision=lax.Precision.HIGHEST, preferred_element_type=f32
        )
        total = term if total is None else total + term
    out_ref[...] = total


def point0_kernel(sz, s_ref, keep_ref, recv_ref, d_ref, out_ref):
    field = jnp.where(s_ref[0] == 0, keep_ref[...], recv_ref[...])
    point_kernel(sz, field, d_ref, out_ref)


def point1_kernel(sz, v_ref, d_ref, out_ref):
    point_kernel(sz, v_ref[...], d_ref, out_ref)


def point_call(sz, kernel, specs, *args):
    return pl.pallas_call(
        lambda *refs: kernel(sz, *refs),
        out_shape=jax.ShapeDtypeStruct((sz.chans // 4 + 8, 128), f32),
        in_specs=specs,
        out_specs=vmem(1)[0],
        compiler_params=params,
        name="point",
    )(*args)


def outer_kernel(sz, sv_ref, su_ref, out_ref):
    jk, groups, kk_count = sz.jk, sz.groups, sz.blk_k
    sv = sv_ref[0]
    su = su_ref[0]
    shape = (kk_count * 8, kk_count)
    one = (iota(shape, 0) // 8 == iota(shape, 1)).astype(bf16)
    diag = diagonal(sz, kk_count * 8)
    for lg in range(sz.lgs):
        cut = slice(lg * 128, (lg + 1) * 128)

        def block(rows):
            wide = jnp.concatenate([rows[h * kk_count : (h + 1) * kk_count, cut] for h in range(groups)], axis=1)
            return jnp.where(diag, nn(one, wide), 0.0)

        left = block(sv)
        right = nn(block(su).astype(bf16), chan_lanes(sz))
        for kk in range(kk_count):
            res = tn(left[kk * 8 : (kk + 1) * 8].astype(bf16), right[kk * 8 : (kk + 1) * 8].astype(bf16))
            for h in range(groups):
                out_ref[0, 0, kk, lg * 8 : (lg + 1) * 8, h * sz.cpl : (h + 1) * sz.cpl, :] = res[
                    h * 128 : (h + 1) * 128
                ].reshape(8, sz.cpl, sz.chans)


def outer_call(sz, sv, su):
    wide = sz.modes_y * sz.cpl
    rows = sz.groups * sz.blk_k
    return pl.pallas_call(
        lambda *refs: outer_kernel(sz, *refs),
        grid=(sz.blk_j,),
        out_shape=jax.ShapeDtypeStruct(
            (1, sz.blk_j, sz.blk_k, sz.modes_y, sz.chans, sz.chans), f32
        ),
        in_specs=[pl.BlockSpec((1, rows, wide), lambda i: (i, 0, 0))] * 2,
        out_specs=pl.BlockSpec(
            (1, 1, sz.blk_k, sz.modes_y, sz.chans, sz.chans), lambda i: (0, i, 0, 0, 0, 0)
        ),
        compiler_params=params,
        name="outer",
    )(sv, su)


def exchange(block):
    return lax.all_to_all(block, AXES, split_axis=0, concat_axis=0, tiled=True)


def swap(block):
    return lax.ppermute(block, "section", [(0, 1), (1, 0)])


def local(ends, spectral_weight, point_weight, point_bias):
    sz = Sizes(ends, spectral_weight)
    section = lax.axis_index("section")
    first = section == 0
    s = section.astype(jnp.int32).reshape(1)
    bx, bz, by = mode_tables(sz)
    bx = lax.dynamic_slice_in_dim(jnp.asarray(bx), lax.axis_index("gx") * sz.len_x, sz.len_x, axis=1)

    def half(which):
        part = lax.dynamic_slice_in_dim(ends[0], which * sz.len_y, sz.len_y, axis=2)
        return jnp.swapaxes(part, 1, 2).reshape(sz.rows, sz.cells)

    recv = swap(half(1 - section))
    keep = half(section)
    own_small = jnp.concatenate(
        [point_weight[0], jnp.broadcast_to(point_bias, (16, sz.chans))], axis=0
    )
    other_small = swap(own_small)
    other_weight = swap(spectral_weight[0, sz.half_j :])

    bb, ya, out = first_call(sz, s, keep, recv, bx, jnp.asarray(bz), jnp.asarray(by))
    sv0, out = mix_call(sz, 0, False, s, exchange(out), ya, spectral_weight, other_weight)
    v1, slope0, out = forward_call(sz, s, keep, recv, exchange(out), bb, own_small, other_small)
    sv1, out = mix_call(sz, 1, False, s, exchange(out), ya, spectral_weight, other_weight)
    d1, out = turn_call(sz, s, keep, recv, v1, exchange(out), bb, own_small, other_small)
    su1, out = mix_call(sz, 1, True, s, exchange(out), ya, spectral_weight, other_weight)
    d0, out = back_call(sz, s, d1, slope0, exchange(out), bb, own_small, other_small)
    su0 = spec_call(sz, exchange(out), ya)
    pg1 = point_call(sz, point1_kernel, vmem(2), v1, d1)
    pg0 = point_call(sz, point0_kernel, [smem] + vmem(3), s, keep, recv, d0)

    half_places = sz.places // 2
    sums = jnp.concatenate(
        [jnp.broadcast_to(pg0, (half_places,) + pg0.shape), jnp.broadcast_to(pg1, (half_places,) + pg1.shape)]
    )
    sums = jnp.sum(lax.all_to_all(sums, AXES, split_axis=0, concat_axis=0, tiled=True), axis=0)
    part = sz.chans // 4
    point_grad = jnp.swapaxes(sums[:part].reshape(part, 4, sz.chans), 0, 1).reshape(1, sz.chans, sz.chans)
    bias_grad = sums[part : part + 1, : sz.chans]

    def both(own, other):
        mine = jnp.where(first, own, other)
        theirs = swap(jnp.where(first, other, own))
        full = jnp.stack([mine, theirs]).reshape(2, sz.groups, sz.half_j, sz.blk_k, -1)
        return jnp.swapaxes(full, 1, 2).reshape(sz.blk_j, sz.groups * sz.blk_k, -1)

    spectral_grad = outer_call(sz, both(sv0, sv1), both(su0, su1))
    return (spectral_grad, point_grad, bias_grad)


def solution(mesh):
    return jax.shard_map(
        local,
        mesh=mesh,
        in_specs=(
            P("section", None, "gx", "gy", None),
            P("section", "gy", "gx", None, None, None),
            P("section", None, None),
            P("section", None),
        ),
        out_specs=(
            P("section", "gy", "gx", None, None, None),
            P("section", None, None),
            P("section", None),
        ),
        check_vma=False,
    )
```

```python
import math

import jax
import jax.numpy as jnp
import ml_dtypes
import numpy as np
from jax import lax
from jax.experimental import pallas as pl
from jax.experimental.pallas import tpu as pltpu
from jax.sharding import PartitionSpec as P

gelu_coef = 0.7978845608028654
f32 = jnp.float32
bf16 = jnp.bfloat16
AXES = ("section", "gx", "gy")


def table(length, count):
    half = count // 2
    modes = np.arange(count)
    is_cos = modes < half
    wave = np.where(is_cos, modes, modes - half + 1)
    phase = wave[:, None] * np.arange(length)[None, :] % length
    angle = phase.astype(np.float32) * np.float32(2.0 * math.pi / length)
    values = np.where(is_cos[:, None], np.cos(angle), np.sin(angle)).astype(np.float32)
    scale = np.where(is_cos & (wave == 0), math.sqrt(1.0 / length), math.sqrt(2.0 / length))
    return (values * scale.astype(np.float32)[:, None]).astype(ml_dtypes.bfloat16).astype(np.float32)


def nn(a, b):
    return lax.dot_general(a, b, (((1,), (0,)), ((), ())), preferred_element_type=f32)


def nt(a, b):
    return lax.dot_general(a, b, (((1,), (1,)), ((), ())), preferred_element_type=f32)


def tn(a, b):
    return lax.dot_general(a, b, (((0,), (0,)), ((), ())), preferred_element_type=f32)


def iota(shape, dim):
    return lax.broadcasted_iota(jnp.int32, shape, dim)


limit = 24 * 1024 * 1024
smem = pl.BlockSpec(memory_space=pltpu.SMEM)
hbm = pl.BlockSpec(memory_space=pltpu.HBM)
vmem = pl.BlockSpec(memory_space=pltpu.VMEM)


def shape(dims, dtype=bf16):
    return jax.ShapeDtypeStruct(dims, dtype)


def kept(dims, dtype=bf16):
    return pltpu.VMEM(dims, dtype)


def near(value):
    return pltpu.with_memory_space_constraint(value, pltpu.VMEM)


def far(value):
    return pltpu.with_memory_space_constraint(value, pltpu.HBM)


def run(name, kernel, outs, specs, args, scratch=(), copies=0, micros=1):
    return pl.pallas_call(
        kernel,
        out_shape=tuple(pltpu.HBM(o.shape, o.dtype) if away else o for o, away in outs),
        in_specs=list(specs),
        out_specs=tuple(hbm if away else vmem for _, away in outs),
        scratch_shapes=list(scratch) + ([pltpu.SemaphoreType.DMA((copies,))] if copies else []),
        compiler_params=pltpu.CompilerParams(vmem_limit_bytes=limit),
        cost_estimate=pl.CostEstimate(flops=0, transcendentals=0, bytes_accessed=micros * 3000000),
        name=name,
    )(*[far(a) if spec is hbm else a for a, spec in zip(args, specs)])


class Copies:
    def __init__(self, sems):
        self.sems = sems
        self.used = 0
        self.open = []

    def make(self, src, dst):
        copy = pltpu.make_async_copy(src, dst, self.sems.at[self.used])
        self.used += 1
        return copy

    def start(self, src, dst):
        copy = self.make(src, dst)
        copy.start()
        return copy

    def choose(self, pick, triples):
        firsts, others = [], []
        for src, other, dst in triples:
            firsts.append(pltpu.make_async_copy(src, dst, self.sems.at[self.used]))
            others.append(self.make(other, dst))

        @pl.when(pick)
        def _():
            for copy in firsts:
                copy.start()

        @pl.when(jnp.logical_not(pick))
        def _():
            for copy in others:
                copy.start()

        return others

    def send(self, src, dst):
        self.open.append(self.start(src, dst))

    def finish(self):
        for copy in self.open:
            copy.wait()


class Sizes:
    def __init__(self, ends, weight):
        self.n_gx = lax.axis_size("gx")
        self.n_gy = lax.axis_size("gy")
        _, self.chans, self.len_x, full, self.depth = ends.shape
        self.len_y = full // 2
        _, self.blk_j, self.blk_k, self.modes_y, _, _ = weight.shape
        self.half_j = self.blk_j // 2
        self.jk = self.half_j * self.blk_k
        self.places = 2 * self.n_gx * self.n_gy
        self.modes = self.places * self.jk
        self.rows = self.chans * self.len_y
        self.cells = self.len_x * self.depth
        self.lines = 2 * self.n_gy
        self.cpl = 128 // self.len_y
        self.groups = self.rows // 128
        self.lgs = self.modes_y // 8
        self.full_x = self.len_x * self.n_gx
        self.full_y = full * self.n_gy


def mode_tables(sz):
    bx = table(sz.full_x, sz.blk_j * sz.n_gy)
    bz = table(sz.depth, sz.blk_k * sz.n_gx)
    by = table(sz.full_y, sz.modes_y)
    sec, gx, gy, jj, kk = np.meshgrid(
        np.arange(2), np.arange(sz.n_gx), np.arange(sz.n_gy), np.arange(sz.half_j), np.arange(sz.blk_k), indexing="ij"
    )
    row_j = (gy * sz.blk_j + sec * sz.half_j + jj).reshape(-1)
    row_k = (gx * sz.blk_k + kk).reshape(-1)
    sec, gy, yy = np.meshgrid(np.arange(2), np.arange(sz.n_gy), np.arange(sz.len_y), indexing="ij")
    row_y = (gy * 2 * sz.len_y + sec * sz.len_y + yy).reshape(-1)
    bx = np.moveaxis(bx[row_j].reshape(sz.modes, sz.n_gx, sz.len_x), 1, 0)
    return bx, bz[row_k], np.repeat(by[:, row_y].T, sz.cpl, axis=1)


def activate(pre):
    inner = gelu_coef * (pre + 0.044715 * pre * pre * pre)
    tanh_val = jnp.tanh(inner)
    value = 0.5 * pre * (1.0 + tanh_val)
    slope = 0.5 * (1.0 + tanh_val) + 0.5 * pre * (1.0 - tanh_val * tanh_val) * gelu_coef * (
        1.0 + 3.0 * 0.044715 * pre * pre
    )
    return value, slope


def spread(sz):
    shape = (sz.rows, sz.chans)
    return (iota(shape, 0) // sz.len_y == iota(shape, 1)).astype(bf16)


def same_y(sz):
    shape = (sz.rows, sz.rows)
    return iota(shape, 0) % sz.len_y == iota(shape, 1) % sz.len_y


def point_matrix(sz, weight, forward):
    one = spread(sz)
    part = nt(one, weight) if forward else nn(one, weight)
    full = nt(part.astype(bf16), one)
    return jnp.where(same_y(sz), full, 0.0).astype(bf16)


def swapped(rows, half):
    return jnp.concatenate([rows[half:], rows[:half]], axis=0)


def send_analysis(sz, bb_ref, field, out_ref, layer):
    out = nt(bb_ref[...], field).astype(bf16)
    out_ref[...] = swapped(out, sz.modes // 2) if layer == 1 else out


def fill_table(sz, bx, bz, bb):
    depth = sz.depth
    for x in range(sz.len_x):
        bb[:, x * depth : (x + 1) * depth] = (bx[:, x : x + 1] * bz[...]).astype(bf16)


def tables_kernel(sz, gx_ref, bx_hbm, bz_hbm, bb, bx, bz, sems):
    copies = Copies(sems)
    get_bx = copies.start(bx_hbm.at[gx_ref[0]], bx)
    get_bz = copies.start(bz_hbm, bz)
    get_bx.wait()
    get_bz.wait()
    fill_table(sz, bx, bz, bb)


def tables_call(sz, gx, bx, bz):
    (bb,) = run(
        "tables",
        lambda *refs: tables_kernel(sz, *refs),
        [(kept((sz.modes, sz.cells)), False)],
        [smem, hbm, hbm],
        (gx, bx, bz),
        [pltpu.VMEM(bx.shape[1:], f32), pltpu.VMEM(bz.shape, f32)],
        2,
    )
    return bb


def first_kernel(sz, s_ref, keep_hbm, recv_hbm, small_ref, bb, out_hbm, v, out, sems):
    copies = Copies(sems)
    (get_v,) = copies.choose(s_ref[0] == 0, [(keep_hbm, recv_hbm, v)])
    get_v.wait()
    send_analysis(sz, bb, v[...], out, 0)
    copies.send(out, out_hbm)
    copies.finish()


def first_call(sz, s, keep, recv, small, bb):
    line = (sz.modes, sz.rows)
    (out,) = run(
        "first",
        lambda *refs: first_kernel(sz, *refs),
        [(shape(line), True)],
        [smem, hbm, hbm, vmem, vmem],
        (s, keep, recv, small, near(bb)),
        [pltpu.VMEM((sz.rows, sz.cells), bf16), pltpu.VMEM(line, bf16)],
        2,
    )
    return out


def pack_kernel(sz, tables, w_ref, *rest):
    if tables:
        by_ref, out_ref, ya_ref = rest

        @pl.when(pl.program_id(0) == 0)
        def _():
            wide = sz.modes_y * sz.cpl
            lane_c = iota((sz.len_y, wide), 1) % sz.cpl
            for g in range(sz.lines):
                part = by_ref[g * sz.len_y : (g + 1) * sz.len_y, :]
                block = jnp.concatenate([jnp.where(lane_c == c, part, 0.0) for c in range(sz.cpl)], axis=0)
                ya_ref[g * 128 : (g + 1) * 128, :] = block.astype(bf16)

    else:
        (out_ref,) = rest
    width = sz.lgs * sz.chans
    dims = (sz.chans, width)
    places = [(iota(dims, 0) + lg * sz.chans == iota(dims, 1)).astype(bf16) for lg in range(sz.lgs)]
    for kk in range(sz.blk_k):
        total = None
        for lg in range(sz.lgs):
            rows = jnp.concatenate(
                [
                    w_ref[0, 0, kk, lg * 8 : (lg + 1) * 8, h * sz.cpl : (h + 1) * sz.cpl, :].reshape(128, sz.chans)
                    for h in range(sz.groups)
                ],
                axis=0,
            )
            part = nn(rows, places[lg])
            total = part if total is None else total + part
        out_ref[0, kk] = total.astype(bf16)


def pack_call(sz, weight, start, micros, by=None):
    rows, width, half = sz.groups * 128, sz.lgs * sz.chans, sz.half_j
    block = (1, sz.blk_k, rows, width)
    lines = (sz.lines * 128, sz.modes_y * sz.cpl)
    packed = pltpu.HBM((half, sz.blk_k, rows, width), bf16)
    tables = by is not None
    weight_spec = pl.BlockSpec((1, 1) + weight.shape[2:], lambda i: (0, i + start, 0, 0, 0, 0))
    packed_spec = pl.BlockSpec(block, lambda i: (i, 0, 0, 0))
    return pl.pallas_call(
        lambda *refs: pack_kernel(sz, tables, *refs),
        grid=(half,),
        out_shape=(packed, pltpu.HBM(lines, bf16)) if tables else packed,
        in_specs=[weight_spec, pl.BlockSpec(by.shape, lambda i: (0, 0))] if tables else [weight_spec],
        out_specs=(packed_spec, pl.BlockSpec(lines, lambda i: (0, 0))) if tables else packed_spec,
        compiler_params=pltpu.CompilerParams(vmem_limit_bytes=limit),
        cost_estimate=pl.CostEstimate(flops=0, transcendentals=0, bytes_accessed=micros * 3000000),
        name="pack",
    )(*([far(weight), far(by)] if tables else [far(weight)]))


def line_analysis(sz, r_ref, ya_ref, get_ya):
    jk = sz.jk
    lines = []
    for sec in range(2):
        for gy in range(sz.n_gy):
            total = None
            for gx in range(sz.n_gx):
                at = ((sec * sz.n_gx + gx) * sz.n_gy + gy) * jk
                part = r_ref[at : at + jk, :].astype(f32)
                total = part if total is None else total + part
            lines.append(total.astype(bf16))
    halves = [
        jnp.concatenate([line[:, h * 128 : (h + 1) * 128] for line in lines], axis=1) for h in range(sz.groups)
    ]
    if get_ya is not None:
        get_ya.wait()
    return nn(jnp.concatenate(halves, axis=0), ya_ref[...]).astype(bf16)


def diagonal(sz, count):
    shape = (count, sz.groups * 128)
    return iota(shape, 0) % 8 == (iota(shape, 1) % 128) // sz.cpl


def row_spread(sz):
    shape = (sz.jk * 8, sz.jk)
    return (iota(shape, 0) // 8 == iota(shape, 1)).astype(bf16)


def row_gather(sz):
    shape = (sz.jk, sz.jk * 8)
    return (iota(shape, 1) // 8 == iota(shape, 0)).astype(bf16)


def chan_lanes(sz):
    shape = (sz.groups * 128, sz.chans)
    lane = iota(shape, 0)
    return ((lane // 128) * sz.cpl + lane % sz.cpl == iota(shape, 1)).astype(bf16)


def to_blocks(sz, rows, lg):
    jk = sz.jk
    wide = jnp.concatenate(
        [rows[h * jk : (h + 1) * jk, lg * 128 : (lg + 1) * 128] for h in range(sz.groups)], axis=1
    )
    return jnp.where(diagonal(sz, jk * 8), nn(row_spread(sz), wide), 0.0)


def from_blocks(sz, blocks):
    jk = sz.jk
    pieces = []
    for block in blocks:
        kept = jnp.where(diagonal(sz, jk * 8), block, 0.0).astype(bf16)
        pieces.append(nn(row_gather(sz), kept).astype(bf16))
    return jnp.concatenate(
        [
            jnp.concatenate([piece[:, h * 128 : (h + 1) * 128] for piece in pieces], axis=1)
            for h in range(sz.groups)
        ],
        axis=0,
    )


def send_lines(sz, rows, ya_ref, out_ref):
    jk = sz.jk
    lines = nt(rows, ya_ref[...]).astype(bf16)
    for sec in range(2):
        for gy in range(sz.n_gy):
            line = sec * sz.n_gy + gy
            block = jnp.concatenate(
                [lines[h * jk : (h + 1) * jk, line * 128 : (line + 1) * 128] for h in range(sz.groups)], axis=1
            )
            for gx in range(sz.n_gx):
                at = ((sec * sz.n_gx + gx) * sz.n_gy + gy) * jk
                out_ref[at : at + jk, :] = block


def lane_group(sz):
    dims = (sz.lgs * sz.jk * 8, sz.lgs * sz.chans)
    return iota(dims, 0) // (sz.jk * 8) == iota(dims, 1) // sz.chans


def mix_kernel(sz, layer, turn, s_ref, r, ya_in, low_hbm, high_hbm, spec_hbm, out, *rest):
    if layer == 0:
        ya, w, spec_b, blk, mix, sems = rest
    else:
        ya = ya_in
        w, spec_b, blk, mix, sems = rest
    copies = Copies(sems)
    get_ya = copies.start(ya_in, ya) if layer == 0 else None
    get_w = copies.choose(s_ref[0] == layer, [(low_hbm.at[jj], high_hbm.at[jj], w.at[jj]) for jj in range(sz.half_j)])
    spec = line_analysis(sz, r, ya, get_ya)
    spec_b[...] = spec
    copies.send(spec_b, spec_hbm)
    count = sz.jk * 8
    width = sz.lgs * sz.chans
    rep = jnp.concatenate([chan_lanes(sz)] * sz.lgs, axis=1)
    blocks = [to_blocks(sz, spec, lg) for lg in range(sz.lgs)]
    if turn:
        flat = nn(jnp.concatenate(blocks, axis=0).astype(bf16), rep)
        mix[:, :width] = jnp.where(lane_group(sz), flat, 0.0)
        left_ref, right_ref, left_width = mix, blk, width
    else:
        for lg in range(sz.lgs):
            blk[lg * count : (lg + 1) * count, :] = blocks[lg]
        left_ref, right_ref, left_width = blk, mix, blk.shape[1]
    for jk in range(sz.jk):
        jj, kk = jk // sz.blk_k, jk % sz.blk_k
        if kk == 0:
            get_w[jj].wait()
        at = [slice((lg * sz.jk + jk) * 8, (lg * sz.jk + jk + 1) * 8) for lg in range(sz.lgs)]
        left = jnp.concatenate([left_ref[a, :left_width] for a in at], axis=0).astype(bf16)
        part = nt(left, w[jj, kk]) if turn else nn(left, w[jj, kk])
        for lg, a in enumerate(at):
            right_ref[a, : part.shape[1]] = part[lg * 8 : (lg + 1) * 8]
    if not turn:
        kept_mix = jnp.where(lane_group(sz), mix[:, :width], 0.0).astype(bf16)
        full = nt(kept_mix, rep)
    else:
        full = blk[...]
    blocks = [full[lg * count : (lg + 1) * count] for lg in range(sz.lgs)]
    send_lines(sz, from_blocks(sz, blocks), ya, out)
    copies.finish()


def mix_call(sz, layer, turn, s, r, ya, low, high):
    count = sz.jk * 8 * sz.lgs
    spec = (sz.groups * sz.jk, sz.modes_y * sz.cpl)
    line = (sz.modes, sz.rows)
    outs = [(shape(spec), True), (kept(line), False)]
    if layer == 0:
        outs.append((kept(ya.shape), False))
    else:
        ya = near(ya)
    return run(
        "mix",
        lambda *refs: mix_kernel(sz, layer, turn, *refs),
        outs,
        [smem, vmem, hbm if layer == 0 else vmem, hbm, hbm],
        (s, r, ya, low, high),
        [
            pltpu.VMEM(low.shape, bf16),
            pltpu.VMEM(spec, bf16),
            pltpu.VMEM((count, sz.groups * 128), f32),
            pltpu.VMEM((count, sz.groups * 128), f32),
        ],
        sz.half_j + 2,
    )


def spec_kernel(sz, s_ref, r, sv0, sv1, su1, ya, out_hbm, send_hbm, out, sends, sems):
    copies = Copies(sems)
    first = s_ref[0] == 0
    spec = line_analysis(sz, r, ya, None)
    out[...] = spec
    sends[0] = jnp.where(first, sv1[...], sv0[...])
    sends[1] = jnp.where(first, su1[...], spec)
    copies.send(sends, send_hbm)
    copies.send(out, out_hbm)
    copies.finish()


def spec_call(sz, s, r, sv0, sv1, su1, ya):
    spec = (sz.groups * sz.jk, sz.modes_y * sz.cpl)
    return run(
        "spec",
        lambda *refs: spec_kernel(sz, *refs),
        [(shape(spec), True), (shape((2,) + spec), True)],
        [smem] + [vmem] * 5,
        (s, r, sv0, sv1, su1, near(ya)),
        [pltpu.VMEM(spec, bf16), pltpu.VMEM((2,) + spec, bf16)],
        2,
    )


def turned_modes(sz, u_ref, layer):
    left = jnp.transpose(u_ref[...])
    half = sz.modes // 2
    if layer == 1:
        left = jnp.concatenate([left[:, half:], left[:, :half]], axis=1)
    return left


CHUNK = 512


def cuts(sz):
    return [slice(at, at + CHUNK) for at in range(0, sz.cells, CHUNK)]


def buffers(sz, kinds):
    dims = {"m": (sz.modes, sz.cells), "u": (sz.modes, sz.rows), "f": (sz.rows, sz.cells), "w": (sz.rows, sz.cells)}
    return [pltpu.VMEM(dims[kind], f32 if kind == "w" else bf16) for kind in kinds]


def small_parts(sz, s_ref, own_ref, other_ref, layer):
    chosen = jnp.where(s_ref[0] == layer, own_ref[...].astype(f32), other_ref[...].astype(f32)).astype(bf16)
    return chosen[: sz.chans], chosen[sz.chans :]


def point_sums(sz, v, d):
    pairs = jnp.where(same_y(sz), nt(v, d), 0.0)
    pairs = jnp.sum(pairs.reshape(sz.chans, sz.len_y, sz.rows), axis=1)
    bias = nt(jnp.ones((8, sz.cells), bf16), d)
    part = sz.chans // 4
    total = None
    for t in range(4):
        dims = (sz.rows, 128)
        place = (iota(dims, 0) // sz.len_y + t * sz.chans == iota(dims, 1)).astype(f32)
        both = pairs[t * part : (t + 1) * part]
        both = jnp.concatenate([both, bias if t == 0 else jnp.zeros_like(bias)], axis=0)
        term = lax.dot_general(
            both, place, (((1,), (0,)), ((), ())), precision=lax.Precision.HIGHEST, preferred_element_type=f32
        )
        total = term if total is None else total + term
    return total


def forward_kernel(
    sz, s_ref, gx_ref, own_ref, other_ref, u, keep_hbm, recv_hbm, bx_hbm, bz_hbm, v, slope, bb, out, field, bx, bz, sems
):
    copies = Copies(sems)
    get_bx = copies.start(bx_hbm.at[gx_ref[0]], bx)
    get_bz = copies.start(bz_hbm, bz)
    (get_v,) = copies.choose(s_ref[0] == 0, [(keep_hbm, recv_hbm, field)])
    weight, bias = small_parts(sz, s_ref, own_ref, other_ref, 0)
    matrix = point_matrix(sz, weight, True)
    column = nt(spread(sz), bias)[:, :1]
    left = turned_modes(sz, u, 0)
    get_bx.wait()
    get_bz.wait()
    fill_table(sz, bx, bz, bb)
    get_v.wait()
    for cut in cuts(sz):
        pre = nn(left, bb[:, cut]) + nn(matrix, field[:, cut]) + column
        value, rate = activate(pre)
        v[:, cut] = value.astype(bf16)
        slope[:, cut] = rate
    send_analysis(sz, bb, v[...], out, 1)


def forward_call(sz, s, gx, keep, recv, u, bx, bz, own, other):
    field, line = (sz.rows, sz.cells), (sz.modes, sz.rows)
    return run(
        "forward",
        lambda *refs: forward_kernel(sz, *refs),
        [(kept(field), False), (kept(field, f32), False), (kept((sz.modes, sz.cells)), False), (kept(line), False)],
        [smem, smem, vmem, vmem, vmem, hbm, hbm, hbm, hbm],
        (s, gx, own, other, u, keep, recv, bx, bz),
        buffers(sz, "f") + [pltpu.VMEM(bx.shape[1:], f32), pltpu.VMEM(bz.shape, f32)],
        3,
    )


def turn_kernel(sz, s_ref, own_ref, other_ref, u, v, bb, keep_hbm, recv_hbm, d, sums, out, grad, sems):
    copies = Copies(sems)
    (get_g,) = copies.choose(s_ref[0] == 0, [(recv_hbm, keep_hbm, grad)])
    weight, bias = small_parts(sz, s_ref, own_ref, other_ref, 1)
    matrix = point_matrix(sz, weight, True)
    column = nt(spread(sz), bias)[:, :1]
    left = turned_modes(sz, u, 1)
    for at, cut in enumerate(cuts(sz)):
        pre = nn(left, bb[:, cut]) + nn(matrix, v[:, cut]) + column
        _, rate = activate(pre)
        if at == 0:
            get_g.wait()
        d[:, cut] = (grad[:, cut].astype(f32) * rate).astype(bf16)
    send_analysis(sz, bb, d[...], out, 1)
    sums[...] = point_sums(sz, v[...], d[...])


def turn_call(sz, s, keep, recv, v, u, bb, own, other):
    field, line = (sz.rows, sz.cells), (sz.modes, sz.rows)
    return run(
        "turn",
        lambda *refs: turn_kernel(sz, *refs),
        [(kept(field), False), (kept((sz.chans // 4 + 8, 128), f32), False), (kept(line), False)],
        [smem, vmem, vmem, vmem, vmem, vmem, hbm, hbm],
        (s, own, other, u, near(v), near(bb), keep, recv),
        buffers(sz, "f"),
        1,
    )


def back_kernel(sz, s_ref, own_ref, other_ref, u, d, slope, bb, sums, keep_hbm, recv_hbm, parts_hbm, out, new, field, parts, sems):
    copies = Copies(sems)
    (get_v,) = copies.choose(s_ref[0] == 0, [(keep_hbm, recv_hbm, field)])
    weight, _ = small_parts(sz, s_ref, own_ref, other_ref, 1)
    matrix = point_matrix(sz, weight, False)
    left = turned_modes(sz, u, 1)
    for cut in cuts(sz):
        grad = (nn(left, bb[:, cut]) + nn(matrix, d[:, cut])).astype(bf16).astype(f32)
        new[:, cut] = (grad * slope[:, cut]).astype(bf16)
    send_analysis(sz, bb, new[...], out, 0)
    get_v.wait()
    first = point_sums(sz, field[...], new[...])
    half = sz.places // 2
    for place in range(half):
        parts[place] = first
        parts[half + place] = sums[...]
    copies.send(parts, parts_hbm)
    copies.finish()


def back_call(sz, s, keep, recv, d, slope, u, bb, sums, own, other):
    parts, line = (sz.places, sz.chans // 4 + 8, 128), (sz.modes, sz.rows)
    return run(
        "back",
        lambda *refs: back_kernel(sz, *refs),
        [(shape(parts, f32), True), (kept(line), False)],
        [smem] + [vmem] * 7 + [hbm, hbm],
        (s, own, other, u, near(d), near(slope), near(bb), near(sums), keep, recv),
        buffers(sz, "ff") + [pltpu.VMEM(parts, f32)],
        2,
    )


def finish_kernel(sz, parts_ref, after_ref, point_ref, bias_ref):
    total = jnp.sum(parts_ref[...], axis=0)
    part = sz.chans // 4
    for t in range(4):
        point_ref[0, t * part : (t + 1) * part, :] = total[:part, t * sz.chans : (t + 1) * sz.chans]
    bias_ref[...] = total[part : part + 1, : sz.chans]


def finish_call(sz, parts, after):
    return pl.pallas_call(
        lambda *refs: finish_kernel(sz, *refs),
        out_shape=(shape((1, sz.chans, sz.chans), f32), shape((1, sz.chans), f32)),
        in_specs=[vmem, hbm],
        out_specs=(vmem, vmem),
        compiler_params=pltpu.CompilerParams(vmem_limit_bytes=limit),
        name="finish",
    )(parts, far(after))


def outer_kernel(sz, s_ref, sv0_ref, sv1_ref, su0_ref, su1_ref, theirs_ref, out_ref, left_ref, right_ref):
    jk, groups, kk_count = sz.jk, sz.groups, sz.blk_k
    step = pl.program_id(0)

    def prepare(side, sv, su):
        sv = sv.astype(f32)
        for jj in range(sz.half_j):
            place = side * sz.half_j + jj
            rows = jnp.concatenate(
                [sv[h * jk + jj * kk_count : h * jk + (jj + 1) * kk_count] for h in range(groups)], axis=0
            )
            left_ref[place] = jnp.transpose(rows)
        for lg in range(sz.lgs):
            flat = nn(to_blocks(sz, su, lg).astype(bf16), chan_lanes(sz))
            for at in range(jk):
                place = side * sz.half_j + at // kk_count
                right_ref[place, at % kk_count, lg * 8 : (lg + 1) * 8, :] = flat[at * 8 : (at + 1) * 8]

    @pl.when(step == 0)
    def _():
        first = s_ref[0] == 0
        prepare(
            0, jnp.where(first, sv0_ref[...], sv1_ref[...]), jnp.where(first, su0_ref[...], su1_ref[...])
        )

    @pl.when(step == 1)
    def _():
        prepare(1, theirs_ref[0], theirs_ref[1])

    for kk in range(kk_count):
        for h in range(groups):
            column = left_ref[step, :, h * kk_count + kk : h * kk_count + kk + 1]
            for ll in range(sz.modes_y):
                row = right_ref[step, kk, ll : ll + 1, :]
                part = column[ll * sz.cpl : (ll + 1) * sz.cpl] * row
                out_ref[0, 0, kk, ll, h * sz.cpl : (h + 1) * sz.cpl, :] = part


def outer_call(sz, s, sv0, sv1, su0, su1, theirs):
    wide = sz.modes_y * sz.cpl
    return pl.pallas_call(
        lambda *refs: outer_kernel(sz, *refs),
        grid=(sz.blk_j,),
        out_shape=pltpu.HBM((1, sz.blk_j, sz.blk_k, sz.modes_y, sz.chans, sz.chans), f32),
        in_specs=[smem] + [vmem] * 5,
        out_specs=pl.BlockSpec((1, 1, sz.blk_k, sz.modes_y, sz.chans, sz.chans), lambda i: (0, i, 0, 0, 0, 0)),
        scratch_shapes=[
            pltpu.VMEM((sz.blk_j, wide, sz.groups * sz.blk_k), f32),
            pltpu.VMEM((sz.blk_j, sz.blk_k, sz.modes_y, sz.chans), f32),
        ],
        compiler_params=pltpu.CompilerParams(vmem_limit_bytes=limit),
        cost_estimate=pl.CostEstimate(flops=0, transcendentals=0, bytes_accessed=20000000),
        name="outer",
    )(s, sv0, sv1, su0, su1, theirs)


def exchange(block):
    return lax.all_to_all(block, AXES, split_axis=0, concat_axis=0, tiled=True)


def swap(block):
    return lax.ppermute(block, "section", [(0, 1), (1, 0)])


def local(ends, spectral_weight, point_weight, point_bias):
    sz = Sizes(ends, spectral_weight)
    section = lax.axis_index("section")
    first = section == 0
    s = section.astype(jnp.int32).reshape(1)

    def half(field, which):
        part = lax.dynamic_slice_in_dim(field, which * sz.len_y, sz.len_y, axis=2)
        return jnp.swapaxes(part, 1, 2).reshape(sz.rows, sz.cells)

    bx, bz, by = [jnp.asarray(t) for t in mode_tables(sz)]
    send = half(ends[0], 1 - section)
    send, later = lax.optimization_barrier((send, ends[0]))
    recv = swap(send)
    keep = half(later, section)
    gx = lax.axis_index("gx").astype(jnp.int32).reshape(1)
    bb = tables_call(sz, gx, bx, bz)
    own_small = jnp.concatenate([point_weight[0], jnp.broadcast_to(point_bias, (16, sz.chans))], axis=0)
    other_small = swap(own_small)

    out = first_call(sz, s, keep, recv, other_small, bb)
    out, weight = lax.optimization_barrier((out, spectral_weight))
    r = exchange(out)
    high = swap(pack_call(sz, weight, sz.half_j, 2))
    low, ya = pack_call(sz, weight, 0, 6, by)
    sv0, out, ya = mix_call(sz, 0, False, s, r, ya, low, high)
    v1, slope0, bb, out = forward_call(sz, s, gx, keep, recv, exchange(out), bx, bz, own_small, other_small)
    sv1, out = mix_call(sz, 1, False, s, exchange(out), ya, low, high)
    d1, sums, out = turn_call(sz, s, keep, recv, v1, exchange(out), bb, own_small, other_small)
    su1, out = mix_call(sz, 1, True, s, exchange(out), ya, low, high)
    parts, out = back_call(sz, s, keep, recv, d1, slope0, exchange(out), bb, sums, own_small, other_small)
    r, parts = lax.optimization_barrier((exchange(out), parts))
    su0, send = spec_call(sz, s, r, sv0, sv1, su1, ya)
    theirs = swap(send)
    parts = lax.all_to_all(parts, AXES, split_axis=0, concat_axis=0, tiled=True)
    spectral_grad = outer_call(sz, s, sv0, sv1, su0, su1, theirs)
    point_grad, bias_grad = finish_call(sz, parts, spectral_grad)
    return (spectral_grad, point_grad, bias_grad)


def solution(mesh):
    return jax.shard_map(
        local,
        mesh=mesh,
        in_specs=(
            P("section", None, "gx", "gy", None),
            P("section", "gy", "gx", None, None, None),
            P("section", None, None),
            P("section", None),
        ),
        out_specs=(
            P("section", "gy", "gx", None, None, None),
            P("section", None, None),
            P("section", None),
        ),
        check_vma=False,
    )
```

```python
import math

import jax
import jax.numpy as jnp
import ml_dtypes
import numpy as np
from jax import lax
from jax.experimental import pallas as pl
from jax.experimental.pallas import tpu as pltpu
from jax.sharding import PartitionSpec as P

gelu_coef = 0.7978845608028654
f32 = jnp.float32
bf16 = jnp.bfloat16
AXES = ("section", "gx", "gy")


def table(length, count):
    half = count // 2
    modes = np.arange(count)
    is_cos = modes < half
    wave = np.where(is_cos, modes, modes - half + 1)
    phase = wave[:, None] * np.arange(length)[None, :] % length
    angle = phase.astype(np.float32) * np.float32(2.0 * math.pi / length)
    values = np.where(is_cos[:, None], np.cos(angle), np.sin(angle)).astype(np.float32)
    scale = np.where(is_cos & (wave == 0), math.sqrt(1.0 / length), math.sqrt(2.0 / length))
    return (values * scale.astype(np.float32)[:, None]).astype(ml_dtypes.bfloat16).astype(np.float32)


def nn(a, b):
    return lax.dot_general(a, b, (((1,), (0,)), ((), ())), preferred_element_type=f32)


def nt(a, b):
    return lax.dot_general(a, b, (((1,), (1,)), ((), ())), preferred_element_type=f32)


def tn(a, b):
    return lax.dot_general(a, b, (((0,), (0,)), ((), ())), preferred_element_type=f32)


def iota(shape, dim):
    return lax.broadcasted_iota(jnp.int32, shape, dim)


limit = 24 * 1024 * 1024
smem = pl.BlockSpec(memory_space=pltpu.SMEM)
hbm = pl.BlockSpec(memory_space=pltpu.HBM)
vmem = pl.BlockSpec(memory_space=pltpu.VMEM)


def shape(dims, dtype=bf16):
    return jax.ShapeDtypeStruct(dims, dtype)


def kept(dims, dtype=bf16):
    return pltpu.VMEM(dims, dtype)


def near(value):
    return pltpu.with_memory_space_constraint(value, pltpu.VMEM)


def far(value):
    return pltpu.with_memory_space_constraint(value, pltpu.HBM)


def run(name, kernel, outs, specs, args, scratch=(), copies=0, micros=1):
    return pl.pallas_call(
        kernel,
        out_shape=tuple(pltpu.HBM(o.shape, o.dtype) if away else o for o, away in outs),
        in_specs=list(specs),
        out_specs=tuple(hbm if away else vmem for _, away in outs),
        scratch_shapes=list(scratch) + ([pltpu.SemaphoreType.DMA((copies,))] if copies else []),
        compiler_params=pltpu.CompilerParams(vmem_limit_bytes=limit),
        cost_estimate=pl.CostEstimate(flops=0, transcendentals=0, bytes_accessed=micros * 3000000),
        name=name,
    )(*[far(a) if spec is hbm else a for a, spec in zip(args, specs)])


class Copies:
    def __init__(self, sems):
        self.sems = sems
        self.used = 0
        self.open = []

    def make(self, src, dst):
        copy = pltpu.make_async_copy(src, dst, self.sems.at[self.used])
        self.used += 1
        return copy

    def start(self, src, dst):
        copy = self.make(src, dst)
        copy.start()
        return copy

    def choose(self, pick, triples):
        firsts, others = [], []
        for src, other, dst in triples:
            firsts.append(pltpu.make_async_copy(src, dst, self.sems.at[self.used]))
            others.append(self.make(other, dst))

        @pl.when(pick)
        def _():
            for copy in firsts:
                copy.start()

        @pl.when(jnp.logical_not(pick))
        def _():
            for copy in others:
                copy.start()

        return others

    def send(self, src, dst):
        self.open.append(self.start(src, dst))

    def finish(self):
        for copy in self.open:
            copy.wait()


class Sizes:
    def __init__(self, ends, weight):
        self.n_gx = lax.axis_size("gx")
        self.n_gy = lax.axis_size("gy")
        _, self.chans, self.len_x, full, self.depth = ends.shape
        self.len_y = full // 2
        _, self.blk_j, self.blk_k, self.modes_y, _, _ = weight.shape
        self.half_j = self.blk_j // 2
        self.jk = self.half_j * self.blk_k
        self.places = 2 * self.n_gx * self.n_gy
        self.modes = self.places * self.jk
        self.rows = self.chans * self.len_y
        self.cells = self.len_x * self.depth
        self.lines = 2 * self.n_gy
        self.cpl = 128 // self.len_y
        self.groups = self.rows // 128
        self.lgs = self.modes_y // 8
        self.full_x = self.len_x * self.n_gx
        self.fine = self.len_y // 2
        self.thin = self.chans * self.fine
        self.wide = 2 * self.cells
        self.full_y = full * self.n_gy


def mode_tables(sz):
    bx = table(sz.full_x, sz.blk_j * sz.n_gy)
    bz = table(sz.depth, sz.blk_k * sz.n_gx)
    by = table(sz.full_y, sz.modes_y)
    sec, gx, gy, jj, kk = np.meshgrid(
        np.arange(2), np.arange(sz.n_gx), np.arange(sz.n_gy), np.arange(sz.half_j), np.arange(sz.blk_k), indexing="ij"
    )
    row_j = (gy * sz.blk_j + sec * sz.half_j + jj).reshape(-1)
    row_k = (gx * sz.blk_k + kk).reshape(-1)
    sec, gy, yy = np.meshgrid(np.arange(2), np.arange(sz.n_gy), np.arange(sz.len_y), indexing="ij")
    row_y = (gy * 2 * sz.len_y + sec * sz.len_y + yy).reshape(-1)
    bx = np.moveaxis(bx[row_j].reshape(sz.modes, sz.n_gx, sz.len_x), 1, 0)
    lines = by[:, row_y].T.reshape(sz.lines, 2, 1, sz.fine, sz.modes_y)
    lines = np.broadcast_to(lines, (sz.lines, 2, 8 // sz.fine, sz.fine, sz.modes_y)).reshape(-1, sz.modes_y)
    return bx, bz[row_k], np.repeat(lines, sz.cpl, axis=1)


def activate(pre):
    inner = gelu_coef * (pre + 0.044715 * pre * pre * pre)
    tanh_val = jnp.tanh(inner)
    value = 0.5 * pre * (1.0 + tanh_val)
    slope = 0.5 * (1.0 + tanh_val) + 0.5 * pre * (1.0 - tanh_val * tanh_val) * gelu_coef * (
        1.0 + 3.0 * 0.044715 * pre * pre
    )
    return value, slope


def spread(sz):
    shape = (sz.thin, sz.chans)
    return (iota(shape, 0) // sz.fine == iota(shape, 1)).astype(bf16)


def same_y(sz):
    shape = (sz.thin, sz.thin)
    return iota(shape, 0) % sz.fine == iota(shape, 1) % sz.fine


def point_matrix(sz, weight, forward):
    one = spread(sz)
    part = nt(one, weight) if forward else nn(one, weight)
    full = nt(part.astype(bf16), one)
    return jnp.where(same_y(sz), full, 0.0).astype(bf16)


def swapped(rows, half):
    return jnp.concatenate([rows[half:], rows[:half]], axis=0)


def send_analysis(sz, bb_ref, field, out_ref, layer):
    out = nt(bb_ref[...], field).astype(bf16)
    out_ref[...] = swapped(out, sz.modes // 2) if layer == 1 else out


def fill_table(sz, bx, bz, bb):
    depth = sz.depth
    across, along = bx[...].astype(f32), bz[...].astype(f32)
    for x in range(sz.len_x):
        bb[:, x * depth : (x + 1) * depth] = (across[:, x : x + 1] * along).astype(bf16)


def tables_kernel(sz, gx_ref, bx_hbm, bz_hbm, bb, bx, bz, sems):
    copies = Copies(sems)
    get_bx = copies.start(bx_hbm.at[gx_ref[0]], bx)
    get_bz = copies.start(bz_hbm, bz)
    get_bx.wait()
    get_bz.wait()
    fill_table(sz, bx, bz, bb)


def tables_call(sz, gx, bx, bz):
    (bb,) = run(
        "tables",
        lambda *refs: tables_kernel(sz, *refs),
        [(kept((sz.modes, sz.cells)), False)],
        [smem, hbm, hbm],
        (gx, bx, bz),
        [pltpu.VMEM(bx.shape[1:], bf16), pltpu.VMEM(bz.shape, bf16)],
        2,
    )
    return bb


def reorder(sz):
    dims = (sz.rows, sz.rows)
    row = iota(dims, 0)
    group, quarter = row // 128, row % 128 // 64
    chan, y = group * sz.cpl + row % 64 // sz.fine, quarter * sz.fine + row % sz.fine
    return (chan * sz.len_y + y == iota(dims, 1)).astype(bf16)


def send_quarters(sz, gx_ref, field, mine_hbm, send_hbm, copies):
    quarter = gx_ref[0] % 2
    for h in range(sz.groups):
        to = slice(h * 64, (h + 1) * 64)
        copies.send(field.at[pl.ds(h * 128 + quarter * 64, 64)], mine_hbm.at[to])
        copies.send(field.at[pl.ds(h * 128 + (1 - quarter) * 64, 64)], send_hbm.at[to])


def wide_kernel(sz, gx_ref, bx_hbm, bz_hbm, after_hbm, bb_hbm, bx, bz, bb, sems):
    copies = Copies(sems)
    gets = [copies.start(bx_hbm.at[gx_ref[side]], bx.at[side]) for side in range(2)]
    gets.append(copies.start(bz_hbm, bz))
    for get in gets:
        get.wait()
    for side in range(2):
        at = slice(side * sz.cells, (side + 1) * sz.cells)
        fill_table(sz, bx.at[side], bz, bb.at[:, at])
        copies.send(bb.at[:, at], bb_hbm.at[:, at])
    copies.finish()


def wide_call(sz, gx, bx, bz, after):
    (bb,) = run(
        "wide",
        lambda *refs: wide_kernel(sz, *refs),
        [(shape((sz.modes, sz.wide)), True)],
        [smem, hbm, hbm, hbm],
        (gx, bx, bz, after),
        [pltpu.VMEM((2,) + bx.shape[1:], bf16), pltpu.VMEM(bz.shape, bf16), pltpu.VMEM((sz.modes, sz.wide), bf16)],
        5,
        0,
    )
    return bb


def first_kernel(sz, s_ref, gx_ref, keep, recv, bb, mine_hbm, send_hbm, raw_hbm, out_hbm, v, out, sems):
    copies = Copies(sems)
    first = s_ref[0] == 0
    (put_raw,) = copies.choose(first, [(recv, keep, raw_hbm)])
    v[...] = nn(reorder(sz), jnp.where(first, keep[...], recv[...])).astype(bf16)
    send_quarters(sz, gx_ref, v, mine_hbm, send_hbm, copies)
    send_analysis(sz, bb, v[...], out, 0)
    copies.send(out, out_hbm)
    put_raw.wait()
    copies.finish()


def first_call(sz, s, gx, keep, recv, bb):
    line, field, part = (sz.modes, sz.rows), (sz.rows, sz.cells), (sz.thin, sz.cells)
    return run(
        "first",
        lambda *refs: first_kernel(sz, *refs),
        [(shape(part), True), (shape(part), True), (shape(field), True), (shape(line), True)],
        [smem, smem, vmem, vmem, vmem],
        (s, gx, keep, recv, near(bb)),
        [pltpu.VMEM(field, bf16), pltpu.VMEM(line, bf16)],
        2 + 2 * sz.groups,
    )


def split_kernel(sz, gx_ref, raw_hbm, after_hbm, mine_hbm, send_hbm, raw, field, sems):
    copies = Copies(sems)
    copies.start(raw_hbm, raw).wait()
    field[...] = nn(reorder(sz), raw[...]).astype(bf16)
    send_quarters(sz, gx_ref, field, mine_hbm, send_hbm, copies)
    copies.finish()


def split_call(sz, gx, raw, after):
    field, part = (sz.rows, sz.cells), (sz.thin, sz.cells)
    return run(
        "split",
        lambda *refs: split_kernel(sz, *refs),
        [(shape(part), True), (shape(part), True)],
        [smem, hbm, hbm],
        (gx, raw, after),
        [pltpu.VMEM(field, bf16), pltpu.VMEM(field, bf16)],
        1 + 2 * sz.groups,
        0,
    )


def pack_kernel(sz, start, tables, *refs):
    if tables:
        after_hbm, w_hbm, by_hbm, out_hbm, ya_hbm, w, out, by, ya, sems = refs
    else:
        after_hbm, w_hbm, out_hbm, w, out, sems = refs
    copies = Copies(sems)
    if tables:
        get_by = copies.start(by_hbm, by)
    gets = [copies.start(w_hbm.at[0, start + jj], w.at[jj]) for jj in range(sz.half_j)]
    if tables:
        get_by.wait()
        table = by[...].astype(f32)
        wide = sz.modes_y * sz.cpl
        lane_c = iota((8, wide), 1) % sz.cpl
        each = 8 // sz.fine
        row_c = iota((8, wide), 0) // sz.fine
        for g in range(sz.lines):
            pieces = []
            for quarter in range(2):
                at = (g * 2 + quarter) * 8
                part = table[at : at + 8, :]
                pieces += [jnp.where(lane_c == c + row_c, part, 0.0) for c in range(0, sz.cpl, each)]
            ya[g * 128 : (g + 1) * 128, :] = jnp.concatenate(pieces, axis=0).astype(bf16)
        copies.send(ya, ya_hbm)
    for jj in range(sz.half_j):
        gets[jj].wait()
        for kk in range(sz.blk_k):
            for h in range(sz.groups):
                lanes = [
                    w[jj, kk, lg * 8 : (lg + 1) * 8, h * sz.cpl : (h + 1) * sz.cpl, :].reshape(128, sz.chans)
                    for lg in range(sz.lgs)
                ]
                out[jj, kk, h * 128 : (h + 1) * 128, :] = jnp.concatenate(lanes, axis=1)
        copies.send(out.at[jj], out_hbm.at[jj])
    copies.finish()


def pack_call(sz, after, weight, start, by=None):
    half = sz.half_j
    packed = (half, sz.blk_k, sz.groups * 128, sz.lgs * sz.chans)
    lines = (sz.lines * 128, sz.modes_y * sz.cpl)
    outs = [(shape(packed), True)]
    args = (after, weight)
    scratch = [pltpu.VMEM((half,) + weight.shape[2:], bf16), pltpu.VMEM(packed, bf16)]
    tables = by is not None
    if tables:
        outs.append((shape(lines), True))
        args += (by,)
        scratch += [pltpu.VMEM(by.shape, bf16), pltpu.VMEM(lines, bf16)]
    result = run(
        "pack",
        lambda *refs: pack_kernel(sz, start, tables, *refs),
        outs,
        [hbm] * len(args),
        args,
        scratch,
        2 * half + 2 * tables,
        0,
    )
    return result if tables else result[0]


def line_analysis(sz, r_ref, ya_ref, get_ya, fine=True):
    jk = sz.jk

    def total(sec, gy, start, step):
        result = None
        for gx in range(start, sz.n_gx, step):
            at = ((sec * sz.n_gx + gx) * sz.n_gy + gy) * jk
            part = r_ref[at : at + jk, :].astype(f32)
            result = part if result is None else result + part
        return result

    halves = [[], []]
    low = iota((jk, 128), 1) < 64
    for sec in range(2):
        for gy in range(sz.n_gy):
            if fine:
                a, b = total(sec, gy, 0, 2), total(sec, gy, 1, 2)
                halves[0].append(jnp.where(low, a, pltpu.roll(b, 64, 1)).astype(bf16))
                halves[1].append(jnp.where(low, pltpu.roll(a, 64, 1), b).astype(bf16))
            else:
                line = total(sec, gy, 0, 1).astype(bf16)
                for h in range(sz.groups):
                    halves[h].append(line[:, h * 128 : (h + 1) * 128])
    rows = jnp.concatenate([jnp.concatenate(half, axis=1) for half in halves], axis=0)
    if get_ya is not None:
        get_ya.wait()
    return nn(rows, ya_ref[...]).astype(bf16)


def diagonal(sz, count):
    shape = (count, sz.groups * 128)
    return iota(shape, 0) % 8 == (iota(shape, 1) % 128) // sz.cpl


def row_spread(sz):
    shape = (sz.jk * 8, sz.jk)
    return (iota(shape, 0) // 8 == iota(shape, 1)).astype(bf16)


def row_gather(sz):
    shape = (sz.jk, sz.jk * 8)
    return (iota(shape, 1) // 8 == iota(shape, 0)).astype(bf16)


def chan_lanes(sz):
    shape = (sz.groups * 128, sz.chans)
    lane = iota(shape, 0)
    return ((lane // 128) * sz.cpl + lane % sz.cpl == iota(shape, 1)).astype(bf16)


def to_blocks(sz, rows, lg):
    jk = sz.jk
    wide = jnp.concatenate(
        [rows[h * jk : (h + 1) * jk, lg * 128 : (lg + 1) * 128] for h in range(sz.groups)], axis=1
    )
    return jnp.where(diagonal(sz, jk * 8), nn(row_spread(sz), wide), 0.0)


def from_blocks(sz, blocks):
    jk = sz.jk
    pieces = []
    for block in blocks:
        kept = jnp.where(diagonal(sz, jk * 8), block, 0.0).astype(bf16)
        pieces.append(nn(row_gather(sz), kept).astype(bf16))
    return jnp.concatenate(
        [
            jnp.concatenate([piece[:, h * 128 : (h + 1) * 128] for piece in pieces], axis=1)
            for h in range(sz.groups)
        ],
        axis=0,
    )


def send_lines(sz, rows, ya_ref, out_ref):
    jk = sz.jk
    lines = nt(rows, ya_ref[...])
    low = iota((jk, 128), 1) < 64
    for sec in range(2):
        for gy in range(sz.n_gy):
            line = sec * sz.n_gy + gy
            a, b = [lines[h * jk : (h + 1) * jk, line * 128 : (line + 1) * 128] for h in range(2)]
            quarters = [
                jnp.where(low, a, pltpu.roll(b, 64, 1)).astype(bf16),
                jnp.where(low, pltpu.roll(a, 64, 1), b).astype(bf16),
            ]
            for gx in range(sz.n_gx):
                at = ((sec * sz.n_gx + gx) * sz.n_gy + gy) * jk
                out_ref[at : at + jk, :] = quarters[gx % 2]


def lane_group(sz):
    dims = (sz.lgs * sz.jk * 8, sz.lgs * sz.chans)
    return iota(dims, 0) // (sz.jk * 8) == iota(dims, 1) // sz.chans


def mix_kernel(sz, layer, turn, s_ref, r, ya_in, low_hbm, high_hbm, *rest):
    if layer == 0:
        rest = rest[3:]
    spec_hbm, out, *rest = rest
    if layer == 0:
        ya, w, spec_b, blk, mix, sems = rest
    else:
        ya = ya_in
        w, spec_b, blk, mix, sems = rest
    copies = Copies(sems)
    get_ya = copies.start(ya_in, ya) if layer == 0 else None
    get_w = copies.choose(s_ref[0] == layer, [(low_hbm.at[jj], high_hbm.at[jj], w.at[jj]) for jj in range(sz.half_j)])
    spec = line_analysis(sz, r, ya, get_ya, layer > 0)
    spec_b[...] = spec
    copies.send(spec_b, spec_hbm)
    count = sz.jk * 8
    width = sz.lgs * sz.chans
    rep = jnp.concatenate([chan_lanes(sz)] * sz.lgs, axis=1)
    blocks = [to_blocks(sz, spec, lg) for lg in range(sz.lgs)]
    if turn:
        flat = nn(jnp.concatenate(blocks, axis=0).astype(bf16), rep)
        mix[:, :width] = jnp.where(lane_group(sz), flat, 0.0)
        left_ref, right_ref, left_width = mix, blk, width
    else:
        for lg in range(sz.lgs):
            blk[lg * count : (lg + 1) * count, :] = blocks[lg]
        left_ref, right_ref, left_width = blk, mix, blk.shape[1]
    for jk in range(sz.jk):
        jj, kk = jk // sz.blk_k, jk % sz.blk_k
        if kk == 0:
            get_w[jj].wait()
        at = [slice((lg * sz.jk + jk) * 8, (lg * sz.jk + jk + 1) * 8) for lg in range(sz.lgs)]
        left = jnp.concatenate([left_ref[a, :left_width] for a in at], axis=0).astype(bf16)
        part = nt(left, w[jj, kk]) if turn else nn(left, w[jj, kk])
        for lg, a in enumerate(at):
            right_ref[a, : part.shape[1]] = part[lg * 8 : (lg + 1) * 8]
    if not turn:
        kept_mix = jnp.where(lane_group(sz), mix[:, :width], 0.0).astype(bf16)
        full = nt(kept_mix, rep)
    else:
        full = blk[...]
    blocks = [full[lg * count : (lg + 1) * count] for lg in range(sz.lgs)]
    send_lines(sz, from_blocks(sz, blocks), ya, out)
    copies.finish()


def mix_call(sz, layer, turn, s, r, ya, low, high, after=()):
    count = sz.jk * 8 * sz.lgs
    spec = (sz.groups * sz.jk, sz.modes_y * sz.cpl)
    line = (sz.modes, sz.thin)
    outs = [(shape(spec), True), (kept(line), False)]
    if layer == 0:
        outs.append((kept(ya.shape), False))
    else:
        ya = near(ya)
    return run(
        "mix",
        lambda *refs: mix_kernel(sz, layer, turn, *refs),
        outs,
        [smem, vmem, hbm if layer == 0 else vmem, hbm, hbm] + [hbm] * len(after),
        (s, r, ya, low, high) + after,
        [
            pltpu.VMEM(low.shape, bf16),
            pltpu.VMEM(spec, bf16),
            pltpu.VMEM((count, sz.groups * 128), f32),
            pltpu.VMEM((count, sz.groups * 128), f32),
        ],
        sz.half_j + 2,
    )


def gate_kernel(sz, in_ref, after_hbm, out_ref):
    out_ref[...] = in_ref[...]


def gate_call(sz, value, after):
    (out,) = run(
        "gate",
        lambda *refs: gate_kernel(sz, *refs),
        [(kept(value.shape), False)],
        [vmem, hbm],
        (near(value), after),
        micros=0,
    )
    return out


def spec_kernel(sz, s_ref, r, ya, sv0_hbm, sv1_hbm, su1_hbm, mine_hbm, send_hbm, before, mine, sends, sems):
    copies = Copies(sems)
    gets = [copies.start(src, before.at[at]) for at, src in enumerate((sv0_hbm, sv1_hbm, su1_hbm))]
    first = s_ref[0] == 0
    spec = line_analysis(sz, r, ya, None)
    for get in gets:
        get.wait()
    sv0, sv1, su1 = [before[at] for at in range(3)]
    sends[0] = jnp.where(first, sv1, sv0)
    sends[1] = jnp.where(first, su1, spec)
    copies.send(sends, send_hbm)
    mine[0] = jnp.where(first, sv0, sv1)
    mine[1] = jnp.where(first, spec, su1)
    copies.send(mine, mine_hbm)
    copies.finish()


def spec_call(sz, s, r, sv0, sv1, su1, ya):
    spec = (sz.groups * sz.jk, sz.modes_y * sz.cpl)
    return run(
        "spec",
        lambda *refs: spec_kernel(sz, *refs),
        [(shape((2,) + spec), True), (shape((2,) + spec), True)],
        [smem, vmem, vmem, hbm, hbm, hbm],
        (s, r, near(ya), sv0, sv1, su1),
        [pltpu.VMEM((3,) + spec, bf16), pltpu.VMEM((2,) + spec, bf16), pltpu.VMEM((2,) + spec, bf16)],
        5,
    )


def turned_modes(sz, u_ref, layer):
    left = jnp.transpose(u_ref[...])
    half = sz.modes // 2
    if layer == 1:
        left = jnp.concatenate([left[:, half:], left[:, :half]], axis=1)
    return left


CHUNK = 1024


def cuts(sz):
    return [slice(at, at + CHUNK) for at in range(0, sz.wide, CHUNK)]


def small_parts(sz, s_ref, own_ref, other_ref, layer):
    chosen = jnp.where(s_ref[0] == layer, own_ref[...].astype(f32), other_ref[...].astype(f32)).astype(bf16)
    return chosen[: sz.chans], chosen[sz.chans :]


def field_copies(sz, copies, mine_hbm, other_hbm, field):
    return [
        copies.start(mine_hbm, field.at[:, : sz.cells]),
        copies.start(other_hbm, field.at[:, sz.cells :]),
    ]


def thirds(value):
    high = value.astype(bf16)
    rest = value - high.astype(f32)
    middle = rest.astype(bf16)
    return [high, middle, (rest - middle.astype(f32)).astype(bf16)]


def point_sums(sz, v, d):
    pairs = jnp.where(same_y(sz), nt(v, d), 0.0)
    bias = nt(jnp.ones((8, sz.wide), bf16), d)
    dims = (sz.chans, 3 * sz.thin)
    fold = (iota(dims, 1) % sz.thin // sz.fine == iota(dims, 0)).astype(bf16)
    pairs = nn(fold, jnp.concatenate(thirds(pairs), axis=0))
    part = sz.chans // 4
    rows = []
    for t in range(4):
        below = bias if t == 0 else jnp.zeros_like(bias)
        both = jnp.concatenate([pairs[t * part : (t + 1) * part], below], axis=0)
        rows.append(jnp.concatenate(thirds(both), axis=0))
    dims = (4 * sz.thin, 128)
    row = iota(dims, 0)
    place = (row // sz.thin * sz.chans + row % sz.thin // sz.fine == iota(dims, 1)).astype(bf16)
    total = nn(jnp.concatenate(rows, axis=1), place)
    count = part + 8
    return total[:count] + total[count : 2 * count] + total[2 * count :]


def forward_kernel(
    sz, s_ref, own_ref, other_ref, u, mine_hbm, next_hbm, bb_hbm, after_hbm, v, slope, bb, out, field, sems
):
    copies = Copies(sems)
    get_bb, get_v = [], []
    for at, cut in enumerate(cuts(sz)):
        get_bb.append(copies.start(bb_hbm.at[:, cut], bb.at[:, cut]))
        if at == 0:
            get_v = field_copies(sz, copies, mine_hbm, next_hbm, field)
    weight, bias = small_parts(sz, s_ref, own_ref, other_ref, 0)
    matrix = point_matrix(sz, weight, True)
    column = nt(spread(sz), bias)[:, :1]
    left = turned_modes(sz, u, 0)
    for at, cut in enumerate(cuts(sz)):
        get_bb[at].wait()
        if cut.start % sz.cells == 0:
            get_v[cut.start // sz.cells].wait()
        pre = nn(left, bb[:, cut]) + nn(matrix, field[:, cut]) + column
        value, rate = activate(pre)
        v[:, cut] = value.astype(bf16)
        slope[:, cut] = rate
    send_analysis(sz, bb, v[...], out, 1)


def forward_call(sz, s, mine, other, u, bb, own_small, other_small, after):
    field, line = (sz.thin, sz.wide), (sz.modes, sz.thin)
    return run(
        "forward",
        lambda *refs: forward_kernel(sz, *refs),
        [(kept(field), False), (kept(field, f32), False), (kept((sz.modes, sz.wide)), False), (kept(line), False)],
        [smem, vmem, vmem, vmem, hbm, hbm, hbm, hbm],
        (s, own_small, other_small, u, mine, other, bb, after),
        [pltpu.VMEM(field, bf16)],
        2 + len(cuts(sz)),
    )


def turn_kernel(sz, s_ref, own_ref, other_ref, u, v, bb, mine_hbm, next_hbm, d, sums, out, grad, sems):
    copies = Copies(sems)
    get_g = field_copies(sz, copies, mine_hbm, next_hbm, grad)
    weight, bias = small_parts(sz, s_ref, own_ref, other_ref, 1)
    matrix = point_matrix(sz, weight, True)
    column = nt(spread(sz), bias)[:, :1]
    left = turned_modes(sz, u, 1)
    for at, cut in enumerate(cuts(sz)):
        pre = nn(left, bb[:, cut]) + nn(matrix, v[:, cut]) + column
        _, rate = activate(pre)
        if at == 0:
            for get in get_g:
                get.wait()
        d[:, cut] = (grad[:, cut].astype(f32) * rate).astype(bf16)
    send_analysis(sz, bb, d[...], out, 1)
    sums[...] = point_sums(sz, v[...], d[...])


def turn_call(sz, s, mine, other, v, u, bb, own_small, other_small):
    field, line = (sz.thin, sz.wide), (sz.modes, sz.thin)
    return run(
        "turn",
        lambda *refs: turn_kernel(sz, *refs),
        [(kept(field), False), (kept((sz.chans // 4 + 8, 128), f32), False), (kept(line), False)],
        [smem, vmem, vmem, vmem, vmem, vmem, hbm, hbm],
        (s, own_small, other_small, u, near(v), near(bb), mine, other),
        [pltpu.VMEM(field, bf16)],
        2,
    )


def back_kernel(
    sz, s_ref, own_ref, other_ref, u, d, slope, bb, sums, mine_hbm, next_hbm, parts, out, new, field, sems
):
    copies = Copies(sems)
    get_v = field_copies(sz, copies, mine_hbm, next_hbm, field)
    weight, _ = small_parts(sz, s_ref, own_ref, other_ref, 1)
    matrix = point_matrix(sz, weight, False)
    left = turned_modes(sz, u, 1)
    for cut in cuts(sz):
        grad = (nn(left, bb[:, cut]) + nn(matrix, d[:, cut])).astype(bf16).astype(f32)
        new[:, cut] = (grad * slope[:, cut]).astype(bf16)
    send_analysis(sz, bb, new[...], out, 0)
    for get in get_v:
        get.wait()
    first = point_sums(sz, field[...], new[...])
    half = sz.places // 2
    for place in range(half):
        parts[place] = first
        parts[half + place] = sums[...]


def back_call(sz, s, mine, other, d, slope, u, bb, sums, own_small, other_small):
    parts, line, field = (sz.places, sz.chans // 4 + 8, 128), (sz.modes, sz.thin), (sz.thin, sz.wide)
    return run(
        "back",
        lambda *refs: back_kernel(sz, *refs),
        [(kept(parts, f32), False), (kept(line), False)],
        [smem] + [vmem] * 7 + [hbm, hbm],
        (s, own_small, other_small, u, near(d), near(slope), near(bb), near(sums), mine, other),
        [pltpu.VMEM(field, bf16), pltpu.VMEM(field, bf16)],
        2,
    )


def finish_kernel(sz, parts_ref, after_ref, point_ref, bias_ref):
    total = jnp.sum(parts_ref[...], axis=0)
    part = sz.chans // 4
    for t in range(4):
        point_ref[0, t * part : (t + 1) * part, :] = total[:part, t * sz.chans : (t + 1) * sz.chans]
    bias_ref[...] = total[part : part + 1, : sz.chans]


def finish_call(sz, parts, after):
    return pl.pallas_call(
        lambda *refs: finish_kernel(sz, *refs),
        out_shape=(shape((1, sz.chans, sz.chans), f32), shape((1, sz.chans), f32)),
        in_specs=[vmem, hbm],
        out_specs=(vmem, vmem),
        compiler_params=pltpu.CompilerParams(vmem_limit_bytes=limit),
        name="finish",
    )(parts, far(after))


def outer_kernel(sz, mine_ref, theirs_ref, out_ref, left_ref, right_ref):
    jk, groups, kk_count = sz.jk, sz.groups, sz.blk_k
    step = pl.program_id(0)

    def prepare(side, sv, su):
        sv = sv.astype(f32)
        for jj in range(sz.half_j):
            place = side * sz.half_j + jj
            rows = jnp.concatenate(
                [sv[h * jk + jj * kk_count : h * jk + (jj + 1) * kk_count] for h in range(groups)], axis=0
            )
            left_ref[place] = jnp.transpose(rows).astype(bf16)
        for lg in range(sz.lgs):
            flat = nn(to_blocks(sz, su, lg).astype(bf16), chan_lanes(sz))
            for at in range(jk):
                place = side * sz.half_j + at // kk_count
                right_ref[place, at % kk_count, lg * 8 : (lg + 1) * 8, :] = flat[at * 8 : (at + 1) * 8]

    @pl.when(step == 0)
    def _():
        prepare(0, mine_ref[0], mine_ref[1])

    @pl.when(step == 1)
    def _():
        prepare(1, theirs_ref[0], theirs_ref[1])

    dims = (groups * kk_count, groups * kk_count * 128)
    spread_lanes = (iota(dims, 0) == iota(dims, 1) // 128).astype(bf16)
    columns = nn(left_ref[step], spread_lanes)
    for kk in range(kk_count):
        for ll in range(sz.modes_y):
            row = right_ref[step, kk, ll : ll + 1, :]
            for h in range(groups):
                at = (h * kk_count + kk) * 128
                part = columns[ll * sz.cpl : (ll + 1) * sz.cpl, at : at + sz.chans] * row
                out_ref[0, 0, kk, ll, h * sz.cpl : (h + 1) * sz.cpl, :] = part


def outer_call(sz, mine, theirs):
    wide = sz.modes_y * sz.cpl
    return pl.pallas_call(
        lambda *refs: outer_kernel(sz, *refs),
        grid=(sz.blk_j,),
        out_shape=pltpu.HBM((1, sz.blk_j, sz.blk_k, sz.modes_y, sz.chans, sz.chans), f32),
        in_specs=[vmem] * 2,
        out_specs=pl.BlockSpec((1, 1, sz.blk_k, sz.modes_y, sz.chans, sz.chans), lambda i: (0, i, 0, 0, 0, 0)),
        scratch_shapes=[
            pltpu.VMEM((sz.blk_j, wide, sz.groups * sz.blk_k), bf16),
            pltpu.VMEM((sz.blk_j, sz.blk_k, sz.modes_y, sz.chans), f32),
        ],
        compiler_params=pltpu.CompilerParams(vmem_limit_bytes=limit),
        cost_estimate=pl.CostEstimate(flops=0, transcendentals=0, bytes_accessed=20000000),
        name="outer",
    )(mine, theirs)


def exchange(block):
    return lax.all_to_all(block, AXES, split_axis=0, concat_axis=0, tiled=True)


def swap(block):
    return lax.ppermute(block, "section", [(0, 1), (1, 0)])


def swap_near(sz, block):
    return lax.ppermute(block, "gx", [(i, i ^ 1) for i in range(sz.n_gx)])


def local(ends, spectral_weight, point_weight, point_bias):
    sz = Sizes(ends, spectral_weight)
    section = lax.axis_index("section")
    first = section == 0
    s = section.astype(jnp.int32).reshape(1)

    def half(field, which):
        part = lax.dynamic_slice_in_dim(field, which * sz.len_y, sz.len_y, axis=2)
        return jnp.swapaxes(part, 1, 2).reshape(sz.rows, sz.cells)

    bx, bz, by = [jnp.asarray(t.astype(ml_dtypes.bfloat16)) for t in mode_tables(sz)]
    send = half(ends[0], 1 - section)
    send, later = lax.optimization_barrier((send, ends[0]))
    recv = swap(send)
    keep = half(later, section)
    gx = lax.axis_index("gx").astype(jnp.int32)
    gx = jnp.stack([gx, gx + 1 - 2 * (gx % 2)])
    bb = tables_call(sz, gx, bx, bz)
    own_small = jnp.concatenate([point_weight[0], jnp.broadcast_to(point_bias, (16, sz.chans))], axis=0)
    other_small = swap(own_small)
    mine_v, send_v, raw_g, out = first_call(sz, s, gx, keep, recv, bb)
    next_v = swap_near(sz, send_v)
    r = exchange(out)
    high = swap(pack_call(sz, mine_v, spectral_weight, sz.half_j))
    mine_g, send_g = split_call(sz, gx, raw_g, mine_v)
    next_g = swap_near(sz, send_g)
    low, ya = pack_call(sz, mine_v, spectral_weight, 0, by)
    sv0, out, ya = mix_call(sz, 0, False, s, r, ya, low, high, (other_small, mine_g, next_v))
    bb = wide_call(sz, gx, bx, bz, sv0)
    v1, slope0, bb, out = forward_call(sz, s, mine_v, next_v, exchange(out), bb, own_small, other_small, mine_g)
    sv1, out = mix_call(sz, 1, False, s, exchange(out), ya, low, high)
    out = gate_call(sz, out, next_g)
    d1, sums, out = turn_call(sz, s, mine_g, next_g, v1, exchange(out), bb, own_small, other_small)
    su1, out = mix_call(sz, 1, True, s, exchange(out), ya, low, high)
    parts, out = back_call(sz, s, mine_v, next_v, d1, slope0, exchange(out), bb, sums, own_small, other_small)
    r, parts = lax.optimization_barrier((exchange(out), parts))
    mine, send = spec_call(sz, s, r, sv0, sv1, su1, ya)
    theirs = swap(send)
    parts = lax.all_to_all(parts, AXES, split_axis=0, concat_axis=0, tiled=True)
    spectral_grad = outer_call(sz, mine, theirs)
    point_grad, bias_grad = finish_call(sz, parts, spectral_grad)
    return (spectral_grad, point_grad, bias_grad)


def solution(mesh):
    return jax.shard_map(
        local,
        mesh=mesh,
        in_specs=(
            P("section", None, "gx", "gy", None),
            P("section", "gy", "gx", None, None, None),
            P("section", None, None),
            P("section", None),
        ),
        out_specs=(
            P("section", "gy", "gx", None, None, None),
            P("section", None, None),
            P("section", None),
        ),
        check_vma=False,
    )
```

```python
import math

import jax
import jax.numpy as jnp
import ml_dtypes
import numpy as np
from jax import lax
from jax.experimental import pallas as pl
from jax.experimental.pallas import tpu as pltpu
from jax.sharding import PartitionSpec as P

gelu_coef = 0.7978845608028654
f32 = jnp.float32
bf16 = jnp.bfloat16
AXES = ("section", "gx", "gy")


def table(length, count):
    half = count // 2
    modes = np.arange(count)
    is_cos = modes < half
    wave = np.where(is_cos, modes, modes - half + 1)
    phase = wave[:, None] * np.arange(length)[None, :] % length
    angle = phase.astype(np.float32) * np.float32(2.0 * math.pi / length)
    values = np.where(is_cos[:, None], np.cos(angle), np.sin(angle)).astype(np.float32)
    scale = np.where(is_cos & (wave == 0), math.sqrt(1.0 / length), math.sqrt(2.0 / length))
    return (values * scale.astype(np.float32)[:, None]).astype(ml_dtypes.bfloat16).astype(np.float32)


def nn(a, b):
    return lax.dot_general(a, b, (((1,), (0,)), ((), ())), preferred_element_type=f32)


def nt(a, b):
    return lax.dot_general(a, b, (((1,), (1,)), ((), ())), preferred_element_type=f32)


def tn(a, b):
    return lax.dot_general(a, b, (((0,), (0,)), ((), ())), preferred_element_type=f32)


def iota(shape, dim):
    return lax.broadcasted_iota(jnp.int32, shape, dim)


limit = 24 * 1024 * 1024
smem = pl.BlockSpec(memory_space=pltpu.SMEM)
hbm = pl.BlockSpec(memory_space=pltpu.HBM)
vmem = pl.BlockSpec(memory_space=pltpu.VMEM)


def shape(dims, dtype=bf16):
    return jax.ShapeDtypeStruct(dims, dtype)


def kept(dims, dtype=bf16):
    return pltpu.VMEM(dims, dtype)


def near(value):
    return pltpu.with_memory_space_constraint(value, pltpu.VMEM)


def far(value):
    return pltpu.with_memory_space_constraint(value, pltpu.HBM)


def run(name, kernel, outs, specs, args, scratch=(), copies=0, micros=1):
    return pl.pallas_call(
        kernel,
        out_shape=tuple(pltpu.HBM(o.shape, o.dtype) if away else o for o, away in outs),
        in_specs=list(specs),
        out_specs=tuple(hbm if away else vmem for _, away in outs),
        scratch_shapes=list(scratch) + ([pltpu.SemaphoreType.DMA((copies,))] if copies else []),
        compiler_params=pltpu.CompilerParams(vmem_limit_bytes=limit),
        cost_estimate=pl.CostEstimate(flops=0, transcendentals=0, bytes_accessed=micros * 3000000),
        name=name,
    )(*[far(a) if spec is hbm else a for a, spec in zip(args, specs)])


class Copies:
    def __init__(self, sems):
        self.sems = sems
        self.used = 0
        self.open = []

    def make(self, src, dst):
        copy = pltpu.make_async_copy(src, dst, self.sems.at[self.used])
        self.used += 1
        return copy

    def start(self, src, dst):
        copy = self.make(src, dst)
        copy.start()
        return copy

    def choose(self, pick, triples):
        firsts, others = [], []
        for src, other, dst in triples:
            firsts.append(pltpu.make_async_copy(src, dst, self.sems.at[self.used]))
            others.append(self.make(other, dst))

        @pl.when(pick)
        def _():
            for copy in firsts:
                copy.start()

        @pl.when(jnp.logical_not(pick))
        def _():
            for copy in others:
                copy.start()

        return others

    def send(self, src, dst):
        self.open.append(self.start(src, dst))

    def finish(self):
        for copy in self.open:
            copy.wait()


class Sizes:
    def __init__(self, ends, weight):
        self.n_gx = lax.axis_size("gx")
        self.n_gy = lax.axis_size("gy")
        _, self.chans, self.len_x, full, self.depth = ends.shape
        self.len_y = full // 2
        _, self.blk_j, self.blk_k, self.modes_y, _, _ = weight.shape
        self.half_j = self.blk_j // 2
        self.jk = self.half_j * self.blk_k
        self.places = 2 * self.n_gx * self.n_gy
        self.modes = self.places * self.jk
        self.rows = self.chans * self.len_y
        self.cells = self.len_x * self.depth
        self.lines = 2 * self.n_gy
        self.cpl = 128 // self.len_y
        self.groups = self.rows // 128
        self.lgs = self.modes_y // 8
        self.full_x = self.len_x * self.n_gx
        self.fine = self.len_y // 2
        self.thin = self.chans * self.fine
        self.wide = 2 * self.cells
        self.full_y = full * self.n_gy


def mode_tables(sz):
    bx = table(sz.full_x, sz.blk_j * sz.n_gy)
    bz = table(sz.depth, sz.blk_k * sz.n_gx)
    by = table(sz.full_y, sz.modes_y)
    sec, gx, gy, jj, kk = np.meshgrid(
        np.arange(2), np.arange(sz.n_gx), np.arange(sz.n_gy), np.arange(sz.half_j), np.arange(sz.blk_k), indexing="ij"
    )
    row_j = (gy * sz.blk_j + sec * sz.half_j + jj).reshape(-1)
    row_k = (gx * sz.blk_k + kk).reshape(-1)
    sec, gy, yy = np.meshgrid(np.arange(2), np.arange(sz.n_gy), np.arange(sz.len_y), indexing="ij")
    row_y = (gy * 2 * sz.len_y + sec * sz.len_y + yy).reshape(-1)
    bx = np.moveaxis(bx[row_j].reshape(sz.modes, sz.n_gx, sz.len_x), 1, 0)
    lines = by[:, row_y].T.reshape(sz.lines, 2, 1, sz.fine, sz.modes_y)
    lines = np.broadcast_to(lines, (sz.lines, 2, 8 // sz.fine, sz.fine, sz.modes_y)).reshape(-1, sz.modes_y)
    return bx, bz[row_k], np.repeat(lines, sz.cpl, axis=1)


def activate(pre):
    inner = gelu_coef * (pre + 0.044715 * pre * pre * pre)
    tanh_val = jnp.tanh(inner)
    value = 0.5 * pre * (1.0 + tanh_val)
    slope = 0.5 * (1.0 + tanh_val) + 0.5 * pre * (1.0 - tanh_val * tanh_val) * gelu_coef * (
        1.0 + 3.0 * 0.044715 * pre * pre
    )
    return value, slope


def spread(sz):
    shape = (sz.thin, sz.chans)
    return (iota(shape, 0) // sz.fine == iota(shape, 1)).astype(bf16)


def same_y(sz):
    shape = (sz.thin, sz.thin)
    return iota(shape, 0) % sz.fine == iota(shape, 1) % sz.fine


def point_matrix(sz, weight, forward):
    one = spread(sz)
    part = nt(one, weight) if forward else nn(one, weight)
    full = nt(part.astype(bf16), one)
    return jnp.where(same_y(sz), full, 0.0).astype(bf16)


def swapped(rows, half):
    return jnp.concatenate([rows[half:], rows[:half]], axis=0)


def send_analysis(sz, bb_ref, field, out_ref, layer):
    out = nt(bb_ref[...], field).astype(bf16)
    out_ref[...] = swapped(out, sz.modes // 2) if layer == 1 else out


def fill_table(sz, bx, bz, bb):
    depth = sz.depth
    across, along = bx[...].astype(f32), bz[...].astype(f32)
    for x in range(sz.len_x):
        bb[:, x * depth : (x + 1) * depth] = (across[:, x : x + 1] * along).astype(bf16)


def tables_kernel(sz, gx_ref, bx_hbm, bz_hbm, bb, bx, bz, sems):
    copies = Copies(sems)
    get_bx = copies.start(bx_hbm.at[gx_ref[0]], bx)
    get_bz = copies.start(bz_hbm, bz)
    get_bx.wait()
    get_bz.wait()
    fill_table(sz, bx, bz, bb)


def tables_call(sz, gx, bx, bz):
    (bb,) = run(
        "tables",
        lambda *refs: tables_kernel(sz, *refs),
        [(kept((sz.modes, sz.cells)), False)],
        [smem, hbm, hbm],
        (gx, bx, bz),
        [pltpu.VMEM(bx.shape[1:], bf16), pltpu.VMEM(bz.shape, bf16)],
        2,
    )
    return bb


def reorder(sz):
    dims = (sz.rows, sz.rows)
    row = iota(dims, 0)
    group, quarter = row // 128, row % 128 // 64
    chan, y = group * sz.cpl + row % 64 // sz.fine, quarter * sz.fine + row % sz.fine
    return (chan * sz.len_y + y == iota(dims, 1)).astype(bf16)


def send_quarters(sz, gx_ref, field, mine_hbm, send_hbm, copies):
    quarter = gx_ref[0] % 2
    for h in range(sz.groups):
        to = slice(h * 64, (h + 1) * 64)
        copies.send(field.at[pl.ds(h * 128 + quarter * 64, 64)], mine_hbm.at[to])
        copies.send(field.at[pl.ds(h * 128 + (1 - quarter) * 64, 64)], send_hbm.at[to])


def wide_kernel(sz, gx_ref, bx_hbm, bz_hbm, after_hbm, bb_hbm, bx, bz, bb, sems):
    copies = Copies(sems)
    gets = [copies.start(bx_hbm.at[gx_ref[side]], bx.at[side]) for side in range(2)]
    gets.append(copies.start(bz_hbm, bz))
    for get in gets:
        get.wait()
    for side in range(2):
        at = slice(side * sz.cells, (side + 1) * sz.cells)
        fill_table(sz, bx.at[side], bz, bb.at[:, at])
        copies.send(bb.at[:, at], bb_hbm.at[:, at])
    copies.finish()


def wide_call(sz, gx, bx, bz, after):
    (bb,) = run(
        "wide",
        lambda *refs: wide_kernel(sz, *refs),
        [(shape((sz.modes, sz.wide)), True)],
        [smem, hbm, hbm, hbm],
        (gx, bx, bz, after),
        [pltpu.VMEM((2,) + bx.shape[1:], bf16), pltpu.VMEM(bz.shape, bf16), pltpu.VMEM((sz.modes, sz.wide), bf16)],
        5,
        0,
    )
    return bb


def first_kernel(sz, s_ref, gx_ref, keep, recv, bb, mine_hbm, send_hbm, raw_hbm, out_hbm, v, out, sems):
    copies = Copies(sems)
    first = s_ref[0] == 0
    (put_raw,) = copies.choose(first, [(recv, keep, raw_hbm)])
    v[...] = nn(reorder(sz), jnp.where(first, keep[...], recv[...])).astype(bf16)
    send_quarters(sz, gx_ref, v, mine_hbm, send_hbm, copies)
    send_analysis(sz, bb, v[...], out, 0)
    copies.send(out, out_hbm)
    put_raw.wait()
    copies.finish()


def first_call(sz, s, gx, keep, recv, bb):
    line, field, part = (sz.modes, sz.rows), (sz.rows, sz.cells), (sz.thin, sz.cells)
    return run(
        "first",
        lambda *refs: first_kernel(sz, *refs),
        [(shape(part), True), (shape(part), True), (shape(field), True), (shape(line), True)],
        [smem, smem, vmem, vmem, vmem],
        (s, gx, keep, recv, near(bb)),
        [pltpu.VMEM(field, bf16), pltpu.VMEM(line, bf16)],
        2 + 2 * sz.groups,
    )


def split_kernel(sz, gx_ref, raw_hbm, after_hbm, mine_hbm, send_hbm, raw, field, sems):
    copies = Copies(sems)
    copies.start(raw_hbm, raw).wait()
    field[...] = nn(reorder(sz), raw[...]).astype(bf16)
    send_quarters(sz, gx_ref, field, mine_hbm, send_hbm, copies)
    copies.finish()


def split_call(sz, gx, raw, after):
    field, part = (sz.rows, sz.cells), (sz.thin, sz.cells)
    return run(
        "split",
        lambda *refs: split_kernel(sz, *refs),
        [(shape(part), True), (shape(part), True)],
        [smem, hbm, hbm],
        (gx, raw, after),
        [pltpu.VMEM(field, bf16), pltpu.VMEM(field, bf16)],
        1 + 2 * sz.groups,
        0,
    )


def pack_kernel(sz, start, tables, *refs):
    if tables:
        after_hbm, w_hbm, by_hbm, out_hbm, ya_hbm, w, out, by, ya, sems = refs
    else:
        after_hbm, w_hbm, out_hbm, w, out, sems = refs
    copies = Copies(sems)
    if tables:
        get_by = copies.start(by_hbm, by)
    gets = [copies.start(w_hbm.at[0, start + jj], w.at[jj]) for jj in range(sz.half_j)]
    if tables:
        get_by.wait()
        table = by[...].astype(f32)
        wide = sz.modes_y * sz.cpl
        lane_c = iota((8, wide), 1) % sz.cpl
        each = 8 // sz.fine
        row_c = iota((8, wide), 0) // sz.fine
        for g in range(sz.lines):
            pieces = []
            for quarter in range(2):
                at = (g * 2 + quarter) * 8
                part = table[at : at + 8, :]
                pieces += [jnp.where(lane_c == c + row_c, part, 0.0) for c in range(0, sz.cpl, each)]
            ya[g * 128 : (g + 1) * 128, :] = jnp.concatenate(pieces, axis=0).astype(bf16)
        copies.send(ya, ya_hbm)
    for jj in range(sz.half_j):
        gets[jj].wait()
        for kk in range(sz.blk_k):
            for h in range(sz.groups):
                lanes = [
                    w[jj, kk, lg * 8 : (lg + 1) * 8, h * sz.cpl : (h + 1) * sz.cpl, :].reshape(128, sz.chans)
                    for lg in range(sz.lgs)
                ]
                out[jj, kk, h * 128 : (h + 1) * 128, :] = jnp.concatenate(lanes, axis=1)
        copies.send(out.at[jj], out_hbm.at[jj])
    copies.finish()


def pack_call(sz, after, weight, start, by=None):
    half = sz.half_j
    packed = (half, sz.blk_k, sz.groups * 128, sz.lgs * sz.chans)
    lines = (sz.lines * 128, sz.modes_y * sz.cpl)
    outs = [(shape(packed), True)]
    args = (after, weight)
    scratch = [pltpu.VMEM((half,) + weight.shape[2:], bf16), pltpu.VMEM(packed, bf16)]
    tables = by is not None
    if tables:
        outs.append((shape(lines), True))
        args += (by,)
        scratch += [pltpu.VMEM(by.shape, bf16), pltpu.VMEM(lines, bf16)]
    result = run(
        "pack",
        lambda *refs: pack_kernel(sz, start, tables, *refs),
        outs,
        [hbm] * len(args),
        args,
        scratch,
        2 * half + 2 * tables,
        0,
    )
    return result if tables else result[0]


def line_analysis(sz, r_ref, ya_ref, get_ya, fine=True):
    jk = sz.jk

    def total(sec, gy, start, step):
        result = None
        for gx in range(start, sz.n_gx, step):
            at = ((sec * sz.n_gx + gx) * sz.n_gy + gy) * jk
            part = r_ref[at : at + jk, :].astype(f32)
            result = part if result is None else result + part
        return result

    halves = [[], []]
    low = iota((jk, 128), 1) < 64
    for sec in range(2):
        for gy in range(sz.n_gy):
            if fine:
                a, b = total(sec, gy, 0, 2), total(sec, gy, 1, 2)
                halves[0].append(jnp.where(low, a, pltpu.roll(b, 64, 1)).astype(bf16))
                halves[1].append(jnp.where(low, pltpu.roll(a, 64, 1), b).astype(bf16))
            else:
                line = total(sec, gy, 0, 1).astype(bf16)
                for h in range(sz.groups):
                    halves[h].append(line[:, h * 128 : (h + 1) * 128])
    rows = jnp.concatenate([jnp.concatenate(half, axis=1) for half in halves], axis=0)
    if get_ya is not None:
        get_ya.wait()
    return nn(rows, ya_ref[...]).astype(bf16)


def diagonal(sz, count):
    shape = (count, sz.groups * 128)
    return iota(shape, 0) % 8 == (iota(shape, 1) % 128) // sz.cpl


def row_spread(sz):
    shape = (sz.jk * 8, sz.jk)
    return (iota(shape, 0) // 8 == iota(shape, 1)).astype(bf16)


def row_gather(sz):
    shape = (sz.jk, sz.jk * 8)
    return (iota(shape, 1) // 8 == iota(shape, 0)).astype(bf16)


def chan_lanes(sz):
    shape = (sz.groups * 128, sz.chans)
    lane = iota(shape, 0)
    return ((lane // 128) * sz.cpl + lane % sz.cpl == iota(shape, 1)).astype(bf16)


def to_blocks(sz, rows, lg):
    jk = sz.jk
    wide = jnp.concatenate(
        [rows[h * jk : (h + 1) * jk, lg * 128 : (lg + 1) * 128] for h in range(sz.groups)], axis=1
    )
    return jnp.where(diagonal(sz, jk * 8), nn(row_spread(sz), wide), 0.0)


def from_blocks(sz, blocks):
    jk = sz.jk
    pieces = []
    for block in blocks:
        kept = jnp.where(diagonal(sz, jk * 8), block, 0.0).astype(bf16)
        pieces.append(nn(row_gather(sz), kept).astype(bf16))
    return jnp.concatenate(
        [
            jnp.concatenate([piece[:, h * 128 : (h + 1) * 128] for piece in pieces], axis=1)
            for h in range(sz.groups)
        ],
        axis=0,
    )


def send_lines(sz, rows, ya_ref, out_ref):
    jk = sz.jk
    lines = nt(rows, ya_ref[...])
    low = iota((jk, 128), 1) < 64
    for sec in range(2):
        for gy in range(sz.n_gy):
            line = sec * sz.n_gy + gy
            a, b = [lines[h * jk : (h + 1) * jk, line * 128 : (line + 1) * 128] for h in range(2)]
            quarters = [
                jnp.where(low, a, pltpu.roll(b, 64, 1)).astype(bf16),
                jnp.where(low, pltpu.roll(a, 64, 1), b).astype(bf16),
            ]
            for gx in range(sz.n_gx):
                at = ((sec * sz.n_gx + gx) * sz.n_gy + gy) * jk
                out_ref[at : at + jk, :] = quarters[gx % 2]


def lane_group(sz):
    dims = (sz.lgs * sz.jk * 8, sz.lgs * sz.chans)
    return iota(dims, 0) // (sz.jk * 8) == iota(dims, 1) // sz.chans


def mix_kernel(sz, layer, turn, s_ref, r, ya_in, *rest):
    if layer == 0:
        low_hbm, high_hbm, *rest = rest
        spec_hbm, out, ya, w, spec_b, blk, mix, sems = rest[3:]
    else:
        ya = ya_in
        w, spec_hbm, out, spec_b, blk, mix, sems = rest
    copies = Copies(sems)
    get_ya = copies.start(ya_in, ya) if layer == 0 else None
    if layer == 0:
        get_w = copies.choose(s_ref[0] == 0, [(low_hbm.at[jj], high_hbm.at[jj], w.at[jj]) for jj in range(sz.half_j)])
    spec = line_analysis(sz, r, ya, get_ya, layer > 0)
    spec_b[...] = spec
    copies.send(spec_b, spec_hbm)
    count = sz.jk * 8
    width = sz.lgs * sz.chans
    rep = jnp.concatenate([chan_lanes(sz)] * sz.lgs, axis=1)
    blocks = [to_blocks(sz, spec, lg) for lg in range(sz.lgs)]
    if turn:
        flat = nn(jnp.concatenate(blocks, axis=0).astype(bf16), rep)
        mix[:, :width] = jnp.where(lane_group(sz), flat, 0.0)
        left_ref, right_ref, left_width = mix, blk, width
    else:
        for lg in range(sz.lgs):
            blk[lg * count : (lg + 1) * count, :] = blocks[lg]
        left_ref, right_ref, left_width = blk, mix, blk.shape[1]
    for jk in range(sz.jk):
        jj, kk = jk // sz.blk_k, jk % sz.blk_k
        if kk == 0 and layer == 0:
            get_w[jj].wait()
        at = [slice((lg * sz.jk + jk) * 8, (lg * sz.jk + jk + 1) * 8) for lg in range(sz.lgs)]
        left = jnp.concatenate([left_ref[a, :left_width] for a in at], axis=0).astype(bf16)
        part = nt(left, w[jj, kk]) if turn else nn(left, w[jj, kk])
        for lg, a in enumerate(at):
            right_ref[a, : part.shape[1]] = part[lg * 8 : (lg + 1) * 8]
    if not turn:
        kept_mix = jnp.where(lane_group(sz), mix[:, :width], 0.0).astype(bf16)
        full = nt(kept_mix, rep)
    else:
        full = blk[...]
    blocks = [full[lg * count : (lg + 1) * count] for lg in range(sz.lgs)]
    send_lines(sz, from_blocks(sz, blocks), ya, out)
    copies.finish()


def mix_call(sz, layer, turn, s, r, ya, weights, after=()):
    count = sz.jk * 8 * sz.lgs
    spec = (sz.groups * sz.jk, sz.modes_y * sz.cpl)
    line = (sz.modes, sz.thin)
    outs = [(shape(spec), True), (kept(line), False)]
    scratch = [pltpu.VMEM(spec, bf16)] + [pltpu.VMEM((count, sz.groups * 128), f32)] * 2
    if layer == 0:
        outs.append((kept(ya.shape), False))
        scratch = [pltpu.VMEM(weights[0].shape, bf16)] + scratch
        specs = [smem, vmem] + [hbm] * (3 + len(after))
    else:
        ya = near(ya)
        weights = [near(weights)]
        specs = [smem] + [vmem] * 3
    return run(
        "mix",
        lambda *refs: mix_kernel(sz, layer, turn, *refs),
        outs,
        specs,
        (s, r, ya, *weights, *after),
        scratch,
        sz.half_j + 2,
    )


def gate_kernel(sz, in_ref, after_hbm, out_ref):
    out_ref[...] = in_ref[...]


def gate_call(sz, value, after):
    (out,) = run(
        "gate",
        lambda *refs: gate_kernel(sz, *refs),
        [(kept(value.shape), False)],
        [vmem, hbm],
        (near(value), after),
        micros=0,
    )
    return out


def spec_kernel(sz, s_ref, r, ya, sv0_hbm, sv1_hbm, su1_hbm, mine, sends, before, sems):
    copies = Copies(sems)
    gets = [copies.start(src, before.at[at]) for at, src in enumerate((sv0_hbm, sv1_hbm, su1_hbm))]
    first = s_ref[0] == 0
    spec = line_analysis(sz, r, ya, None)
    for get in gets:
        get.wait()
    sv0, sv1, su1 = [before[at] for at in range(3)]
    sends[0] = jnp.where(first, sv1, sv0)
    sends[1] = jnp.where(first, su1, spec)
    mine[0] = jnp.where(first, sv0, sv1)
    mine[1] = jnp.where(first, spec, su1)


def spec_call(sz, s, r, sv0, sv1, su1, ya):
    spec = (sz.groups * sz.jk, sz.modes_y * sz.cpl)
    return run(
        "spec",
        lambda *refs: spec_kernel(sz, *refs),
        [(kept((2,) + spec), False), (kept((2,) + spec), False)],
        [smem, vmem, vmem, hbm, hbm, hbm],
        (s, r, near(ya), sv0, sv1, su1),
        [pltpu.VMEM((3,) + spec, bf16)],
        3,
    )


def turned_modes(sz, u_ref, layer):
    left = jnp.transpose(u_ref[...])
    half = sz.modes // 2
    if layer == 1:
        left = jnp.concatenate([left[:, half:], left[:, :half]], axis=1)
    return left


CHUNK = 1024


def cuts(sz):
    return [slice(at, at + CHUNK) for at in range(0, sz.wide, CHUNK)]


def small_parts(sz, s_ref, own_ref, other_ref, layer):
    chosen = jnp.where(s_ref[0] == layer, own_ref[...].astype(f32), other_ref[...].astype(f32)).astype(bf16)
    return chosen[: sz.chans], chosen[sz.chans :]


def field_copies(sz, copies, mine_hbm, other_hbm, field):
    return [
        copies.start(mine_hbm, field.at[:, : sz.cells]),
        copies.start(other_hbm, field.at[:, sz.cells :]),
    ]


def thirds(value):
    high = value.astype(bf16)
    rest = value - high.astype(f32)
    middle = rest.astype(bf16)
    return [high, middle, (rest - middle.astype(f32)).astype(bf16)]


def point_sums(sz, v, d):
    pairs = jnp.where(same_y(sz), nt(v, d), 0.0)
    bias = nt(jnp.ones((8, sz.wide), bf16), d)
    dims = (sz.chans, 3 * sz.thin)
    fold = (iota(dims, 1) % sz.thin // sz.fine == iota(dims, 0)).astype(bf16)
    pairs = nn(fold, jnp.concatenate(thirds(pairs), axis=0))
    part = sz.chans // 4
    rows = []
    for t in range(4):
        below = bias if t == 0 else jnp.zeros_like(bias)
        both = jnp.concatenate([pairs[t * part : (t + 1) * part], below], axis=0)
        rows.append(jnp.concatenate(thirds(both), axis=0))
    dims = (4 * sz.thin, 128)
    row = iota(dims, 0)
    place = (row // sz.thin * sz.chans + row % sz.thin // sz.fine == iota(dims, 1)).astype(bf16)
    total = nn(jnp.concatenate(rows, axis=1), place)
    count = part + 8
    return total[:count] + total[count : 2 * count] + total[2 * count :]


def forward_kernel(
    sz, s_ref, own_ref, other_ref, u, mine_hbm, next_hbm, bb_hbm, low_hbm, high_hbm, v, slope, bb, out, w, field, sems
):
    copies = Copies(sems)
    get_bb, get_v = [], []
    for at, cut in enumerate(cuts(sz)):
        get_bb.append(copies.start(bb_hbm.at[:, cut], bb.at[:, cut]))
        if at == 0:
            get_v = field_copies(sz, copies, mine_hbm, next_hbm, field)
    (get_w,) = copies.choose(s_ref[0] == 1, [(low_hbm, high_hbm, w)])
    weight, bias = small_parts(sz, s_ref, own_ref, other_ref, 0)
    matrix = point_matrix(sz, weight, True)
    column = nt(spread(sz), bias)[:, :1]
    left = turned_modes(sz, u, 0)
    for at, cut in enumerate(cuts(sz)):
        get_bb[at].wait()
        if cut.start % sz.cells == 0:
            get_v[cut.start // sz.cells].wait()
        pre = nn(left, bb[:, cut]) + nn(matrix, field[:, cut]) + column
        value, rate = activate(pre)
        v[:, cut] = value.astype(bf16)
        slope[:, cut] = rate
    send_analysis(sz, bb, v[...], out, 1)
    get_w.wait()


def forward_call(sz, s, mine, other, u, bb, own_small, other_small, low, high):
    field, line = (sz.thin, sz.wide), (sz.modes, sz.thin)
    return run(
        "forward",
        lambda *refs: forward_kernel(sz, *refs),
        [
            (kept(field), False),
            (kept(field, f32), False),
            (kept((sz.modes, sz.wide)), False),
            (kept(line), False),
            (kept(low.shape), False),
        ],
        [smem, vmem, vmem, vmem, hbm, hbm, hbm, hbm, hbm],
        (s, own_small, other_small, u, mine, other, bb, low, high),
        [pltpu.VMEM(field, bf16)],
        3 + len(cuts(sz)),
    )


def turn_kernel(sz, s_ref, own_ref, other_ref, u, v, bb, mine_hbm, next_hbm, d, sums, out, grad, sems):
    copies = Copies(sems)
    get_g = field_copies(sz, copies, mine_hbm, next_hbm, grad)
    weight, bias = small_parts(sz, s_ref, own_ref, other_ref, 1)
    matrix = point_matrix(sz, weight, True)
    column = nt(spread(sz), bias)[:, :1]
    left = turned_modes(sz, u, 1)
    for at, cut in enumerate(cuts(sz)):
        pre = nn(left, bb[:, cut]) + nn(matrix, v[:, cut]) + column
        _, rate = activate(pre)
        if at == 0:
            for get in get_g:
                get.wait()
        d[:, cut] = (grad[:, cut].astype(f32) * rate).astype(bf16)
    send_analysis(sz, bb, d[...], out, 1)
    sums[...] = point_sums(sz, v[...], d[...])


def turn_call(sz, s, mine, other, v, u, bb, own_small, other_small):
    field, line = (sz.thin, sz.wide), (sz.modes, sz.thin)
    return run(
        "turn",
        lambda *refs: turn_kernel(sz, *refs),
        [(kept(field), False), (kept((sz.chans // 4 + 8, 128), f32), False), (kept(line), False)],
        [smem, vmem, vmem, vmem, vmem, vmem, hbm, hbm],
        (s, own_small, other_small, u, near(v), near(bb), mine, other),
        [pltpu.VMEM(field, bf16)],
        2,
    )


def back_kernel(
    sz, s_ref, own_ref, other_ref, u, d, slope, bb, sums, mine_hbm, next_hbm, parts, out, new, field, sems
):
    copies = Copies(sems)
    get_v = field_copies(sz, copies, mine_hbm, next_hbm, field)
    weight, _ = small_parts(sz, s_ref, own_ref, other_ref, 1)
    matrix = point_matrix(sz, weight, False)
    left = turned_modes(sz, u, 1)
    for cut in cuts(sz):
        grad = (nn(left, bb[:, cut]) + nn(matrix, d[:, cut])).astype(bf16).astype(f32)
        new[:, cut] = (grad * slope[:, cut]).astype(bf16)
    for get in get_v:
        get.wait()
    send_analysis(sz, bb, new[...], out, 0)
    first = point_sums(sz, field[...], new[...])
    half = sz.places // 2
    for place in range(half):
        parts[place] = first
        parts[half + place] = sums[...]


def back_call(sz, s, mine, other, d, slope, u, bb, sums, own_small, other_small):
    parts, line, field = (sz.places, sz.chans // 4 + 8, 128), (sz.modes, sz.thin), (sz.thin, sz.wide)
    return run(
        "back",
        lambda *refs: back_kernel(sz, *refs),
        [(kept(parts, f32), False), (kept(line), False)],
        [smem] + [vmem] * 7 + [hbm, hbm],
        (s, own_small, other_small, u, near(d), near(slope), near(bb), near(sums), mine, other),
        [pltpu.VMEM(field, bf16), pltpu.VMEM(field, bf16)],
        2,
    )


def finish_kernel(sz, parts_ref, after_ref, point_ref, bias_ref):
    total = jnp.sum(parts_ref[...], axis=0)
    part = sz.chans // 4
    for t in range(4):
        point_ref[0, t * part : (t + 1) * part, :] = total[:part, t * sz.chans : (t + 1) * sz.chans]
    bias_ref[...] = total[part : part + 1, : sz.chans]


def finish_call(sz, parts, after):
    return pl.pallas_call(
        lambda *refs: finish_kernel(sz, *refs),
        out_shape=(shape((1, sz.chans, sz.chans), f32), shape((1, sz.chans), f32)),
        in_specs=[vmem, hbm],
        out_specs=(vmem, vmem),
        compiler_params=pltpu.CompilerParams(vmem_limit_bytes=limit),
        name="finish",
    )(parts, far(after))


def outer_kernel(sz, mine_ref, theirs_ref, out_ref, left_ref, right_ref):
    jk, groups, kk_count = sz.jk, sz.groups, sz.blk_k
    step = pl.program_id(0)

    def prepare(side, sv, su):
        sv = sv.astype(f32)
        for jj in range(sz.half_j):
            place = side * sz.half_j + jj
            rows = jnp.concatenate(
                [sv[h * jk + jj * kk_count : h * jk + (jj + 1) * kk_count] for h in range(groups)], axis=0
            )
            left_ref[place] = jnp.transpose(rows).astype(bf16)
        for lg in range(sz.lgs):
            flat = nn(to_blocks(sz, su, lg).astype(bf16), chan_lanes(sz))
            for at in range(jk):
                place = side * sz.half_j + at // kk_count
                right_ref[place, at % kk_count, lg * 8 : (lg + 1) * 8, :] = flat[at * 8 : (at + 1) * 8]

    @pl.when(step == 0)
    def _():
        prepare(0, mine_ref[0], mine_ref[1])

    @pl.when(step == 1)
    def _():
        prepare(1, theirs_ref[0], theirs_ref[1])

    dims = (groups * kk_count, groups * kk_count * 128)
    spread_lanes = (iota(dims, 0) == iota(dims, 1) // 128).astype(bf16)
    columns = nn(left_ref[step], spread_lanes)
    for kk in range(kk_count):
        for ll in range(sz.modes_y):
            row = right_ref[step, kk, ll : ll + 1, :]
            for h in range(groups):
                at = (h * kk_count + kk) * 128
                part = columns[ll * sz.cpl : (ll + 1) * sz.cpl, at : at + sz.chans] * row
                out_ref[0, 0, kk, ll, h * sz.cpl : (h + 1) * sz.cpl, :] = part


def outer_call(sz, mine, theirs):
    wide = sz.modes_y * sz.cpl
    return pl.pallas_call(
        lambda *refs: outer_kernel(sz, *refs),
        grid=(sz.blk_j,),
        out_shape=pltpu.HBM((1, sz.blk_j, sz.blk_k, sz.modes_y, sz.chans, sz.chans), f32),
        in_specs=[vmem] * 2,
        out_specs=pl.BlockSpec((1, 1, sz.blk_k, sz.modes_y, sz.chans, sz.chans), lambda i: (0, i, 0, 0, 0, 0)),
        scratch_shapes=[
            pltpu.VMEM((sz.blk_j, wide, sz.groups * sz.blk_k), bf16),
            pltpu.VMEM((sz.blk_j, sz.blk_k, sz.modes_y, sz.chans), f32),
        ],
        compiler_params=pltpu.CompilerParams(vmem_limit_bytes=limit),
        cost_estimate=pl.CostEstimate(flops=0, transcendentals=0, bytes_accessed=20000000),
        name="outer",
    )(near(mine), theirs)


def exchange(block):
    return lax.all_to_all(block, AXES, split_axis=0, concat_axis=0, tiled=True)


def swap(block):
    return lax.ppermute(block, "section", [(0, 1), (1, 0)])


def swap_near(sz, block):
    return lax.ppermute(block, "gx", [(i, i ^ 1) for i in range(sz.n_gx)])


def local(ends, spectral_weight, point_weight, point_bias):
    sz = Sizes(ends, spectral_weight)
    section = lax.axis_index("section")
    first = section == 0
    s = section.astype(jnp.int32).reshape(1)

    def half(field, which):
        part = lax.dynamic_slice_in_dim(field, which * sz.len_y, sz.len_y, axis=2)
        return jnp.swapaxes(part, 1, 2).reshape(sz.rows, sz.cells)

    bx, bz, by = [jnp.asarray(t.astype(ml_dtypes.bfloat16)) for t in mode_tables(sz)]
    send = half(ends[0], 1 - section)
    send, later = lax.optimization_barrier((send, ends[0]))
    recv = swap(send)
    keep = half(later, section)
    gx = lax.axis_index("gx").astype(jnp.int32)
    gx = jnp.stack([gx, gx + 1 - 2 * (gx % 2)])
    bb = tables_call(sz, gx, bx, bz)
    own_small = jnp.concatenate([point_weight[0], jnp.broadcast_to(point_bias, (16, sz.chans))], axis=0)
    other_small = swap(own_small)
    mine_v, send_v, raw_g, out = first_call(sz, s, gx, keep, recv, bb)
    next_v = swap_near(sz, send_v)
    r = exchange(out)
    high = swap(pack_call(sz, mine_v, spectral_weight, sz.half_j))
    mine_g, send_g = split_call(sz, gx, raw_g, mine_v)
    next_g = swap_near(sz, send_g)
    low, ya = pack_call(sz, mine_v, spectral_weight, 0, by)
    sv0, out, ya = mix_call(sz, 0, False, s, r, ya, (low, high), (other_small, mine_g, next_v))
    bb = wide_call(sz, gx, bx, bz, sv0)
    v1, slope0, bb, out, w1 = forward_call(sz, s, mine_v, next_v, exchange(out), bb, own_small, other_small, low, high)
    sv1, out = mix_call(sz, 1, False, s, exchange(out), ya, w1)
    out = gate_call(sz, out, next_g)
    d1, sums, out = turn_call(sz, s, mine_g, next_g, v1, exchange(out), bb, own_small, other_small)
    su1, out = mix_call(sz, 1, True, s, exchange(out), ya, w1)
    parts, out = back_call(sz, s, mine_v, next_v, d1, slope0, exchange(out), bb, sums, own_small, other_small)
    r, parts = lax.optimization_barrier((exchange(out), parts))
    mine, send = spec_call(sz, s, r, sv0, sv1, su1, ya)
    theirs = swap(send)
    parts = lax.all_to_all(parts, AXES, split_axis=0, concat_axis=0, tiled=True)
    spectral_grad = outer_call(sz, mine, theirs)
    point_grad, bias_grad = finish_call(sz, parts, spectral_grad)
    return (spectral_grad, point_grad, bias_grad)


def solution(mesh):
    return jax.shard_map(
        local,
        mesh=mesh,
        in_specs=(
            P("section", None, "gx", "gy", None),
            P("section", "gy", "gx", None, None, None),
            P("section", None, None),
            P("section", None),
        ),
        out_specs=(
            P("section", "gy", "gx", None, None, None),
            P("section", None, None),
            P("section", None),
        ),
        check_vma=False,
    )
```

```python
import math

import jax
import jax.numpy as jnp
import ml_dtypes
import numpy as np
from jax import lax
from jax.experimental import pallas as pl
from jax.experimental.pallas import tpu as pltpu
from jax.sharding import PartitionSpec as P

gelu_coef = 0.7978845608028654
f32 = jnp.float32
bf16 = jnp.bfloat16
AXES = ("section", "gx", "gy")


def table(length, count):
    half = count // 2
    modes = np.arange(count)
    is_cos = modes < half
    wave = np.where(is_cos, modes, modes - half + 1)
    phase = wave[:, None] * np.arange(length)[None, :] % length
    angle = phase.astype(np.float32) * np.float32(2.0 * math.pi / length)
    values = np.where(is_cos[:, None], np.cos(angle), np.sin(angle)).astype(np.float32)
    scale = np.where(is_cos & (wave == 0), math.sqrt(1.0 / length), math.sqrt(2.0 / length))
    return (values * scale.astype(np.float32)[:, None]).astype(ml_dtypes.bfloat16).astype(np.float32)


def nn(a, b):
    return lax.dot_general(a, b, (((1,), (0,)), ((), ())), preferred_element_type=f32)


def nt(a, b):
    return lax.dot_general(a, b, (((1,), (1,)), ((), ())), preferred_element_type=f32)


def tn(a, b):
    return lax.dot_general(a, b, (((0,), (0,)), ((), ())), preferred_element_type=f32)


def iota(shape, dim):
    return lax.broadcasted_iota(jnp.int32, shape, dim)


limit = 24 * 1024 * 1024
smem = pl.BlockSpec(memory_space=pltpu.SMEM)
hbm = pl.BlockSpec(memory_space=pltpu.HBM)
vmem = pl.BlockSpec(memory_space=pltpu.VMEM)


def shape(dims, dtype=bf16):
    return jax.ShapeDtypeStruct(dims, dtype)


def kept(dims, dtype=bf16):
    return pltpu.VMEM(dims, dtype)


def near(value):
    return pltpu.with_memory_space_constraint(value, pltpu.VMEM)


def far(value):
    return pltpu.with_memory_space_constraint(value, pltpu.HBM)


def run(name, kernel, outs, specs, args, scratch=(), copies=0, micros=1):
    return pl.pallas_call(
        kernel,
        out_shape=tuple(pltpu.HBM(o.shape, o.dtype) if away else o for o, away in outs),
        in_specs=list(specs),
        out_specs=tuple(hbm if away else vmem for _, away in outs),
        scratch_shapes=list(scratch) + ([pltpu.SemaphoreType.DMA((copies,))] if copies else []),
        compiler_params=pltpu.CompilerParams(vmem_limit_bytes=limit),
        cost_estimate=pl.CostEstimate(flops=0, transcendentals=0, bytes_accessed=micros * 3000000),
        name=name,
    )(*[far(a) if spec is hbm else a for a, spec in zip(args, specs)])


class Copies:
    def __init__(self, sems):
        self.sems = sems
        self.used = 0
        self.open = []

    def make(self, src, dst):
        copy = pltpu.make_async_copy(src, dst, self.sems.at[self.used])
        self.used += 1
        return copy

    def start(self, src, dst):
        copy = self.make(src, dst)
        copy.start()
        return copy

    def choose(self, pick, triples):
        firsts, others = [], []
        for src, other, dst in triples:
            firsts.append(pltpu.make_async_copy(src, dst, self.sems.at[self.used]))
            others.append(self.make(other, dst))

        @pl.when(pick)
        def _():
            for copy in firsts:
                copy.start()

        @pl.when(jnp.logical_not(pick))
        def _():
            for copy in others:
                copy.start()

        return others

    def send(self, src, dst):
        self.open.append(self.start(src, dst))

    def finish(self):
        for copy in self.open:
            copy.wait()


class Sizes:
    def __init__(self, ends, weight):
        self.n_gx = lax.axis_size("gx")
        self.n_gy = lax.axis_size("gy")
        _, self.chans, self.len_x, full, self.depth = ends.shape
        self.len_y = full // 2
        _, self.blk_j, self.blk_k, self.modes_y, _, _ = weight.shape
        self.half_j = self.blk_j // 2
        self.jk = self.half_j * self.blk_k
        self.places = 2 * self.n_gx * self.n_gy
        self.modes = self.places * self.jk
        self.rows = self.chans * self.len_y
        self.cells = self.len_x * self.depth
        self.lines = 2 * self.n_gy
        self.cpl = 128 // self.len_y
        self.groups = self.rows // 128
        self.lgs = self.modes_y // 8
        self.full_x = self.len_x * self.n_gx
        self.fine = self.len_y // 2
        self.thin = self.chans * self.fine
        self.wide = 2 * self.cells
        self.full_y = full * self.n_gy


def mode_tables(sz):
    bx = table(sz.full_x, sz.blk_j * sz.n_gy)
    bz = table(sz.depth, sz.blk_k * sz.n_gx)
    by = table(sz.full_y, sz.modes_y)
    sec, gx, gy, jj, kk = np.meshgrid(
        np.arange(2), np.arange(sz.n_gx), np.arange(sz.n_gy), np.arange(sz.half_j), np.arange(sz.blk_k), indexing="ij"
    )
    row_j = (gy * sz.blk_j + sec * sz.half_j + jj).reshape(-1)
    row_k = (gx * sz.blk_k + kk).reshape(-1)
    sec, gy, yy = np.meshgrid(np.arange(2), np.arange(sz.n_gy), np.arange(sz.len_y), indexing="ij")
    row_y = (gy * 2 * sz.len_y + sec * sz.len_y + yy).reshape(-1)
    bx = np.moveaxis(bx[row_j].reshape(sz.modes, sz.n_gx, sz.len_x), 1, 0)
    lines = by[:, row_y].T.reshape(sz.lines, 2, 1, sz.fine, sz.modes_y)
    lines = np.broadcast_to(lines, (sz.lines, 2, 8 // sz.fine, sz.fine, sz.modes_y)).reshape(-1, sz.modes_y)
    return bx, bz[row_k], np.repeat(lines, sz.cpl, axis=1)


def activate(pre):
    square = pre * pre
    tanh_val = jnp.tanh(pre * (gelu_coef + (gelu_coef * 0.044715) * square))
    half = 0.5 + 0.5 * tanh_val
    value = pre * half
    slope = half + value * (1.0 - tanh_val) * (gelu_coef + (3.0 * gelu_coef * 0.044715) * square)
    return value, slope


def spread(sz):
    shape = (sz.thin, sz.chans)
    return (iota(shape, 0) // sz.fine == iota(shape, 1)).astype(bf16)


def same_y(sz):
    shape = (sz.thin, sz.thin)
    return iota(shape, 0) % sz.fine == iota(shape, 1) % sz.fine


def point_matrix(sz, weight, forward):
    one = spread(sz)
    part = nt(one, weight) if forward else nn(one, weight)
    full = nt(part.astype(bf16), one)
    return jnp.where(same_y(sz), full, 0.0).astype(bf16)


def swapped(rows, half):
    return jnp.concatenate([rows[half:], rows[:half]], axis=0)


def send_analysis(sz, bb_ref, field, out_ref, layer):
    out = nt(bb_ref[...], field).astype(bf16)
    out_ref[...] = swapped(out, sz.modes // 2) if layer == 1 else out


def fill_table(sz, bx, bz, bb):
    depth = sz.depth
    across, along = bx[...].astype(f32), bz[...].astype(f32)
    for x in range(sz.len_x):
        bb[:, x * depth : (x + 1) * depth] = (across[:, x : x + 1] * along).astype(bf16)


def tables_kernel(sz, gx_ref, bx_hbm, bz_hbm, bb, bx, bz, sems):
    copies = Copies(sems)
    get_bx = copies.start(bx_hbm.at[gx_ref[0]], bx)
    get_bz = copies.start(bz_hbm, bz)
    get_bx.wait()
    get_bz.wait()
    fill_table(sz, bx, bz, bb)


def tables_call(sz, gx, bx, bz):
    (bb,) = run(
        "tables",
        lambda *refs: tables_kernel(sz, *refs),
        [(kept((sz.modes, sz.cells)), False)],
        [smem, hbm, hbm],
        (gx, bx, bz),
        [pltpu.VMEM(bx.shape[1:], bf16), pltpu.VMEM(bz.shape, bf16)],
        2,
    )
    return bb


def reorder(sz):
    dims = (sz.rows, sz.rows)
    row = iota(dims, 0)
    group, quarter = row // 128, row % 128 // 64
    chan, y = group * sz.cpl + row % 64 // sz.fine, quarter * sz.fine + row % sz.fine
    return (chan * sz.len_y + y == iota(dims, 1)).astype(bf16)


def send_quarters(sz, gx_ref, field, mine_hbm, send_hbm, copies):
    quarter = gx_ref[0] % 2
    for h in range(sz.groups):
        to = slice(h * 64, (h + 1) * 64)
        copies.send(field.at[pl.ds(h * 128 + quarter * 64, 64)], mine_hbm.at[to])
        copies.send(field.at[pl.ds(h * 128 + (1 - quarter) * 64, 64)], send_hbm.at[to])


def wide_kernel(sz, gx_ref, bx_hbm, bz_hbm, after_hbm, bb_hbm, bx, bz, bb, sems):
    copies = Copies(sems)
    gets = [copies.start(bx_hbm.at[gx_ref[side]], bx.at[side]) for side in range(2)]
    gets.append(copies.start(bz_hbm, bz))
    for get in gets:
        get.wait()
    for side in range(2):
        at = slice(side * sz.cells, (side + 1) * sz.cells)
        fill_table(sz, bx.at[side], bz, bb.at[:, at])
        copies.send(bb.at[:, at], bb_hbm.at[:, at])
    copies.finish()


def wide_call(sz, gx, bx, bz, after):
    (bb,) = run(
        "wide",
        lambda *refs: wide_kernel(sz, *refs),
        [(shape((sz.modes, sz.wide)), True)],
        [smem, hbm, hbm, hbm],
        (gx, bx, bz, after),
        [pltpu.VMEM((2,) + bx.shape[1:], bf16), pltpu.VMEM(bz.shape, bf16), pltpu.VMEM((sz.modes, sz.wide), bf16)],
        5,
        0,
    )
    return bb


def first_kernel(sz, s_ref, gx_ref, keep, recv, bb, mine_hbm, send_hbm, raw_hbm, out_hbm, v, out, sems):
    copies = Copies(sems)
    first = s_ref[0] == 0
    (put_raw,) = copies.choose(first, [(recv, keep, raw_hbm)])
    v[...] = nn(reorder(sz), jnp.where(first, keep[...], recv[...])).astype(bf16)
    send_quarters(sz, gx_ref, v, mine_hbm, send_hbm, copies)
    send_analysis(sz, bb, v[...], out, 0)
    copies.send(out, out_hbm)
    put_raw.wait()
    copies.finish()


def first_call(sz, s, gx, keep, recv, bb):
    line, field, part = (sz.modes, sz.rows), (sz.rows, sz.cells), (sz.thin, sz.cells)
    return run(
        "first",
        lambda *refs: first_kernel(sz, *refs),
        [(shape(part), True), (shape(part), True), (shape(field), True), (shape(line), True)],
        [smem, smem, vmem, vmem, vmem],
        (s, gx, keep, recv, near(bb)),
        [pltpu.VMEM(field, bf16), pltpu.VMEM(line, bf16)],
        2 + 2 * sz.groups,
    )


def split_kernel(sz, gx_ref, raw_hbm, after_hbm, mine_hbm, send_hbm, raw, field, sems):
    copies = Copies(sems)
    copies.start(raw_hbm, raw).wait()
    field[...] = nn(reorder(sz), raw[...]).astype(bf16)
    send_quarters(sz, gx_ref, field, mine_hbm, send_hbm, copies)
    copies.finish()


def split_call(sz, gx, raw, after):
    field, part = (sz.rows, sz.cells), (sz.thin, sz.cells)
    return run(
        "split",
        lambda *refs: split_kernel(sz, *refs),
        [(shape(part), True), (shape(part), True)],
        [smem, hbm, hbm],
        (gx, raw, after),
        [pltpu.VMEM(field, bf16), pltpu.VMEM(field, bf16)],
        1 + 2 * sz.groups,
        0,
    )


def pack_kernel(sz, start, tables, *refs):
    if tables:
        after_hbm, w_hbm, by_hbm, out_hbm, ya_hbm, w, out, by, ya, sems = refs
    else:
        after_hbm, w_hbm, out_hbm, w, out, sems = refs
    copies = Copies(sems)
    if tables:
        get_by = copies.start(by_hbm, by)
    gets = [copies.start(w_hbm.at[0, start + jj], w.at[jj]) for jj in range(sz.half_j)]
    if tables:
        get_by.wait()
        table = by[...].astype(f32)
        wide = sz.modes_y * sz.cpl
        lane_c = iota((8, wide), 1) % sz.cpl
        each = 8 // sz.fine
        row_c = iota((8, wide), 0) // sz.fine
        for g in range(sz.lines):
            pieces = []
            for quarter in range(2):
                at = (g * 2 + quarter) * 8
                part = table[at : at + 8, :]
                pieces += [jnp.where(lane_c == c + row_c, part, 0.0) for c in range(0, sz.cpl, each)]
            ya[g * 128 : (g + 1) * 128, :] = jnp.concatenate(pieces, axis=0).astype(bf16)
        copies.send(ya, ya_hbm)
    for jj in range(sz.half_j):
        gets[jj].wait()
        for kk in range(sz.blk_k):
            for h in range(sz.groups):
                lanes = [
                    w[jj, kk, lg * 8 : (lg + 1) * 8, h * sz.cpl : (h + 1) * sz.cpl, :].reshape(128, sz.chans)
                    for lg in range(sz.lgs)
                ]
                out[jj, kk, h * 128 : (h + 1) * 128, :] = jnp.concatenate(lanes, axis=1)
        copies.send(out.at[jj], out_hbm.at[jj])
    copies.finish()


def pack_call(sz, after, weight, start, by=None):
    half = sz.half_j
    packed = (half, sz.blk_k, sz.groups * 128, sz.lgs * sz.chans)
    lines = (sz.lines * 128, sz.modes_y * sz.cpl)
    outs = [(shape(packed), True)]
    args = (after, weight)
    scratch = [pltpu.VMEM((half,) + weight.shape[2:], bf16), pltpu.VMEM(packed, bf16)]
    tables = by is not None
    if tables:
        outs.append((shape(lines), True))
        args += (by,)
        scratch += [pltpu.VMEM(by.shape, bf16), pltpu.VMEM(lines, bf16)]
    result = run(
        "pack",
        lambda *refs: pack_kernel(sz, start, tables, *refs),
        outs,
        [hbm] * len(args),
        args,
        scratch,
        2 * half + 2 * tables,
        0,
    )
    return result if tables else result[0]


def line_analysis(sz, r_ref, ya_ref, get_ya, fine=True):
    jk = sz.jk

    def total(sec, gy, start, step):
        result = None
        for gx in range(start, sz.n_gx, step):
            at = ((sec * sz.n_gx + gx) * sz.n_gy + gy) * jk
            part = r_ref[at : at + jk, :].astype(f32)
            result = part if result is None else result + part
        return result

    halves = [[], []]
    low = iota((jk, 128), 1) < 64
    for sec in range(2):
        for gy in range(sz.n_gy):
            if fine:
                a, b = total(sec, gy, 0, 2), total(sec, gy, 1, 2)
                halves[0].append(jnp.where(low, a, pltpu.roll(b, 64, 1)).astype(bf16))
                halves[1].append(jnp.where(low, pltpu.roll(a, 64, 1), b).astype(bf16))
            else:
                line = total(sec, gy, 0, 1).astype(bf16)
                for h in range(sz.groups):
                    halves[h].append(line[:, h * 128 : (h + 1) * 128])
    rows = jnp.concatenate([jnp.concatenate(half, axis=1) for half in halves], axis=0)
    if get_ya is not None:
        get_ya.wait()
    return nn(rows, ya_ref[...]).astype(bf16)


def diagonal(sz, count):
    shape = (count, sz.groups * 128)
    return iota(shape, 0) % 8 == (iota(shape, 1) % 128) // sz.cpl


def row_spread(sz):
    shape = (sz.jk * 8, sz.jk)
    return (iota(shape, 0) // 8 == iota(shape, 1)).astype(bf16)


def row_gather(sz):
    shape = (sz.jk, sz.jk * 8)
    return (iota(shape, 1) // 8 == iota(shape, 0)).astype(bf16)


def chan_lanes(sz):
    shape = (sz.groups * 128, sz.chans)
    lane = iota(shape, 0)
    return ((lane // 128) * sz.cpl + lane % sz.cpl == iota(shape, 1)).astype(bf16)


def to_blocks(sz, rows, lg):
    jk = sz.jk
    wide = jnp.concatenate(
        [rows[h * jk : (h + 1) * jk, lg * 128 : (lg + 1) * 128] for h in range(sz.groups)], axis=1
    )
    return jnp.where(diagonal(sz, jk * 8), nn(row_spread(sz), wide), 0.0)


def from_blocks(sz, blocks):
    jk = sz.jk
    pieces = []
    for block in blocks:
        kept = jnp.where(diagonal(sz, jk * 8), block, 0.0).astype(bf16)
        pieces.append(nn(row_gather(sz), kept).astype(bf16))
    return jnp.concatenate(
        [
            jnp.concatenate([piece[:, h * 128 : (h + 1) * 128] for piece in pieces], axis=1)
            for h in range(sz.groups)
        ],
        axis=0,
    )


def send_lines(sz, rows, ya_ref, out_ref):
    jk = sz.jk
    lines = nt(rows, ya_ref[...])
    low = iota((jk, 128), 1) < 64
    for sec in range(2):
        for gy in range(sz.n_gy):
            line = sec * sz.n_gy + gy
            a, b = [lines[h * jk : (h + 1) * jk, line * 128 : (line + 1) * 128] for h in range(2)]
            quarters = [
                jnp.where(low, a, pltpu.roll(b, 64, 1)).astype(bf16),
                jnp.where(low, pltpu.roll(a, 64, 1), b).astype(bf16),
            ]
            for gx in range(sz.n_gx):
                at = ((sec * sz.n_gx + gx) * sz.n_gy + gy) * jk
                out_ref[at : at + jk, :] = quarters[gx % 2]


def lane_group(sz):
    dims = (sz.lgs * sz.jk * 8, sz.lgs * sz.chans)
    return iota(dims, 0) // (sz.jk * 8) == iota(dims, 1) // sz.chans


def mix_kernel(sz, layer, turn, s_ref, r, ya_in, *rest):
    if layer == 0:
        low_hbm, high_hbm, *rest = rest
        spec_hbm, out, ya, w, spec_b, blk, mix, sems = rest[3:]
    else:
        ya = ya_in
        w, spec_hbm, out, spec_b, blk, mix, sems = rest
    copies = Copies(sems)
    get_ya = copies.start(ya_in, ya) if layer == 0 else None
    if layer == 0:
        get_w = copies.choose(s_ref[0] == 0, [(low_hbm.at[jj], high_hbm.at[jj], w.at[jj]) for jj in range(sz.half_j)])
    spec = line_analysis(sz, r, ya, get_ya, layer > 0)
    spec_b[...] = spec
    copies.send(spec_b, spec_hbm)
    count = sz.jk * 8
    width = sz.lgs * sz.chans
    rep = jnp.concatenate([chan_lanes(sz)] * sz.lgs, axis=1)
    blocks = [to_blocks(sz, spec, lg) for lg in range(sz.lgs)]
    if turn:
        flat = nn(jnp.concatenate(blocks, axis=0).astype(bf16), rep)
        mix[:, :width] = jnp.where(lane_group(sz), flat, 0.0)
        left_ref, right_ref, left_width = mix, blk, width
    else:
        for lg in range(sz.lgs):
            blk[lg * count : (lg + 1) * count, :] = blocks[lg]
        left_ref, right_ref, left_width = blk, mix, blk.shape[1]
    for jk in range(sz.jk):
        jj, kk = jk // sz.blk_k, jk % sz.blk_k
        if kk == 0 and layer == 0:
            get_w[jj].wait()
        at = [slice((lg * sz.jk + jk) * 8, (lg * sz.jk + jk + 1) * 8) for lg in range(sz.lgs)]
        left = jnp.concatenate([left_ref[a, :left_width] for a in at], axis=0).astype(bf16)
        part = nt(left, w[jj, kk]) if turn else nn(left, w[jj, kk])
        for lg, a in enumerate(at):
            right_ref[a, : part.shape[1]] = part[lg * 8 : (lg + 1) * 8]
    if not turn:
        kept_mix = jnp.where(lane_group(sz), mix[:, :width], 0.0).astype(bf16)
        full = nt(kept_mix, rep)
    else:
        full = blk[...]
    blocks = [full[lg * count : (lg + 1) * count] for lg in range(sz.lgs)]
    send_lines(sz, from_blocks(sz, blocks), ya, out)
    copies.finish()


def mix_call(sz, layer, turn, s, r, ya, weights, after=()):
    count = sz.jk * 8 * sz.lgs
    spec = (sz.groups * sz.jk, sz.modes_y * sz.cpl)
    line = (sz.modes, sz.thin)
    outs = [(shape(spec), True), (kept(line), False)]
    scratch = [pltpu.VMEM(spec, bf16)] + [pltpu.VMEM((count, sz.groups * 128), f32)] * 2
    if layer == 0:
        outs.append((kept(ya.shape), False))
        scratch = [pltpu.VMEM(weights[0].shape, bf16)] + scratch
        specs = [smem, vmem] + [hbm] * (3 + len(after))
    else:
        ya = near(ya)
        weights = [near(weights)]
        specs = [smem] + [vmem] * 3
    return run(
        "mix",
        lambda *refs: mix_kernel(sz, layer, turn, *refs),
        outs,
        specs,
        (s, r, ya, *weights, *after),
        scratch,
        sz.half_j + 2,
    )


def gate_kernel(sz, in_ref, after_hbm, out_ref):
    out_ref[...] = in_ref[...]


def gate_call(sz, value, after):
    (out,) = run(
        "gate",
        lambda *refs: gate_kernel(sz, *refs),
        [(kept(value.shape), False)],
        [vmem, hbm],
        (near(value), after),
        micros=0,
    )
    return out


def spec_kernel(sz, s_ref, r, ya, sv0_hbm, sv1_hbm, su1_hbm, mine, sends, before, sems):
    copies = Copies(sems)
    gets = [copies.start(src, before.at[at]) for at, src in enumerate((sv0_hbm, sv1_hbm, su1_hbm))]
    first = s_ref[0] == 0
    spec = line_analysis(sz, r, ya, None)
    for get in gets:
        get.wait()
    sv0, sv1, su1 = [before[at] for at in range(3)]
    sends[0] = jnp.where(first, sv1, sv0)
    sends[1] = jnp.where(first, su1, spec)
    mine[0] = jnp.where(first, sv0, sv1)
    mine[1] = jnp.where(first, spec, su1)


def spec_call(sz, s, r, sv0, sv1, su1, ya):
    spec = (sz.groups * sz.jk, sz.modes_y * sz.cpl)
    return run(
        "spec",
        lambda *refs: spec_kernel(sz, *refs),
        [(kept((2,) + spec), False), (kept((2,) + spec), False)],
        [smem, vmem, vmem, hbm, hbm, hbm],
        (s, r, near(ya), sv0, sv1, su1),
        [pltpu.VMEM((3,) + spec, bf16)],
        3,
    )


def turned_modes(sz, u_ref, layer):
    left = jnp.transpose(u_ref[...])
    half = sz.modes // 2
    if layer == 1:
        left = jnp.concatenate([left[:, half:], left[:, :half]], axis=1)
    return left


CHUNK = 1024


def cuts(sz):
    return [slice(at, at + CHUNK) for at in range(0, sz.wide, CHUNK)]


def small_parts(sz, s_ref, own_ref, other_ref, layer):
    chosen = jnp.where(s_ref[0] == layer, own_ref[...].astype(f32), other_ref[...].astype(f32)).astype(bf16)
    return chosen[: sz.chans], chosen[sz.chans :]


def field_copies(sz, copies, mine_hbm, other_hbm, field):
    return [
        copies.start(mine_hbm, field.at[:, : sz.cells]),
        copies.start(other_hbm, field.at[:, sz.cells :]),
    ]


def thirds(value):
    high = value.astype(bf16)
    rest = value - high.astype(f32)
    middle = rest.astype(bf16)
    return [high, middle, (rest - middle.astype(f32)).astype(bf16)]


def point_sums(sz, v, d):
    pairs = jnp.where(same_y(sz), nt(v, d), 0.0)
    bias = nt(jnp.ones((8, sz.wide), bf16), d)
    dims = (sz.chans, 3 * sz.thin)
    fold = (iota(dims, 1) % sz.thin // sz.fine == iota(dims, 0)).astype(bf16)
    pairs = nn(fold, jnp.concatenate(thirds(pairs), axis=0))
    part = sz.chans // 4
    rows = []
    for t in range(4):
        below = bias if t == 0 else jnp.zeros_like(bias)
        both = jnp.concatenate([pairs[t * part : (t + 1) * part], below], axis=0)
        rows.append(jnp.concatenate(thirds(both), axis=0))
    dims = (4 * sz.thin, 128)
    row = iota(dims, 0)
    place = (row // sz.thin * sz.chans + row % sz.thin // sz.fine == iota(dims, 1)).astype(bf16)
    total = nn(jnp.concatenate(rows, axis=1), place)
    count = part + 8
    return total[:count] + total[count : 2 * count] + total[2 * count :]


def forward_kernel(
    sz, s_ref, own_ref, other_ref, u, mine_hbm, next_hbm, bb_hbm, low_hbm, high_hbm, v, slope, bb, out, w, field, sems
):
    copies = Copies(sems)
    get_bb, get_v = [], []
    for at, cut in enumerate(cuts(sz)):
        get_bb.append(copies.start(bb_hbm.at[:, cut], bb.at[:, cut]))
        if at == 0:
            get_v = field_copies(sz, copies, mine_hbm, next_hbm, field)
    (get_w,) = copies.choose(s_ref[0] == 1, [(low_hbm, high_hbm, w)])
    weight, bias = small_parts(sz, s_ref, own_ref, other_ref, 0)
    matrix = point_matrix(sz, weight, True)
    column = nt(spread(sz), bias)[:, :1]
    left = turned_modes(sz, u, 0)
    for at, cut in enumerate(cuts(sz)):
        get_bb[at].wait()
        if cut.start % sz.cells == 0:
            get_v[cut.start // sz.cells].wait()
        pre = nn(left, bb[:, cut]) + nn(matrix, field[:, cut]) + column
        value, rate = activate(pre)
        v[:, cut] = value.astype(bf16)
        slope[:, cut] = rate
    send_analysis(sz, bb, v[...], out, 1)
    get_w.wait()


def forward_call(sz, s, mine, other, u, bb, own_small, other_small, low, high):
    field, line = (sz.thin, sz.wide), (sz.modes, sz.thin)
    return run(
        "forward",
        lambda *refs: forward_kernel(sz, *refs),
        [
            (kept(field), False),
            (kept(field, f32), False),
            (kept((sz.modes, sz.wide)), False),
            (kept(line), False),
            (kept(low.shape), False),
        ],
        [smem, vmem, vmem, vmem, hbm, hbm, hbm, hbm, hbm],
        (s, own_small, other_small, u, mine, other, bb, low, high),
        [pltpu.VMEM(field, bf16)],
        3 + len(cuts(sz)),
    )


def turn_kernel(sz, s_ref, own_ref, other_ref, u, v, bb, mine_hbm, next_hbm, d, sums, out, grad, sems):
    copies = Copies(sems)
    get_g = field_copies(sz, copies, mine_hbm, next_hbm, grad)
    weight, bias = small_parts(sz, s_ref, own_ref, other_ref, 1)
    matrix = point_matrix(sz, weight, True)
    column = nt(spread(sz), bias)[:, :1]
    left = turned_modes(sz, u, 1)
    for at, cut in enumerate(cuts(sz)):
        pre = nn(left, bb[:, cut]) + nn(matrix, v[:, cut]) + column
        _, rate = activate(pre)
        if at == 0:
            for get in get_g:
                get.wait()
        d[:, cut] = (grad[:, cut].astype(f32) * rate).astype(bf16)
    send_analysis(sz, bb, d[...], out, 1)
    sums[...] = point_sums(sz, v[...], d[...])


def turn_call(sz, s, mine, other, v, u, bb, own_small, other_small):
    field, line = (sz.thin, sz.wide), (sz.modes, sz.thin)
    return run(
        "turn",
        lambda *refs: turn_kernel(sz, *refs),
        [(kept(field), False), (kept((sz.chans // 4 + 8, 128), f32), False), (kept(line), False)],
        [smem, vmem, vmem, vmem, vmem, vmem, hbm, hbm],
        (s, own_small, other_small, u, near(v), near(bb), mine, other),
        [pltpu.VMEM(field, bf16)],
        2,
    )


def pieces(sz, value):
    part = sz.chans // 4
    high = value.astype(bf16).astype(f32)
    low = value - high
    bias = jnp.where(iota((8, 128), 0) < 4, high[part:], low[part:])
    return jnp.concatenate([high[:part], low[:part], bias], axis=0).astype(bf16)


def back_kernel(
    sz, s_ref, own_ref, other_ref, u, d, slope, bb, sums, mine_hbm, next_hbm, parts, out, new, field, sems
):
    copies = Copies(sems)
    get_v = field_copies(sz, copies, mine_hbm, next_hbm, field)
    weight, _ = small_parts(sz, s_ref, own_ref, other_ref, 1)
    matrix = point_matrix(sz, weight, False)
    left = turned_modes(sz, u, 1)
    for cut in cuts(sz):
        grad = (nn(left, bb[:, cut]) + nn(matrix, d[:, cut])).astype(bf16).astype(f32)
        new[:, cut] = (grad * slope[:, cut]).astype(bf16)
    for get in get_v:
        get.wait()
    send_analysis(sz, bb, new[...], out, 0)
    first = point_sums(sz, field[...], new[...])
    half = sz.places // 2
    for layer, value in enumerate((first, sums[...])):
        block = pieces(sz, value)
        for place in range(half):
            parts[layer * half + place] = block


def back_call(sz, s, mine, other, d, slope, u, bb, sums, own_small, other_small):
    parts, line, field = (sz.places, sz.chans // 2 + 8, 128), (sz.modes, sz.thin), (sz.thin, sz.wide)
    return run(
        "back",
        lambda *refs: back_kernel(sz, *refs),
        [(kept(parts), False), (kept(line), False)],
        [smem] + [vmem] * 7 + [hbm, hbm],
        (s, own_small, other_small, u, near(d), near(slope), near(bb), near(sums), mine, other),
        [pltpu.VMEM(field, bf16), pltpu.VMEM(field, bf16)],
        2,
    )


def finish_kernel(sz, parts_ref, after_ref, point_ref, bias_ref):
    total = jnp.sum(parts_ref[...].astype(f32), axis=0)
    part = sz.chans // 4
    bias_ref[...] = (total[2 * part : 2 * part + 1] + total[2 * part + 4 : 2 * part + 5])[:, : sz.chans]
    total = total[:part] + total[part : 2 * part]
    for t in range(4):
        point_ref[0, t * part : (t + 1) * part, :] = total[:part, t * sz.chans : (t + 1) * sz.chans]


def finish_call(sz, parts, after):
    return pl.pallas_call(
        lambda *refs: finish_kernel(sz, *refs),
        out_shape=(shape((1, sz.chans, sz.chans), f32), shape((1, sz.chans), f32)),
        in_specs=[vmem, hbm],
        out_specs=(vmem, vmem),
        compiler_params=pltpu.CompilerParams(vmem_limit_bytes=limit),
        name="finish",
    )(parts, far(after))


def outer_kernel(sz, mine_ref, theirs_ref, out_ref, left_ref, right_ref):
    jk, groups, kk_count = sz.jk, sz.groups, sz.blk_k
    step = pl.program_id(0)

    def prepare(side, sv, su):
        sv = sv.astype(f32)
        for jj in range(sz.half_j):
            place = side * sz.half_j + jj
            rows = jnp.concatenate(
                [sv[h * jk + jj * kk_count : h * jk + (jj + 1) * kk_count] for h in range(groups)], axis=0
            )
            left_ref[place] = jnp.transpose(rows).astype(bf16)
        for lg in range(sz.lgs):
            flat = nn(to_blocks(sz, su, lg).astype(bf16), chan_lanes(sz))
            for at in range(jk):
                place = side * sz.half_j + at // kk_count
                right_ref[place, at % kk_count, lg * 8 : (lg + 1) * 8, :] = flat[at * 8 : (at + 1) * 8]

    @pl.when(step == 0)
    def _():
        prepare(0, mine_ref[0], mine_ref[1])

    @pl.when(step == 1)
    def _():
        prepare(1, theirs_ref[0], theirs_ref[1])

    dims = (groups * kk_count, groups * kk_count * 128)
    spread_lanes = (iota(dims, 0) == iota(dims, 1) // 128).astype(bf16)
    each = out_ref.shape[1]
    for sub in range(each):
        columns = nn(left_ref[step * each + sub], spread_lanes)
        for kk in range(kk_count):
            for ll in range(sz.modes_y):
                row = right_ref[step * each + sub, kk, ll : ll + 1, :]
                for h in range(groups):
                    at = (h * kk_count + kk) * 128
                    part = columns[ll * sz.cpl : (ll + 1) * sz.cpl, at : at + sz.chans] * row
                    out_ref[0, sub, kk, ll, h * sz.cpl : (h + 1) * sz.cpl, :] = part


def outer_call(sz, mine, theirs):
    each = max(1, sz.half_j // 2)
    wide = sz.modes_y * sz.cpl
    return pl.pallas_call(
        lambda *refs: outer_kernel(sz, *refs),
        grid=(sz.blk_j // each,),
        out_shape=pltpu.HBM((1, sz.blk_j, sz.blk_k, sz.modes_y, sz.chans, sz.chans), f32),
        in_specs=[vmem] * 2,
        out_specs=pl.BlockSpec((1, each, sz.blk_k, sz.modes_y, sz.chans, sz.chans), lambda i: (0, i, 0, 0, 0, 0)),
        scratch_shapes=[
            pltpu.VMEM((sz.blk_j, wide, sz.groups * sz.blk_k), bf16),
            pltpu.VMEM((sz.blk_j, sz.blk_k, sz.modes_y, sz.chans), f32),
        ],
        compiler_params=pltpu.CompilerParams(vmem_limit_bytes=limit),
        cost_estimate=pl.CostEstimate(flops=0, transcendentals=0, bytes_accessed=20000000),
        name="outer",
    )(near(mine), theirs)


def exchange(block):
    return lax.all_to_all(block, AXES, split_axis=0, concat_axis=0, tiled=True)


def swap(block):
    return lax.ppermute(block, "section", [(0, 1), (1, 0)])


def swap_near(sz, block):
    return lax.ppermute(block, "gx", [(i, i ^ 1) for i in range(sz.n_gx)])


def local(ends, spectral_weight, point_weight, point_bias):
    sz = Sizes(ends, spectral_weight)
    section = lax.axis_index("section")
    first = section == 0
    s = section.astype(jnp.int32).reshape(1)

    def half(field, which):
        part = lax.dynamic_slice_in_dim(field, which * sz.len_y, sz.len_y, axis=2)
        return jnp.swapaxes(part, 1, 2).reshape(sz.rows, sz.cells)

    bx, bz, by = [jnp.asarray(t.astype(ml_dtypes.bfloat16)) for t in mode_tables(sz)]
    send = half(ends[0], 1 - section)
    send, later = lax.optimization_barrier((send, ends[0]))
    recv = swap(send)
    keep = half(later, section)
    gx = lax.axis_index("gx").astype(jnp.int32)
    gx = jnp.stack([gx, gx + 1 - 2 * (gx % 2)])
    bb = tables_call(sz, gx, bx, bz)
    own_small = jnp.concatenate([point_weight[0], jnp.broadcast_to(point_bias, (16, sz.chans))], axis=0)
    other_small = swap(own_small)
    mine_v, send_v, raw_g, out = first_call(sz, s, gx, keep, recv, bb)
    next_v = swap_near(sz, send_v)
    r = exchange(out)
    high = swap(pack_call(sz, mine_v, spectral_weight, sz.half_j))
    mine_g, send_g = split_call(sz, gx, raw_g, mine_v)
    next_g = swap_near(sz, send_g)
    low, ya = pack_call(sz, mine_v, spectral_weight, 0, by)
    bb = wide_call(sz, gx, bx, bz, mine_v)
    sv0, out, ya = mix_call(sz, 0, False, s, r, ya, (low, high), (other_small, bb, next_v))
    v1, slope0, bb, out, w1 = forward_call(sz, s, mine_v, next_v, exchange(out), bb, own_small, other_small, low, high)
    sv1, out = mix_call(sz, 1, False, s, exchange(out), ya, w1)
    out = gate_call(sz, out, next_g)
    d1, sums, out = turn_call(sz, s, mine_g, next_g, v1, exchange(out), bb, own_small, other_small)
    su1, out = mix_call(sz, 1, True, s, exchange(out), ya, w1)
    parts, out = back_call(sz, s, mine_v, next_v, d1, slope0, exchange(out), bb, sums, own_small, other_small)
    r, parts = lax.optimization_barrier((exchange(out), parts))
    mine, send = spec_call(sz, s, r, sv0, sv1, su1, ya)
    theirs = swap(send)
    parts = lax.all_to_all(parts, AXES, split_axis=0, concat_axis=0, tiled=True)
    spectral_grad = outer_call(sz, mine, theirs)
    point_grad, bias_grad = finish_call(sz, parts, spectral_grad)
    return (spectral_grad, point_grad, bias_grad)


def solution(mesh):
    return jax.shard_map(
        local,
        mesh=mesh,
        in_specs=(
            P("section", None, "gx", "gy", None),
            P("section", "gy", "gx", None, None, None),
            P("section", None, None),
            P("section", None),
        ),
        out_specs=(
            P("section", "gy", "gx", None, None, None),
            P("section", None, None),
            P("section", None),
        ),
        check_vma=False,
    )
```

```python
import math

import jax
import jax.numpy as jnp
import ml_dtypes
import numpy as np
from jax import lax
from jax.experimental import pallas as pl
from jax.experimental.pallas import tpu as pltpu
from jax.sharding import PartitionSpec as P

gelu_coef = 0.7978845608028654
f32 = jnp.float32
bf16 = jnp.bfloat16
AXES = ("section", "gx", "gy")


def table(length, count):
    half = count // 2
    modes = np.arange(count)
    is_cos = modes < half
    wave = np.where(is_cos, modes, modes - half + 1)
    phase = wave[:, None] * np.arange(length)[None, :] % length
    angle = phase.astype(np.float32) * np.float32(2.0 * math.pi / length)
    values = np.where(is_cos[:, None], np.cos(angle), np.sin(angle)).astype(np.float32)
    scale = np.where(is_cos & (wave == 0), math.sqrt(1.0 / length), math.sqrt(2.0 / length))
    return (values * scale.astype(np.float32)[:, None]).astype(ml_dtypes.bfloat16).astype(np.float32)


def nn(a, b):
    return lax.dot_general(a, b, (((1,), (0,)), ((), ())), preferred_element_type=f32)


def nt(a, b):
    return lax.dot_general(a, b, (((1,), (1,)), ((), ())), preferred_element_type=f32)


def tn(a, b):
    return lax.dot_general(a, b, (((0,), (0,)), ((), ())), preferred_element_type=f32)


def iota(shape, dim):
    return lax.broadcasted_iota(jnp.int32, shape, dim)


limit = 24 * 1024 * 1024
smem = pl.BlockSpec(memory_space=pltpu.SMEM)
hbm = pl.BlockSpec(memory_space=pltpu.HBM)
vmem = pl.BlockSpec(memory_space=pltpu.VMEM)


def shape(dims, dtype=bf16):
    return jax.ShapeDtypeStruct(dims, dtype)


def kept(dims, dtype=bf16):
    return pltpu.VMEM(dims, dtype)


def near(value):
    return pltpu.with_memory_space_constraint(value, pltpu.VMEM)


def far(value):
    return pltpu.with_memory_space_constraint(value, pltpu.HBM)


def run(name, kernel, outs, specs, args, scratch=(), copies=0, micros=1):
    return pl.pallas_call(
        kernel,
        out_shape=tuple(pltpu.HBM(o.shape, o.dtype) if away else o for o, away in outs),
        in_specs=list(specs),
        out_specs=tuple(hbm if away else vmem for _, away in outs),
        scratch_shapes=list(scratch) + ([pltpu.SemaphoreType.DMA((copies,))] if copies else []),
        compiler_params=pltpu.CompilerParams(vmem_limit_bytes=limit),
        cost_estimate=pl.CostEstimate(flops=0, transcendentals=0, bytes_accessed=micros * 3000000),
        name=name,
    )(*[far(a) if spec is hbm else a for a, spec in zip(args, specs)])


class Copies:
    def __init__(self, sems):
        self.sems = sems
        self.used = 0
        self.open = []

    def make(self, src, dst):
        copy = pltpu.make_async_copy(src, dst, self.sems.at[self.used])
        self.used += 1
        return copy

    def start(self, src, dst):
        copy = self.make(src, dst)
        copy.start()
        return copy

    def choose(self, pick, triples):
        firsts, others = [], []
        for src, other, dst in triples:
            firsts.append(pltpu.make_async_copy(src, dst, self.sems.at[self.used]))
            others.append(self.make(other, dst))

        @pl.when(pick)
        def _():
            for copy in firsts:
                copy.start()

        @pl.when(jnp.logical_not(pick))
        def _():
            for copy in others:
                copy.start()

        return others

    def send(self, src, dst):
        self.open.append(self.start(src, dst))

    def finish(self):
        for copy in self.open:
            copy.wait()


class Sizes:
    def __init__(self, ends, weight):
        self.n_gx = lax.axis_size("gx")
        self.n_gy = lax.axis_size("gy")
        _, self.chans, self.len_x, full, self.depth = ends.shape
        self.len_y = full // 2
        _, self.blk_j, self.blk_k, self.modes_y, _, _ = weight.shape
        self.half_j = self.blk_j // 2
        self.jk = self.half_j * self.blk_k
        self.places = 2 * self.n_gx * self.n_gy
        self.modes = self.places * self.jk
        self.rows = self.chans * self.len_y
        self.cells = self.len_x * self.depth
        self.lines = 2 * self.n_gy
        self.cpl = 128 // self.len_y
        self.groups = self.rows // 128
        self.lgs = self.modes_y // 8
        self.full_x = self.len_x * self.n_gx
        self.fine = self.len_y // 2
        self.thin = self.chans * self.fine
        self.wide = 2 * self.cells
        self.full_y = full * self.n_gy


def mode_tables(sz):
    bx = table(sz.full_x, sz.blk_j * sz.n_gy)
    bz = table(sz.depth, sz.blk_k * sz.n_gx)
    by = table(sz.full_y, sz.modes_y)
    sec, gx, gy, jj, kk = np.meshgrid(
        np.arange(2), np.arange(sz.n_gx), np.arange(sz.n_gy), np.arange(sz.half_j), np.arange(sz.blk_k), indexing="ij"
    )
    row_j = (gy * sz.blk_j + sec * sz.half_j + jj).reshape(-1)
    row_k = (gx * sz.blk_k + kk).reshape(-1)
    sec, gy, yy = np.meshgrid(np.arange(2), np.arange(sz.n_gy), np.arange(sz.len_y), indexing="ij")
    row_y = (gy * 2 * sz.len_y + sec * sz.len_y + yy).reshape(-1)
    bx = np.moveaxis(bx[row_j].reshape(sz.modes, sz.n_gx, sz.len_x), 1, 0)
    lines = by[:, row_y].T.reshape(sz.lines, 2, 1, sz.fine, sz.modes_y)
    lines = np.broadcast_to(lines, (sz.lines, 2, 8 // sz.fine, sz.fine, sz.modes_y)).reshape(-1, sz.modes_y)
    return bx, bz[row_k], np.repeat(lines, sz.cpl, axis=1)


def activate(pre):
    square = pre * pre
    tanh_val = jnp.tanh(pre * (gelu_coef + (gelu_coef * 0.044715) * square))
    half = 0.5 + 0.5 * tanh_val
    value = pre * half
    slope = half + value * (1.0 - tanh_val) * (gelu_coef + (3.0 * gelu_coef * 0.044715) * square)
    return value, slope


def spread(sz):
    shape = (sz.thin, sz.chans)
    return (iota(shape, 0) // sz.fine == iota(shape, 1)).astype(bf16)


def same_y(sz):
    shape = (sz.thin, sz.thin)
    return iota(shape, 0) % sz.fine == iota(shape, 1) % sz.fine


def point_matrix(sz, weight, forward):
    one = spread(sz)
    part = nt(one, weight) if forward else nn(one, weight)
    full = nt(part.astype(bf16), one)
    return jnp.where(same_y(sz), full, 0.0).astype(bf16)


def swapped(rows, half):
    return jnp.concatenate([rows[half:], rows[:half]], axis=0)


def send_analysis(sz, bb_ref, field, out_ref, layer):
    out = nt(bb_ref[...], field).astype(bf16)
    out_ref[...] = swapped(out, sz.modes // 2) if layer == 1 else out


def fill_table(sz, bx, bz, bb):
    depth = sz.depth
    across, along = bx[...].astype(f32), bz[...].astype(f32)
    for x in range(sz.len_x):
        bb[:, x * depth : (x + 1) * depth] = (across[:, x : x + 1] * along).astype(bf16)


def pack_rows(sz, copies, gets, w, out, out_hbm):
    for jj in range(sz.half_j):
        gets[jj].wait()
        for kk in range(sz.blk_k):
            for h in range(sz.groups):
                lanes = [
                    w[jj, kk, lg * 8 : (lg + 1) * 8, h * sz.cpl : (h + 1) * sz.cpl, :].reshape(128, sz.chans)
                    for lg in range(sz.lgs)
                ]
                out[jj, kk, h * 128 : (h + 1) * 128, :] = jnp.concatenate(lanes, axis=1)
        copies.send(out.at[jj], out_hbm.at[jj])


def tables_kernel(sz, gx_ref, bx_hbm, bz_hbm, bb, bx, bz, sems):
    copies = Copies(sems)
    get_bx = copies.start(bx_hbm.at[gx_ref[0]], bx)
    get_bz = copies.start(bz_hbm, bz)
    get_bx.wait()
    get_bz.wait()
    fill_table(sz, bx, bz, bb)


def tables_call(sz, gx, bx, bz):
    (bb,) = run(
        "tables",
        lambda *refs: tables_kernel(sz, *refs),
        [(kept((sz.modes, sz.cells)), False)],
        [smem, hbm, hbm],
        (gx, bx, bz),
        [pltpu.VMEM(bx.shape[1:], bf16), pltpu.VMEM(bz.shape, bf16)],
        2,
    )
    return bb


def reorder(sz):
    dims = (sz.rows, sz.rows)
    row = iota(dims, 0)
    group, quarter = row // 128, row % 128 // 64
    chan, y = group * sz.cpl + row % 64 // sz.fine, quarter * sz.fine + row % sz.fine
    return (chan * sz.len_y + y == iota(dims, 1)).astype(bf16)


def send_quarters(sz, gx_ref, field, mine_hbm, send_hbm, copies):
    quarter = gx_ref[0] % 2
    for h in range(sz.groups):
        to = slice(h * 64, (h + 1) * 64)
        copies.send(field.at[pl.ds(h * 128 + quarter * 64, 64)], mine_hbm.at[to])
        copies.send(field.at[pl.ds(h * 128 + (1 - quarter) * 64, 64)], send_hbm.at[to])


def wide_kernel(sz, gx_ref, bx_hbm, bz_hbm, after_hbm, bb_hbm, bx, bz, bb, sems):
    copies = Copies(sems)
    gets = [copies.start(bx_hbm.at[gx_ref[side]], bx.at[side]) for side in range(2)]
    gets.append(copies.start(bz_hbm, bz))
    for get in gets:
        get.wait()
    for side in range(2):
        at = slice(side * sz.cells, (side + 1) * sz.cells)
        fill_table(sz, bx.at[side], bz, bb.at[:, at])
        copies.send(bb.at[:, at], bb_hbm.at[:, at])
    copies.finish()


def wide_call(sz, gx, bx, bz, after):
    (bb,) = run(
        "wide",
        lambda *refs: wide_kernel(sz, *refs),
        [(shape((sz.modes, sz.wide)), True)],
        [smem, hbm, hbm, hbm],
        (gx, bx, bz, after),
        [pltpu.VMEM((2,) + bx.shape[1:], bf16), pltpu.VMEM(bz.shape, bf16), pltpu.VMEM((sz.modes, sz.wide), bf16)],
        5,
        0,
    )
    return bb


def first_kernel(
    sz, s_ref, gx_ref, keep, recv, bb, w_hbm, mine_hbm, send_hbm, raw_hbm, out_hbm, high_hbm, v, out, w, high, sems
):
    copies = Copies(sems)
    first = s_ref[0] == 0
    gets = [copies.start(w_hbm.at[0, sz.half_j + jj], w.at[jj]) for jj in range(sz.half_j)]
    v[...] = nn(reorder(sz), jnp.where(first, keep[...], recv[...])).astype(bf16)
    send_quarters(sz, gx_ref, v, mine_hbm, send_hbm, copies)
    send_analysis(sz, bb, v[...], out, 0)
    copies.send(out, out_hbm)
    (put_raw,) = copies.choose(first, [(recv, keep, raw_hbm)])
    pack_rows(sz, copies, gets, w, high, high_hbm)
    put_raw.wait()
    copies.finish()


def first_call(sz, s, gx, keep, recv, bb, weight):
    line, field, part = (sz.modes, sz.rows), (sz.rows, sz.cells), (sz.thin, sz.cells)
    packed = (sz.half_j, sz.blk_k, sz.groups * 128, sz.lgs * sz.chans)
    return run(
        "first",
        lambda *refs: first_kernel(sz, *refs),
        [(shape(part), True), (shape(part), True), (shape(field), True), (shape(line), True), (shape(packed), True)],
        [smem, smem, vmem, vmem, vmem, hbm],
        (s, gx, keep, recv, near(bb), weight),
        [
            pltpu.VMEM(field, bf16),
            pltpu.VMEM(line, bf16),
            pltpu.VMEM((sz.half_j,) + weight.shape[2:], bf16),
            pltpu.VMEM(packed, bf16),
        ],
        2 + 2 * sz.groups + 2 * sz.half_j,
    )


def split_kernel(sz, gx_ref, raw_hbm, after_hbm, mine_hbm, send_hbm, raw, field, sems):
    copies = Copies(sems)
    copies.start(raw_hbm, raw).wait()
    field[...] = nn(reorder(sz), raw[...]).astype(bf16)
    send_quarters(sz, gx_ref, field, mine_hbm, send_hbm, copies)
    copies.finish()


def split_call(sz, gx, raw, after):
    field, part = (sz.rows, sz.cells), (sz.thin, sz.cells)
    return run(
        "split",
        lambda *refs: split_kernel(sz, *refs),
        [(shape(part), True), (shape(part), True)],
        [smem, hbm, hbm],
        (gx, raw, after),
        [pltpu.VMEM(field, bf16), pltpu.VMEM(field, bf16)],
        1 + 2 * sz.groups,
        0,
    )


def pack_kernel(sz, start, tables, *refs):
    if tables:
        after_hbm, w_hbm, by_hbm, out_hbm, ya_hbm, w, out, by, ya, sems = refs
    else:
        after_hbm, w_hbm, out_hbm, w, out, sems = refs
    copies = Copies(sems)
    if tables:
        get_by = copies.start(by_hbm, by)
    gets = [copies.start(w_hbm.at[0, start + jj], w.at[jj]) for jj in range(sz.half_j)]
    if tables:
        get_by.wait()
        table = by[...].astype(f32)
        wide = sz.modes_y * sz.cpl
        lane_c = iota((8, wide), 1) % sz.cpl
        each = 8 // sz.fine
        row_c = iota((8, wide), 0) // sz.fine
        for g in range(sz.lines):
            pieces = []
            for quarter in range(2):
                at = (g * 2 + quarter) * 8
                part = table[at : at + 8, :]
                pieces += [jnp.where(lane_c == c + row_c, part, 0.0) for c in range(0, sz.cpl, each)]
            ya[g * 128 : (g + 1) * 128, :] = jnp.concatenate(pieces, axis=0).astype(bf16)
        copies.send(ya, ya_hbm)
    pack_rows(sz, copies, gets, w, out, out_hbm)
    copies.finish()


def pack_call(sz, after, weight, start, by=None):
    half = sz.half_j
    packed = (half, sz.blk_k, sz.groups * 128, sz.lgs * sz.chans)
    lines = (sz.lines * 128, sz.modes_y * sz.cpl)
    outs = [(shape(packed), True)]
    args = (after, weight)
    scratch = [pltpu.VMEM((half,) + weight.shape[2:], bf16), pltpu.VMEM(packed, bf16)]
    tables = by is not None
    if tables:
        outs.append((shape(lines), True))
        args += (by,)
        scratch += [pltpu.VMEM(by.shape, bf16), pltpu.VMEM(lines, bf16)]
    result = run(
        "pack",
        lambda *refs: pack_kernel(sz, start, tables, *refs),
        outs,
        [hbm] * len(args),
        args,
        scratch,
        2 * half + 2 * tables,
        0,
    )
    return result if tables else result[0]


def line_analysis(sz, r_ref, ya_ref, get_ya, fine=True):
    jk = sz.jk

    def total(sec, gy, start, step):
        result = None
        for gx in range(start, sz.n_gx, step):
            at = ((sec * sz.n_gx + gx) * sz.n_gy + gy) * jk
            part = r_ref[at : at + jk, :].astype(f32)
            result = part if result is None else result + part
        return result

    halves = [[], []]
    low = iota((jk, 128), 1) < 64
    for sec in range(2):
        for gy in range(sz.n_gy):
            if fine:
                a, b = total(sec, gy, 0, 2), total(sec, gy, 1, 2)
                halves[0].append(jnp.where(low, a, pltpu.roll(b, 64, 1)).astype(bf16))
                halves[1].append(jnp.where(low, pltpu.roll(a, 64, 1), b).astype(bf16))
            else:
                line = total(sec, gy, 0, 1).astype(bf16)
                for h in range(sz.groups):
                    halves[h].append(line[:, h * 128 : (h + 1) * 128])
    rows = jnp.concatenate([jnp.concatenate(half, axis=1) for half in halves], axis=0)
    if get_ya is not None:
        get_ya.wait()
    return nn(rows, ya_ref[...]).astype(bf16)


def diagonal(sz, count):
    shape = (count, sz.groups * 128)
    return iota(shape, 0) % 8 == (iota(shape, 1) % 128) // sz.cpl


def row_spread(sz):
    shape = (sz.jk * 8, sz.jk)
    return (iota(shape, 0) // 8 == iota(shape, 1)).astype(bf16)


def row_gather(sz):
    shape = (sz.jk, sz.jk * 8)
    return (iota(shape, 1) // 8 == iota(shape, 0)).astype(bf16)


def chan_lanes(sz):
    shape = (sz.groups * 128, sz.chans)
    lane = iota(shape, 0)
    return ((lane // 128) * sz.cpl + lane % sz.cpl == iota(shape, 1)).astype(bf16)


def to_blocks(sz, rows, lg):
    jk = sz.jk
    wide = jnp.concatenate(
        [rows[h * jk : (h + 1) * jk, lg * 128 : (lg + 1) * 128] for h in range(sz.groups)], axis=1
    )
    return jnp.where(diagonal(sz, jk * 8), nn(row_spread(sz), wide), 0.0)


def from_blocks(sz, blocks):
    jk = sz.jk
    pieces = []
    for block in blocks:
        kept = jnp.where(diagonal(sz, jk * 8), block, 0.0).astype(bf16)
        pieces.append(nn(row_gather(sz), kept).astype(bf16))
    return jnp.concatenate(
        [
            jnp.concatenate([piece[:, h * 128 : (h + 1) * 128] for piece in pieces], axis=1)
            for h in range(sz.groups)
        ],
        axis=0,
    )


def send_lines(sz, rows, ya_ref, out_ref):
    jk = sz.jk
    lines = nt(rows, ya_ref[...])
    low = iota((jk, 128), 1) < 64
    for sec in range(2):
        for gy in range(sz.n_gy):
            line = sec * sz.n_gy + gy
            a, b = [lines[h * jk : (h + 1) * jk, line * 128 : (line + 1) * 128] for h in range(2)]
            quarters = [
                jnp.where(low, a, pltpu.roll(b, 64, 1)).astype(bf16),
                jnp.where(low, pltpu.roll(a, 64, 1), b).astype(bf16),
            ]
            for gx in range(sz.n_gx):
                at = ((sec * sz.n_gx + gx) * sz.n_gy + gy) * jk
                out_ref[at : at + jk, :] = quarters[gx % 2]


def lane_group(sz):
    dims = (sz.lgs * sz.jk * 8, sz.lgs * sz.chans)
    return iota(dims, 0) // (sz.jk * 8) == iota(dims, 1) // sz.chans


def mix_kernel(sz, layer, turn, s_ref, r, ya_in, *rest):
    if layer == 0:
        low_hbm, high_hbm, *rest = rest
        spec_hbm, out, ya, w, spec_b, blk, mix, sems = rest[3:]
    else:
        ya = ya_in
        w, spec_hbm, out, spec_b, blk, mix, sems = rest
    copies = Copies(sems)
    get_ya = copies.start(ya_in, ya) if layer == 0 else None
    if layer == 0:
        get_w = copies.choose(s_ref[0] == 0, [(low_hbm.at[jj], high_hbm.at[jj], w.at[jj]) for jj in range(sz.half_j)])
    spec = line_analysis(sz, r, ya, get_ya, layer > 0)
    spec_b[...] = spec
    copies.send(spec_b, spec_hbm)
    count = sz.jk * 8
    width = sz.lgs * sz.chans
    rep = jnp.concatenate([chan_lanes(sz)] * sz.lgs, axis=1)
    blocks = [to_blocks(sz, spec, lg) for lg in range(sz.lgs)]
    if turn:
        flat = nn(jnp.concatenate(blocks, axis=0).astype(bf16), rep)
        mix[:, :width] = jnp.where(lane_group(sz), flat, 0.0)
        left_ref, right_ref, left_width = mix, blk, width
    else:
        for lg in range(sz.lgs):
            blk[lg * count : (lg + 1) * count, :] = blocks[lg]
        left_ref, right_ref, left_width = blk, mix, blk.shape[1]
    for jk in range(sz.jk):
        jj, kk = jk // sz.blk_k, jk % sz.blk_k
        if kk == 0 and layer == 0:
            get_w[jj].wait()
        at = [slice((lg * sz.jk + jk) * 8, (lg * sz.jk + jk + 1) * 8) for lg in range(sz.lgs)]
        left = jnp.concatenate([left_ref[a, :left_width] for a in at], axis=0).astype(bf16)
        part = nt(left, w[jj, kk]) if turn else nn(left, w[jj, kk])
        for lg, a in enumerate(at):
            right_ref[a, : part.shape[1]] = part[lg * 8 : (lg + 1) * 8]
    if not turn:
        kept_mix = jnp.where(lane_group(sz), mix[:, :width], 0.0).astype(bf16)
        full = nt(kept_mix, rep)
    else:
        full = blk[...]
    blocks = [full[lg * count : (lg + 1) * count] for lg in range(sz.lgs)]
    send_lines(sz, from_blocks(sz, blocks), ya, out)
    copies.finish()


def mix_call(sz, layer, turn, s, r, ya, weights, after=()):
    count = sz.jk * 8 * sz.lgs
    spec = (sz.groups * sz.jk, sz.modes_y * sz.cpl)
    line = (sz.modes, sz.thin)
    outs = [(shape(spec), True), (kept(line), False)]
    scratch = [pltpu.VMEM(spec, bf16)] + [pltpu.VMEM((count, sz.groups * 128), f32)] * 2
    if layer == 0:
        outs.append((kept(ya.shape), False))
        scratch = [pltpu.VMEM(weights[0].shape, bf16)] + scratch
        specs = [smem, vmem] + [hbm] * (3 + len(after))
    else:
        ya = near(ya)
        weights = [near(weights)]
        specs = [smem] + [vmem] * 3
    return run(
        "mix",
        lambda *refs: mix_kernel(sz, layer, turn, *refs),
        outs,
        specs,
        (s, r, ya, *weights, *after),
        scratch,
        sz.half_j + 2,
    )


def gate_kernel(sz, in_ref, after_hbm, out_ref):
    out_ref[...] = in_ref[...]


def gate_call(sz, value, after):
    (out,) = run(
        "gate",
        lambda *refs: gate_kernel(sz, *refs),
        [(kept(value.shape), False)],
        [vmem, hbm],
        (near(value), after),
        micros=0,
    )
    return out


def spec_kernel(sz, s_ref, r, ya, sv0_hbm, sv1_hbm, su1_hbm, mine, sends, before, sems):
    copies = Copies(sems)
    gets = [copies.start(src, before.at[at]) for at, src in enumerate((sv0_hbm, sv1_hbm, su1_hbm))]
    first = s_ref[0] == 0
    spec = line_analysis(sz, r, ya, None)
    for get in gets:
        get.wait()
    sv0, sv1, su1 = [before[at] for at in range(3)]
    sends[0] = jnp.where(first, sv1, sv0)
    sends[1] = jnp.where(first, su1, spec)
    mine[0] = jnp.where(first, sv0, sv1)
    mine[1] = jnp.where(first, spec, su1)


def spec_call(sz, s, r, sv0, sv1, su1, ya):
    spec = (sz.groups * sz.jk, sz.modes_y * sz.cpl)
    return run(
        "spec",
        lambda *refs: spec_kernel(sz, *refs),
        [(kept((2,) + spec), False), (kept((2,) + spec), False)],
        [smem, vmem, vmem, hbm, hbm, hbm],
        (s, r, near(ya), sv0, sv1, su1),
        [pltpu.VMEM((3,) + spec, bf16)],
        3,
    )


def turned_modes(sz, u_ref, layer):
    left = jnp.transpose(u_ref[...])
    half = sz.modes // 2
    if layer == 1:
        left = jnp.concatenate([left[:, half:], left[:, :half]], axis=1)
    return left


CHUNK = 1024


def cuts(sz):
    return [slice(at, at + CHUNK) for at in range(0, sz.wide, CHUNK)]


def small_parts(sz, s_ref, own_ref, other_ref, layer):
    chosen = jnp.where(s_ref[0] == layer, own_ref[...].astype(f32), other_ref[...].astype(f32)).astype(bf16)
    return chosen[: sz.chans], chosen[sz.chans :]


def field_copies(sz, copies, mine_hbm, other_hbm, field):
    return [
        copies.start(mine_hbm, field.at[:, : sz.cells]),
        copies.start(other_hbm, field.at[:, sz.cells :]),
    ]


def thirds(value):
    high = value.astype(bf16)
    rest = value - high.astype(f32)
    middle = rest.astype(bf16)
    return [high, middle, (rest - middle.astype(f32)).astype(bf16)]


def point_sums(sz, v, d):
    pairs = jnp.where(same_y(sz), nt(v, d), 0.0)
    bias = nt(jnp.ones((8, sz.wide), bf16), d)
    dims = (sz.chans, 3 * sz.thin)
    fold = (iota(dims, 1) % sz.thin // sz.fine == iota(dims, 0)).astype(bf16)
    pairs = nn(fold, jnp.concatenate(thirds(pairs), axis=0))
    part = sz.chans // 4
    rows = []
    for t in range(4):
        below = bias if t == 0 else jnp.zeros_like(bias)
        both = jnp.concatenate([pairs[t * part : (t + 1) * part], below], axis=0)
        rows.append(jnp.concatenate(thirds(both), axis=0))
    dims = (4 * sz.thin, 128)
    row = iota(dims, 0)
    place = (row // sz.thin * sz.chans + row % sz.thin // sz.fine == iota(dims, 1)).astype(bf16)
    total = nn(jnp.concatenate(rows, axis=1), place)
    count = part + 8
    return total[:count] + total[count : 2 * count] + total[2 * count :]


def forward_kernel(
    sz, s_ref, own_hbm, other_hbm, u, mine_hbm, next_hbm, bb_hbm, low_hbm, high_hbm, v, slope, bb, out, w, field, own_ref, other_ref, sems
):
    copies = Copies(sems)
    get_small = [copies.start(own_hbm, own_ref), copies.start(other_hbm, other_ref)]
    get_bb, get_v = [], []
    for at, cut in enumerate(cuts(sz)):
        get_bb.append(copies.start(bb_hbm.at[:, cut], bb.at[:, cut]))
        if at == 0:
            get_v = field_copies(sz, copies, mine_hbm, next_hbm, field)
    (get_w,) = copies.choose(s_ref[0] == 1, [(low_hbm, high_hbm, w)])
    for get in get_small:
        get.wait()
    weight, bias = small_parts(sz, s_ref, own_ref, other_ref, 0)
    matrix = point_matrix(sz, weight, True)
    column = nt(spread(sz), bias)[:, :1]
    left = turned_modes(sz, u, 0)
    for at, cut in enumerate(cuts(sz)):
        get_bb[at].wait()
        if cut.start % sz.cells == 0:
            get_v[cut.start // sz.cells].wait()
        pre = nn(left, bb[:, cut]) + nn(matrix, field[:, cut]) + column
        value, rate = activate(pre)
        v[:, cut] = value.astype(bf16)
        slope[:, cut] = rate
    send_analysis(sz, bb, v[...], out, 1)
    get_w.wait()


def forward_call(sz, s, mine, other, u, bb, own_small, other_small, low, high):
    field, line = (sz.thin, sz.wide), (sz.modes, sz.thin)
    return run(
        "forward",
        lambda *refs: forward_kernel(sz, *refs),
        [
            (kept(field), False),
            (kept(field, f32), False),
            (kept((sz.modes, sz.wide)), False),
            (kept(line), False),
            (kept(low.shape), False),
        ],
        [smem, hbm, hbm, vmem, hbm, hbm, hbm, hbm, hbm],
        (s, own_small, other_small, u, mine, other, bb, low, high),
        [pltpu.VMEM(field, bf16), pltpu.VMEM(own_small.shape, bf16), pltpu.VMEM(own_small.shape, bf16)],
        5 + len(cuts(sz)),
    )


def turn_kernel(sz, s_ref, own_ref, other_ref, u, v, bb, mine_hbm, next_hbm, d, sums, out, grad, sems):
    copies = Copies(sems)
    get_g = field_copies(sz, copies, mine_hbm, next_hbm, grad)
    weight, bias = small_parts(sz, s_ref, own_ref, other_ref, 1)
    matrix = point_matrix(sz, weight, True)
    column = nt(spread(sz), bias)[:, :1]
    left = turned_modes(sz, u, 1)
    for at, cut in enumerate(cuts(sz)):
        pre = nn(left, bb[:, cut]) + nn(matrix, v[:, cut]) + column
        _, rate = activate(pre)
        if at == 0:
            for get in get_g:
                get.wait()
        d[:, cut] = (grad[:, cut].astype(f32) * rate).astype(bf16)
    send_analysis(sz, bb, d[...], out, 1)
    sums[...] = point_sums(sz, v[...], d[...])


def turn_call(sz, s, mine, other, v, u, bb, own_small, other_small):
    field, line = (sz.thin, sz.wide), (sz.modes, sz.thin)
    return run(
        "turn",
        lambda *refs: turn_kernel(sz, *refs),
        [(kept(field), False), (kept((sz.chans // 4 + 8, 128), f32), False), (kept(line), False)],
        [smem, vmem, vmem, vmem, vmem, vmem, hbm, hbm],
        (s, own_small, other_small, u, near(v), near(bb), mine, other),
        [pltpu.VMEM(field, bf16)],
        2,
    )


def pieces(sz, value):
    part = sz.chans // 4
    high = value.astype(bf16).astype(f32)
    low = value - high
    bias = jnp.where(iota((8, 128), 0) < 4, high[part:], low[part:])
    return jnp.concatenate([high[:part], low[:part], bias], axis=0).astype(bf16)


def back_kernel(
    sz, s_ref, own_ref, other_ref, u, d, slope, bb, sums, mine_hbm, next_hbm, parts, out, new, field, sems
):
    copies = Copies(sems)
    get_v = field_copies(sz, copies, mine_hbm, next_hbm, field)
    weight, _ = small_parts(sz, s_ref, own_ref, other_ref, 1)
    matrix = point_matrix(sz, weight, False)
    left = turned_modes(sz, u, 1)
    for cut in cuts(sz):
        grad = (nn(left, bb[:, cut]) + nn(matrix, d[:, cut])).astype(bf16).astype(f32)
        new[:, cut] = (grad * slope[:, cut]).astype(bf16)
    for get in get_v:
        get.wait()
    send_analysis(sz, bb, new[...], out, 0)
    first = point_sums(sz, field[...], new[...])
    half = sz.places // 2
    for layer, value in enumerate((first, sums[...])):
        block = pieces(sz, value)
        for place in range(half):
            parts[layer * half + place] = block


def back_call(sz, s, mine, other, d, slope, u, bb, sums, own_small, other_small):
    parts, line, field = (sz.places, sz.chans // 2 + 8, 128), (sz.modes, sz.thin), (sz.thin, sz.wide)
    return run(
        "back",
        lambda *refs: back_kernel(sz, *refs),
        [(kept(parts), False), (kept(line), False)],
        [smem] + [vmem] * 7 + [hbm, hbm],
        (s, own_small, other_small, u, near(d), near(slope), near(bb), near(sums), mine, other),
        [pltpu.VMEM(field, bf16), pltpu.VMEM(field, bf16)],
        2,
    )


def finish_kernel(sz, parts_ref, after_ref, point_ref, bias_ref):
    total = jnp.sum(parts_ref[...].astype(f32), axis=0)
    part = sz.chans // 4
    bias_ref[...] = (total[2 * part : 2 * part + 1] + total[2 * part + 4 : 2 * part + 5])[:, : sz.chans]
    total = total[:part] + total[part : 2 * part]
    for t in range(4):
        point_ref[0, t * part : (t + 1) * part, :] = total[:part, t * sz.chans : (t + 1) * sz.chans]


def finish_call(sz, parts, after):
    return pl.pallas_call(
        lambda *refs: finish_kernel(sz, *refs),
        out_shape=(shape((1, sz.chans, sz.chans), f32), shape((1, sz.chans), f32)),
        in_specs=[vmem, hbm],
        out_specs=(vmem, vmem),
        compiler_params=pltpu.CompilerParams(vmem_limit_bytes=limit),
        name="finish",
    )(parts, far(after))


def outer_kernel(sz, mine_ref, theirs_ref, out_ref, left_ref, right_ref):
    jk, groups, kk_count = sz.jk, sz.groups, sz.blk_k
    step = pl.program_id(0)

    def prepare(side, sv, su):
        sv = sv.astype(f32)
        for jj in range(sz.half_j):
            place = side * sz.half_j + jj
            rows = jnp.concatenate(
                [sv[h * jk + jj * kk_count : h * jk + (jj + 1) * kk_count] for h in range(groups)], axis=0
            )
            left_ref[place] = jnp.transpose(rows).astype(bf16)
        for lg in range(sz.lgs):
            flat = nn(to_blocks(sz, su, lg).astype(bf16), chan_lanes(sz))
            for at in range(jk):
                place = side * sz.half_j + at // kk_count
                right_ref[place, at % kk_count, lg * 8 : (lg + 1) * 8, :] = flat[at * 8 : (at + 1) * 8]

    @pl.when(step == 0)
    def _():
        prepare(0, mine_ref[0], mine_ref[1])

    @pl.when(step == 1)
    def _():
        prepare(1, theirs_ref[0], theirs_ref[1])

    dims = (groups * kk_count, groups * kk_count * 128)
    spread_lanes = (iota(dims, 0) == iota(dims, 1) // 128).astype(bf16)
    each = out_ref.shape[1]
    for sub in range(each):
        columns = nn(left_ref[step * each + sub], spread_lanes)
        for kk in range(kk_count):
            for ll in range(sz.modes_y):
                row = right_ref[step * each + sub, kk, ll : ll + 1, :]
                for h in range(groups):
                    at = (h * kk_count + kk) * 128
                    part = columns[ll * sz.cpl : (ll + 1) * sz.cpl, at : at + sz.chans] * row
                    out_ref[0, sub, kk, ll, h * sz.cpl : (h + 1) * sz.cpl, :] = part


def outer_call(sz, mine, theirs):
    each = max(1, sz.half_j // 2)
    wide = sz.modes_y * sz.cpl
    return pl.pallas_call(
        lambda *refs: outer_kernel(sz, *refs),
        grid=(sz.blk_j // each,),
        out_shape=pltpu.HBM((1, sz.blk_j, sz.blk_k, sz.modes_y, sz.chans, sz.chans), f32),
        in_specs=[vmem] * 2,
        out_specs=pl.BlockSpec((1, each, sz.blk_k, sz.modes_y, sz.chans, sz.chans), lambda i: (0, i, 0, 0, 0, 0)),
        scratch_shapes=[
            pltpu.VMEM((sz.blk_j, wide, sz.groups * sz.blk_k), bf16),
            pltpu.VMEM((sz.blk_j, sz.blk_k, sz.modes_y, sz.chans), f32),
        ],
        compiler_params=pltpu.CompilerParams(vmem_limit_bytes=limit),
        cost_estimate=pl.CostEstimate(flops=0, transcendentals=0, bytes_accessed=20000000),
        name="outer",
    )(near(mine), theirs)


def exchange(block):
    return lax.all_to_all(block, AXES, split_axis=0, concat_axis=0, tiled=True)


def swap(block):
    return lax.ppermute(block, "section", [(0, 1), (1, 0)])


def swap_near(sz, block):
    return lax.ppermute(block, "gx", [(i, i ^ 1) for i in range(sz.n_gx)])


def local(ends, spectral_weight, point_weight, point_bias):
    sz = Sizes(ends, spectral_weight)
    section = lax.axis_index("section")
    first = section == 0
    s = section.astype(jnp.int32).reshape(1)

    def half(field, which):
        part = lax.dynamic_slice_in_dim(field, which * sz.len_y, sz.len_y, axis=2)
        return jnp.swapaxes(part, 1, 2).reshape(sz.rows, sz.cells)

    bx, bz, by = [jnp.asarray(t.astype(ml_dtypes.bfloat16)) for t in mode_tables(sz)]
    send = half(ends[0], 1 - section)
    send, later = lax.optimization_barrier((send, ends[0]))
    recv = swap(send)
    keep = half(later, section)
    gx = lax.axis_index("gx").astype(jnp.int32)
    gx = jnp.stack([gx, gx + 1 - 2 * (gx % 2)])
    bb = tables_call(sz, gx, bx, bz)
    own_small = jnp.concatenate([point_weight[0], jnp.broadcast_to(point_bias, (16, sz.chans))], axis=0)
    other_small = swap(own_small)
    mine_v, send_v, raw_g, out, high = first_call(sz, s, gx, keep, recv, bb, spectral_weight)
    high = swap(high)
    next_v = swap_near(sz, send_v)
    r = exchange(out)
    mine_g, send_g = split_call(sz, gx, raw_g, mine_v)
    next_g = swap_near(sz, send_g)
    low, ya = pack_call(sz, mine_v, spectral_weight, 0, by)
    bb = wide_call(sz, gx, bx, bz, mine_v)
    sv0, out, ya = mix_call(sz, 0, False, s, r, ya, (low, high), (other_small, bb, next_v))
    v1, slope0, bb, out, w1 = forward_call(sz, s, mine_v, next_v, exchange(out), bb, own_small, other_small, low, high)
    sv1, out = mix_call(sz, 1, False, s, exchange(out), ya, w1)
    out = gate_call(sz, out, next_g)
    d1, sums, out = turn_call(sz, s, mine_g, next_g, v1, exchange(out), bb, own_small, other_small)
    su1, out = mix_call(sz, 1, True, s, exchange(out), ya, w1)
    parts, out = back_call(sz, s, mine_v, next_v, d1, slope0, exchange(out), bb, sums, own_small, other_small)
    r, parts = lax.optimization_barrier((exchange(out), parts))
    mine, send = spec_call(sz, s, r, sv0, sv1, su1, ya)
    theirs = swap(send)
    parts = lax.all_to_all(parts, AXES, split_axis=0, concat_axis=0, tiled=True)
    spectral_grad = outer_call(sz, mine, theirs)
    point_grad, bias_grad = finish_call(sz, parts, spectral_grad)
    return (spectral_grad, point_grad, bias_grad)


def solution(mesh):
    return jax.shard_map(
        local,
        mesh=mesh,
        in_specs=(
            P("section", None, "gx", "gy", None),
            P("section", "gy", "gx", None, None, None),
            P("section", None, None),
            P("section", None),
        ),
        out_specs=(
            P("section", "gy", "gx", None, None, None),
            P("section", None, None),
            P("section", None),
        ),
        check_vma=False,
    )
```

```python
import math

import jax
import jax.numpy as jnp
import ml_dtypes
import numpy as np
from jax import lax
from jax.experimental import pallas as pl
from jax.experimental.pallas import tpu as pltpu
from jax.sharding import PartitionSpec as P

gelu_coef = 0.7978845608028654
f32 = jnp.float32
bf16 = jnp.bfloat16
AXES = ("section", "gx", "gy")


def table(length, count):
    half = count // 2
    modes = np.arange(count)
    is_cos = modes < half
    wave = np.where(is_cos, modes, modes - half + 1)
    phase = wave[:, None] * np.arange(length)[None, :] % length
    angle = phase.astype(np.float32) * np.float32(2.0 * math.pi / length)
    values = np.where(is_cos[:, None], np.cos(angle), np.sin(angle)).astype(np.float32)
    scale = np.where(is_cos & (wave == 0), math.sqrt(1.0 / length), math.sqrt(2.0 / length))
    return (values * scale.astype(np.float32)[:, None]).astype(ml_dtypes.bfloat16).astype(np.float32)


def nn(a, b):
    return lax.dot_general(a, b, (((1,), (0,)), ((), ())), preferred_element_type=f32)


def nt(a, b):
    return lax.dot_general(a, b, (((1,), (1,)), ((), ())), preferred_element_type=f32)


def tn(a, b):
    return lax.dot_general(a, b, (((0,), (0,)), ((), ())), preferred_element_type=f32)


def iota(shape, dim):
    return lax.broadcasted_iota(jnp.int32, shape, dim)


limit = 24 * 1024 * 1024
smem = pl.BlockSpec(memory_space=pltpu.SMEM)
hbm = pl.BlockSpec(memory_space=pltpu.HBM)
vmem = pl.BlockSpec(memory_space=pltpu.VMEM)


def shape(dims, dtype=bf16):
    return jax.ShapeDtypeStruct(dims, dtype)


def kept(dims, dtype=bf16):
    return pltpu.VMEM(dims, dtype)


def near(value):
    return pltpu.with_memory_space_constraint(value, pltpu.VMEM)


def far(value):
    return pltpu.with_memory_space_constraint(value, pltpu.HBM)


def run(name, kernel, outs, specs, args, scratch=(), copies=0, micros=1):
    return pl.pallas_call(
        kernel,
        out_shape=tuple(pltpu.HBM(o.shape, o.dtype) if away else o for o, away in outs),
        in_specs=list(specs),
        out_specs=tuple(hbm if away else vmem for _, away in outs),
        scratch_shapes=list(scratch) + ([pltpu.SemaphoreType.DMA((copies,))] if copies else []),
        compiler_params=pltpu.CompilerParams(vmem_limit_bytes=limit),
        cost_estimate=pl.CostEstimate(flops=0, transcendentals=0, bytes_accessed=micros * 3000000),
        name=name,
    )(*[far(a) if spec is hbm else a for a, spec in zip(args, specs)])


class Copies:
    def __init__(self, sems):
        self.sems = sems
        self.used = 0
        self.open = []

    def make(self, src, dst):
        copy = pltpu.make_async_copy(src, dst, self.sems.at[self.used])
        self.used += 1
        return copy

    def start(self, src, dst):
        copy = self.make(src, dst)
        copy.start()
        return copy

    def choose(self, pick, triples):
        firsts, others = [], []
        for src, other, dst in triples:
            firsts.append(pltpu.make_async_copy(src, dst, self.sems.at[self.used]))
            others.append(self.make(other, dst))

        @pl.when(pick)
        def _():
            for copy in firsts:
                copy.start()

        @pl.when(jnp.logical_not(pick))
        def _():
            for copy in others:
                copy.start()

        return others

    def send(self, src, dst):
        self.open.append(self.start(src, dst))

    def finish(self):
        for copy in self.open:
            copy.wait()


class Sizes:
    def __init__(self, ends, weight):
        self.n_gx = lax.axis_size("gx")
        self.n_gy = lax.axis_size("gy")
        _, self.chans, self.len_x, full, self.depth = ends.shape
        self.len_y = full // 2
        _, self.blk_j, self.blk_k, self.modes_y, _, _ = weight.shape
        self.half_j = self.blk_j // 2
        self.jk = self.half_j * self.blk_k
        self.places = 2 * self.n_gx * self.n_gy
        self.modes = self.places * self.jk
        self.rows = self.chans * self.len_y
        self.cells = self.len_x * self.depth
        self.lines = 2 * self.n_gy
        self.cpl = 128 // self.len_y
        self.groups = self.rows // 128
        self.lgs = self.modes_y // 8
        self.full_x = self.len_x * self.n_gx
        self.fine = self.len_y // 2
        self.thin = self.chans * self.fine
        self.wide = 2 * self.cells
        self.full_y = full * self.n_gy


def mode_tables(sz):
    bx = table(sz.full_x, sz.blk_j * sz.n_gy)
    bz = table(sz.depth, sz.blk_k * sz.n_gx)
    by = table(sz.full_y, sz.modes_y)
    sec, gx, gy, jj, kk = np.meshgrid(
        np.arange(2), np.arange(sz.n_gx), np.arange(sz.n_gy), np.arange(sz.half_j), np.arange(sz.blk_k), indexing="ij"
    )
    row_j = (gy * sz.blk_j + sec * sz.half_j + jj).reshape(-1)
    row_k = (gx * sz.blk_k + kk).reshape(-1)
    sec, gy, yy = np.meshgrid(np.arange(2), np.arange(sz.n_gy), np.arange(sz.len_y), indexing="ij")
    row_y = (gy * 2 * sz.len_y + sec * sz.len_y + yy).reshape(-1)
    bx = np.moveaxis(bx[row_j].reshape(sz.modes, sz.n_gx, sz.len_x), 1, 0)
    lines = by[:, row_y].T.reshape(sz.lines, 2, 1, sz.fine, sz.modes_y)
    lines = np.broadcast_to(lines, (sz.lines, 2, 8 // sz.fine, sz.fine, sz.modes_y)).reshape(-1, sz.modes_y)
    return bx, bz[row_k], np.repeat(lines, sz.cpl, axis=1)


def activate(pre):
    square = pre * pre
    tanh_val = jnp.tanh(pre * (gelu_coef + (gelu_coef * 0.044715) * square))
    half = 0.5 + 0.5 * tanh_val
    value = pre * half
    slope = half + value * (1.0 - tanh_val) * (gelu_coef + (3.0 * gelu_coef * 0.044715) * square)
    return value, slope


def spread(sz):
    shape = (sz.thin, sz.chans)
    return (iota(shape, 0) // sz.fine == iota(shape, 1)).astype(bf16)


def same_y(sz):
    shape = (sz.thin, sz.thin)
    return iota(shape, 0) % sz.fine == iota(shape, 1) % sz.fine


def point_matrix(sz, weight, forward):
    one = spread(sz)
    part = nt(one, weight) if forward else nn(one, weight)
    full = nt(part.astype(bf16), one)
    return jnp.where(same_y(sz), full, 0.0).astype(bf16)


def swapped(rows, half):
    return jnp.concatenate([rows[half:], rows[:half]], axis=0)


def send_analysis(sz, bb_ref, field, out_ref, layer):
    out = nt(bb_ref[...], field).astype(bf16)
    out_ref[...] = swapped(out, sz.modes // 2) if layer == 1 else out


def fill_table(sz, bx, bz, bb):
    depth = sz.depth
    across, along = bx[...].astype(f32), bz[...].astype(f32)
    for x in range(sz.len_x):
        bb[:, x * depth : (x + 1) * depth] = (across[:, x : x + 1] * along).astype(bf16)


def pack_rows(sz, copies, gets, w, out, out_hbm):
    for jj in range(sz.half_j):
        gets[jj].wait()
        for kk in range(sz.blk_k):
            for h in range(sz.groups):
                lanes = [
                    w[jj, kk, lg * 8 : (lg + 1) * 8, h * sz.cpl : (h + 1) * sz.cpl, :].reshape(128, sz.chans)
                    for lg in range(sz.lgs)
                ]
                out[jj, kk, h * 128 : (h + 1) * 128, :] = jnp.concatenate(lanes, axis=1)
        copies.send(out.at[jj], out_hbm.at[jj])


def tables_kernel(sz, gx_ref, bx_hbm, bz_hbm, bb, bx, bz, sems):
    copies = Copies(sems)
    get_bx = copies.start(bx_hbm.at[gx_ref[0]], bx)
    get_bz = copies.start(bz_hbm, bz)
    get_bx.wait()
    get_bz.wait()
    fill_table(sz, bx, bz, bb)


def tables_call(sz, gx, bx, bz):
    (bb,) = run(
        "tables",
        lambda *refs: tables_kernel(sz, *refs),
        [(kept((sz.modes, sz.cells)), False)],
        [smem, hbm, hbm],
        (gx, bx, bz),
        [pltpu.VMEM(bx.shape[1:], bf16), pltpu.VMEM(bz.shape, bf16)],
        2,
    )
    return bb


def reorder(sz):
    dims = (sz.rows, sz.rows)
    row = iota(dims, 0)
    group, quarter = row // 128, row % 128 // 64
    chan, y = group * sz.cpl + row % 64 // sz.fine, quarter * sz.fine + row % sz.fine
    return (chan * sz.len_y + y == iota(dims, 1)).astype(bf16)


def send_quarters(sz, gx_ref, field, mine_hbm, send_hbm, copies):
    quarter = gx_ref[0] % 2
    for h in range(sz.groups):
        to = slice(h * 64, (h + 1) * 64)
        copies.send(field.at[pl.ds(h * 128 + quarter * 64, 64)], mine_hbm.at[to])
        copies.send(field.at[pl.ds(h * 128 + (1 - quarter) * 64, 64)], send_hbm.at[to])


def wide_kernel(sz, gx_ref, bx_hbm, bz_hbm, after_hbm, bb_hbm, bx, bz, bb, sems):
    copies = Copies(sems)
    gets = [copies.start(bx_hbm.at[gx_ref[side]], bx.at[side]) for side in range(2)]
    gets.append(copies.start(bz_hbm, bz))
    for get in gets:
        get.wait()
    depth = sz.depth
    along = bz[...].astype(f32)
    for side in range(2):
        across = bx[side].astype(f32)
        for x in range(sz.len_x):
            at = side * sz.cells + x * depth
            bb[:, at : at + depth] = (across[:, x : x + 1] * along).astype(bf16)
            if x % 4 == 3:
                part = slice(at - 3 * depth, at + depth)
                copies.send(bb.at[:, part], bb_hbm.at[:, part])
    copies.finish()


def wide_call(sz, gx, bx, bz, after):
    (bb,) = run(
        "wide",
        lambda *refs: wide_kernel(sz, *refs),
        [(shape((sz.modes, sz.wide)), True)],
        [smem, hbm, hbm, hbm],
        (gx, bx, bz, after),
        [pltpu.VMEM((2,) + bx.shape[1:], bf16), pltpu.VMEM(bz.shape, bf16), pltpu.VMEM((sz.modes, sz.wide), bf16)],
        3 + sz.len_x // 2,
        0,
    )
    return bb


def first_kernel(
    sz, s_ref, gx_ref, keep, recv, bb, w_hbm, mine_hbm, send_hbm, raw_hbm, out_hbm, high_hbm, v, out, w, high, sems
):
    copies = Copies(sems)
    first = s_ref[0] == 0
    gets = [copies.start(w_hbm.at[0, sz.half_j + jj], w.at[jj]) for jj in range(sz.half_j)]
    v[...] = nn(reorder(sz), jnp.where(first, keep[...], recv[...])).astype(bf16)
    send_quarters(sz, gx_ref, v, mine_hbm, send_hbm, copies)
    send_analysis(sz, bb, v[...], out, 0)
    copies.send(out, out_hbm)
    (put_raw,) = copies.choose(first, [(recv, keep, raw_hbm)])
    pack_rows(sz, copies, gets, w, high, high_hbm)
    put_raw.wait()
    copies.finish()


def first_call(sz, s, gx, keep, recv, bb, weight):
    line, field, part = (sz.modes, sz.rows), (sz.rows, sz.cells), (sz.thin, sz.cells)
    packed = (sz.half_j, sz.blk_k, sz.groups * 128, sz.lgs * sz.chans)
    return run(
        "first",
        lambda *refs: first_kernel(sz, *refs),
        [(shape(part), True), (shape(part), True), (shape(field), True), (shape(line), True), (shape(packed), True)],
        [smem, smem, vmem, vmem, vmem, hbm],
        (s, gx, keep, recv, near(bb), weight),
        [
            pltpu.VMEM(field, bf16),
            pltpu.VMEM(line, bf16),
            pltpu.VMEM((sz.half_j,) + weight.shape[2:], bf16),
            pltpu.VMEM(packed, bf16),
        ],
        2 + 2 * sz.groups + 2 * sz.half_j,
    )


def split_kernel(sz, gx_ref, raw_hbm, after_hbm, mine_hbm, send_hbm, raw, field, sems):
    copies = Copies(sems)
    half = sz.cells // 2
    halves = [slice(0, half), slice(half, sz.cells)]
    gets = [copies.start(raw_hbm.at[:, cut], raw.at[:, cut]) for cut in halves]
    matrix = reorder(sz)
    for get, cut in zip(gets, halves):
        get.wait()
        field[:, cut] = nn(matrix, raw[:, cut]).astype(bf16)
        send_quarters(
            sz, gx_ref, field.at[:, cut], mine_hbm.at[:, cut], send_hbm.at[:, cut], copies
        )
    copies.finish()


def split_call(sz, gx, raw, after):
    field, part = (sz.rows, sz.cells), (sz.thin, sz.cells)
    return run(
        "split",
        lambda *refs: split_kernel(sz, *refs),
        [(shape(part), True), (shape(part), True)],
        [smem, hbm, hbm],
        (gx, raw, after),
        [pltpu.VMEM(field, bf16), pltpu.VMEM(field, bf16)],
        2 + 4 * sz.groups,
        0,
    )


def pack_kernel(sz, start, tables, *refs):
    if tables:
        after_hbm, w_hbm, by_hbm, out_hbm, ya_hbm, w, out, by, ya, sems = refs
    else:
        after_hbm, w_hbm, out_hbm, w, out, sems = refs
    copies = Copies(sems)
    if tables:
        get_by = copies.start(by_hbm, by)
    gets = [copies.start(w_hbm.at[0, start + jj], w.at[jj]) for jj in range(sz.half_j)]
    if tables:
        get_by.wait()
        table = by[...].astype(f32)
        wide = sz.modes_y * sz.cpl
        lane_c = iota((8, wide), 1) % sz.cpl
        each = 8 // sz.fine
        row_c = iota((8, wide), 0) // sz.fine
        for g in range(sz.lines):
            pieces = []
            for quarter in range(2):
                at = (g * 2 + quarter) * 8
                part = table[at : at + 8, :]
                pieces += [jnp.where(lane_c == c + row_c, part, 0.0) for c in range(0, sz.cpl, each)]
            ya[g * 128 : (g + 1) * 128, :] = jnp.concatenate(pieces, axis=0).astype(bf16)
        copies.send(ya, ya_hbm)
    pack_rows(sz, copies, gets, w, out, out_hbm)
    copies.finish()


def pack_call(sz, after, weight, start, by=None):
    half = sz.half_j
    packed = (half, sz.blk_k, sz.groups * 128, sz.lgs * sz.chans)
    lines = (sz.lines * 128, sz.modes_y * sz.cpl)
    outs = [(shape(packed), True)]
    args = (after, weight)
    scratch = [pltpu.VMEM((half,) + weight.shape[2:], bf16), pltpu.VMEM(packed, bf16)]
    tables = by is not None
    if tables:
        outs.append((shape(lines), True))
        args += (by,)
        scratch += [pltpu.VMEM(by.shape, bf16), pltpu.VMEM(lines, bf16)]
    result = run(
        "pack",
        lambda *refs: pack_kernel(sz, start, tables, *refs),
        outs,
        [hbm] * len(args),
        args,
        scratch,
        2 * half + 2 * tables,
        0,
    )
    return result if tables else result[0]


def line_analysis(sz, r_ref, ya_ref, get_ya, fine=True):
    jk = sz.jk

    def total(sec, gy, start, step):
        result = None
        for gx in range(start, sz.n_gx, step):
            at = ((sec * sz.n_gx + gx) * sz.n_gy + gy) * jk
            part = r_ref[at : at + jk, :].astype(f32)
            result = part if result is None else result + part
        return result

    halves = [[], []]
    low = iota((jk, 128), 1) < 64
    for sec in range(2):
        for gy in range(sz.n_gy):
            if fine:
                a, b = total(sec, gy, 0, 2), total(sec, gy, 1, 2)
                halves[0].append(jnp.where(low, a, pltpu.roll(b, 64, 1)).astype(bf16))
                halves[1].append(jnp.where(low, pltpu.roll(a, 64, 1), b).astype(bf16))
            else:
                line = total(sec, gy, 0, 1).astype(bf16)
                for h in range(sz.groups):
                    halves[h].append(line[:, h * 128 : (h + 1) * 128])
    rows = jnp.concatenate([jnp.concatenate(half, axis=1) for half in halves], axis=0)
    if get_ya is not None:
        get_ya.wait()
    return nn(rows, ya_ref[...]).astype(bf16)


def diagonal(sz, count):
    shape = (count, sz.groups * 128)
    return iota(shape, 0) % 8 == (iota(shape, 1) % 128) // sz.cpl


def row_spread(sz):
    shape = (sz.jk * 8, sz.jk)
    return (iota(shape, 0) // 8 == iota(shape, 1)).astype(bf16)


def row_gather(sz):
    shape = (sz.jk, sz.jk * 8)
    return (iota(shape, 1) // 8 == iota(shape, 0)).astype(bf16)


def chan_lanes(sz):
    shape = (sz.groups * 128, sz.chans)
    lane = iota(shape, 0)
    return ((lane // 128) * sz.cpl + lane % sz.cpl == iota(shape, 1)).astype(bf16)


def to_blocks(sz, rows, lg):
    jk = sz.jk
    wide = jnp.concatenate(
        [rows[h * jk : (h + 1) * jk, lg * 128 : (lg + 1) * 128] for h in range(sz.groups)], axis=1
    )
    return jnp.where(diagonal(sz, jk * 8), nn(row_spread(sz), wide), 0.0)


def from_blocks(sz, blocks):
    jk = sz.jk
    pieces = []
    for block in blocks:
        kept = jnp.where(diagonal(sz, jk * 8), block, 0.0).astype(bf16)
        pieces.append(nn(row_gather(sz), kept).astype(bf16))
    return jnp.concatenate(
        [
            jnp.concatenate([piece[:, h * 128 : (h + 1) * 128] for piece in pieces], axis=1)
            for h in range(sz.groups)
        ],
        axis=0,
    )


def send_lines(sz, rows, ya_ref, out_ref):
    jk = sz.jk
    lines = nt(rows, ya_ref[...])
    low = iota((jk, 128), 1) < 64
    for sec in range(2):
        for gy in range(sz.n_gy):
            line = sec * sz.n_gy + gy
            a, b = [lines[h * jk : (h + 1) * jk, line * 128 : (line + 1) * 128] for h in range(2)]
            quarters = [
                jnp.where(low, a, pltpu.roll(b, 64, 1)).astype(bf16),
                jnp.where(low, pltpu.roll(a, 64, 1), b).astype(bf16),
            ]
            for gx in range(sz.n_gx):
                at = ((sec * sz.n_gx + gx) * sz.n_gy + gy) * jk
                out_ref[at : at + jk, :] = quarters[gx % 2]


def lane_group(sz):
    dims = (sz.lgs * sz.jk * 8, sz.lgs * sz.chans)
    return iota(dims, 0) // (sz.jk * 8) == iota(dims, 1) // sz.chans


def mix_kernel(sz, layer, turn, s_ref, r, ya_in, *rest):
    if layer == 0:
        low_hbm, high_hbm, *rest = rest
        spec_hbm, out, ya, w, spec_b, blk, mix, sems = rest[3:]
    else:
        ya = ya_in
        w, spec_hbm, out, spec_b, blk, mix, sems = rest
    copies = Copies(sems)
    get_ya = copies.start(ya_in, ya) if layer == 0 else None
    if layer == 0:
        get_w = copies.choose(s_ref[0] == 0, [(low_hbm.at[jj], high_hbm.at[jj], w.at[jj]) for jj in range(sz.half_j)])
    spec = line_analysis(sz, r, ya, get_ya, layer > 0)
    spec_b[...] = spec
    copies.send(spec_b, spec_hbm)
    count = sz.jk * 8
    width = sz.lgs * sz.chans
    rep = jnp.concatenate([chan_lanes(sz)] * sz.lgs, axis=1)
    blocks = [to_blocks(sz, spec, lg) for lg in range(sz.lgs)]
    if turn:
        flat = nn(jnp.concatenate(blocks, axis=0).astype(bf16), rep)
        mix[:, :width] = jnp.where(lane_group(sz), flat, 0.0)
        left_ref, right_ref, left_width = mix, blk, width
    else:
        for lg in range(sz.lgs):
            blk[lg * count : (lg + 1) * count, :] = blocks[lg]
        left_ref, right_ref, left_width = blk, mix, blk.shape[1]
    for jk in range(sz.jk):
        jj, kk = jk // sz.blk_k, jk % sz.blk_k
        if kk == 0 and layer == 0:
            get_w[jj].wait()
        at = [slice((lg * sz.jk + jk) * 8, (lg * sz.jk + jk + 1) * 8) for lg in range(sz.lgs)]
        left = jnp.concatenate([left_ref[a, :left_width] for a in at], axis=0).astype(bf16)
        part = nt(left, w[jj, kk]) if turn else nn(left, w[jj, kk])
        for lg, a in enumerate(at):
            right_ref[a, : part.shape[1]] = part[lg * 8 : (lg + 1) * 8]
    if not turn:
        kept_mix = jnp.where(lane_group(sz), mix[:, :width], 0.0).astype(bf16)
        full = nt(kept_mix, rep)
    else:
        full = blk[...]
    blocks = [full[lg * count : (lg + 1) * count] for lg in range(sz.lgs)]
    send_lines(sz, from_blocks(sz, blocks), ya, out)
    copies.finish()


def mix_call(sz, layer, turn, s, r, ya, weights, after=()):
    count = sz.jk * 8 * sz.lgs
    spec = (sz.groups * sz.jk, sz.modes_y * sz.cpl)
    line = (sz.modes, sz.thin)
    outs = [(shape(spec), True), (kept(line), False)]
    scratch = [pltpu.VMEM(spec, bf16)] + [pltpu.VMEM((count, sz.groups * 128), f32)] * 2
    if layer == 0:
        outs.append((kept(ya.shape), False))
        scratch = [pltpu.VMEM(weights[0].shape, bf16)] + scratch
        specs = [smem, vmem] + [hbm] * (3 + len(after))
    else:
        ya = near(ya)
        weights = [near(weights)]
        specs = [smem] + [vmem] * 3
    return run(
        "mix",
        lambda *refs: mix_kernel(sz, layer, turn, *refs),
        outs,
        specs,
        (s, r, ya, *weights, *after),
        scratch,
        sz.half_j + 2,
    )


def gate_kernel(sz, in_ref, after_hbm, out_ref):
    out_ref[...] = in_ref[...]


def gate_call(sz, value, after):
    (out,) = run(
        "gate",
        lambda *refs: gate_kernel(sz, *refs),
        [(kept(value.shape), False)],
        [vmem, hbm],
        (near(value), after),
        micros=0,
    )
    return out


def spec_kernel(sz, s_ref, r, ya, sv0_hbm, sv1_hbm, su1_hbm, mine, sends, before, sems):
    copies = Copies(sems)
    gets = [copies.start(src, before.at[at]) for at, src in enumerate((sv0_hbm, sv1_hbm, su1_hbm))]
    first = s_ref[0] == 0
    spec = line_analysis(sz, r, ya, None)
    for get in gets:
        get.wait()
    sv0, sv1, su1 = [before[at] for at in range(3)]
    sends[0] = jnp.where(first, sv1, sv0)
    sends[1] = jnp.where(first, su1, spec)
    mine[0] = jnp.where(first, sv0, sv1)
    mine[1] = jnp.where(first, spec, su1)


def spec_call(sz, s, r, sv0, sv1, su1, ya):
    spec = (sz.groups * sz.jk, sz.modes_y * sz.cpl)
    return run(
        "spec",
        lambda *refs: spec_kernel(sz, *refs),
        [(kept((2,) + spec), False), (kept((2,) + spec), False)],
        [smem, vmem, vmem, hbm, hbm, hbm],
        (s, r, near(ya), sv0, sv1, su1),
        [pltpu.VMEM((3,) + spec, bf16)],
        3,
    )


def turned_modes(sz, u_ref, layer):
    left = jnp.transpose(u_ref[...])
    half = sz.modes // 2
    if layer == 1:
        left = jnp.concatenate([left[:, half:], left[:, :half]], axis=1)
    return left


CHUNK = 1024


def cuts(sz):
    return [slice(at, at + CHUNK) for at in range(0, sz.wide, CHUNK)]


def small_parts(sz, s_ref, own_ref, other_ref, layer):
    chosen = jnp.where(s_ref[0] == layer, own_ref[...].astype(f32), other_ref[...].astype(f32)).astype(bf16)
    return chosen[: sz.chans], chosen[sz.chans :]


def field_copies(sz, copies, mine_hbm, other_hbm, field):
    return [
        copies.start(mine_hbm, field.at[:, : sz.cells]),
        copies.start(other_hbm, field.at[:, sz.cells :]),
    ]


def thirds(value):
    high = value.astype(bf16)
    rest = value - high.astype(f32)
    middle = rest.astype(bf16)
    return [high, middle, (rest - middle.astype(f32)).astype(bf16)]


def point_sums(sz, v, d):
    pairs = jnp.where(same_y(sz), nt(v, d), 0.0)
    bias = nt(jnp.ones((8, sz.wide), bf16), d)
    dims = (sz.chans, 3 * sz.thin)
    fold = (iota(dims, 1) % sz.thin // sz.fine == iota(dims, 0)).astype(bf16)
    pairs = nn(fold, jnp.concatenate(thirds(pairs), axis=0))
    part = sz.chans // 4
    rows = []
    for t in range(4):
        below = bias if t == 0 else jnp.zeros_like(bias)
        both = jnp.concatenate([pairs[t * part : (t + 1) * part], below], axis=0)
        rows.append(jnp.concatenate(thirds(both), axis=0))
    dims = (4 * sz.thin, 128)
    row = iota(dims, 0)
    place = (row // sz.thin * sz.chans + row % sz.thin // sz.fine == iota(dims, 1)).astype(bf16)
    total = nn(jnp.concatenate(rows, axis=1), place)
    count = part + 8
    return total[:count] + total[count : 2 * count] + total[2 * count :]


def forward_kernel(
    sz, s_ref, own_hbm, other_hbm, u, mine_hbm, next_hbm, bb_hbm, low_hbm, high_hbm, v, slope, bb, out, w, field, own_ref, other_ref, sems
):
    copies = Copies(sems)
    get_small = [copies.start(own_hbm, own_ref), copies.start(other_hbm, other_ref)]
    get_bb, get_v = [], []
    for at, cut in enumerate(cuts(sz)):
        get_bb.append(copies.start(bb_hbm.at[:, cut], bb.at[:, cut]))
        if at == 0:
            get_v = field_copies(sz, copies, mine_hbm, next_hbm, field)
    (get_w,) = copies.choose(s_ref[0] == 1, [(low_hbm, high_hbm, w)])
    for get in get_small:
        get.wait()
    weight, bias = small_parts(sz, s_ref, own_ref, other_ref, 0)
    matrix = point_matrix(sz, weight, True)
    column = nt(spread(sz), bias)[:, :1]
    left = turned_modes(sz, u, 0)
    for at, cut in enumerate(cuts(sz)):
        get_bb[at].wait()
        if cut.start % sz.cells == 0:
            get_v[cut.start // sz.cells].wait()
        pre = nn(left, bb[:, cut]) + nn(matrix, field[:, cut]) + column
        value, rate = activate(pre)
        v[:, cut] = value.astype(bf16)
        slope[:, cut] = rate
    send_analysis(sz, bb, v[...], out, 1)
    get_w.wait()


def forward_call(sz, s, mine, other, u, bb, own_small, other_small, low, high):
    field, line = (sz.thin, sz.wide), (sz.modes, sz.thin)
    return run(
        "forward",
        lambda *refs: forward_kernel(sz, *refs),
        [
            (kept(field), False),
            (kept(field, f32), False),
            (kept((sz.modes, sz.wide)), False),
            (kept(line), False),
            (kept(low.shape), False),
        ],
        [smem, hbm, hbm, vmem, hbm, hbm, hbm, hbm, hbm],
        (s, own_small, other_small, u, mine, other, bb, low, high),
        [pltpu.VMEM(field, bf16), pltpu.VMEM(own_small.shape, bf16), pltpu.VMEM(own_small.shape, bf16)],
        5 + len(cuts(sz)),
    )


def turn_kernel(sz, s_ref, own_ref, other_ref, u, v, bb, mine_hbm, next_hbm, d, sums, out, grad, sems):
    copies = Copies(sems)
    get_g = field_copies(sz, copies, mine_hbm, next_hbm, grad)
    weight, bias = small_parts(sz, s_ref, own_ref, other_ref, 1)
    matrix = point_matrix(sz, weight, True)
    column = nt(spread(sz), bias)[:, :1]
    left = turned_modes(sz, u, 1)
    for at, cut in enumerate(cuts(sz)):
        pre = nn(left, bb[:, cut]) + nn(matrix, v[:, cut]) + column
        _, rate = activate(pre)
        if at == 0:
            for get in get_g:
                get.wait()
        d[:, cut] = (grad[:, cut].astype(f32) * rate).astype(bf16)
    send_analysis(sz, bb, d[...], out, 1)
    sums[...] = point_sums(sz, v[...], d[...])


def turn_call(sz, s, mine, other, v, u, bb, own_small, other_small):
    field, line = (sz.thin, sz.wide), (sz.modes, sz.thin)
    return run(
        "turn",
        lambda *refs: turn_kernel(sz, *refs),
        [(kept(field), False), (kept((sz.chans // 4 + 8, 128), f32), False), (kept(line), False)],
        [smem, vmem, vmem, vmem, vmem, vmem, hbm, hbm],
        (s, own_small, other_small, u, near(v), near(bb), mine, other),
        [pltpu.VMEM(field, bf16)],
        2,
    )


def pieces(sz, value):
    part = sz.chans // 4
    high = value.astype(bf16).astype(f32)
    low = value - high
    bias = jnp.where(iota((8, 128), 0) < 4, high[part:], low[part:])
    return jnp.concatenate([high[:part], low[:part], bias], axis=0).astype(bf16)


def back_kernel(
    sz, s_ref, own_ref, other_ref, u, d, slope, bb, sums, mine_hbm, next_hbm, parts, out, new, field, sems
):
    copies = Copies(sems)
    get_v = field_copies(sz, copies, mine_hbm, next_hbm, field)
    weight, _ = small_parts(sz, s_ref, own_ref, other_ref, 1)
    matrix = point_matrix(sz, weight, False)
    left = turned_modes(sz, u, 1)
    for cut in cuts(sz):
        grad = (nn(left, bb[:, cut]) + nn(matrix, d[:, cut])).astype(bf16).astype(f32)
        new[:, cut] = (grad * slope[:, cut]).astype(bf16)
    for get in get_v:
        get.wait()
    send_analysis(sz, bb, new[...], out, 0)
    first = point_sums(sz, field[...], new[...])
    half = sz.places // 2
    for layer, value in enumerate((first, sums[...])):
        block = pieces(sz, value)
        for place in range(half):
            parts[layer * half + place] = block


def back_call(sz, s, mine, other, d, slope, u, bb, sums, own_small, other_small):
    parts, line, field = (sz.places, sz.chans // 2 + 8, 128), (sz.modes, sz.thin), (sz.thin, sz.wide)
    return run(
        "back",
        lambda *refs: back_kernel(sz, *refs),
        [(kept(parts), False), (kept(line), False)],
        [smem] + [vmem] * 7 + [hbm, hbm],
        (s, own_small, other_small, u, near(d), near(slope), near(bb), near(sums), mine, other),
        [pltpu.VMEM(field, bf16), pltpu.VMEM(field, bf16)],
        2,
    )


def finish_kernel(sz, parts_ref, after_ref, point_ref, bias_ref):
    total = jnp.sum(parts_ref[...].astype(f32), axis=0)
    part = sz.chans // 4
    bias_ref[...] = (total[2 * part : 2 * part + 1] + total[2 * part + 4 : 2 * part + 5])[:, : sz.chans]
    total = total[:part] + total[part : 2 * part]
    for t in range(4):
        point_ref[0, t * part : (t + 1) * part, :] = total[:part, t * sz.chans : (t + 1) * sz.chans]


def finish_call(sz, parts, after):
    return pl.pallas_call(
        lambda *refs: finish_kernel(sz, *refs),
        out_shape=(shape((1, sz.chans, sz.chans), f32), shape((1, sz.chans), f32)),
        in_specs=[vmem, hbm],
        out_specs=(vmem, vmem),
        compiler_params=pltpu.CompilerParams(vmem_limit_bytes=limit),
        name="finish",
    )(parts, far(after))


def outer_kernel(sz, mine_ref, theirs_ref, out_ref, left_ref, right_ref):
    jk, groups, kk_count = sz.jk, sz.groups, sz.blk_k
    step = pl.program_id(0)

    def prepare(side, sv, su):
        sv = sv.astype(f32)
        for jj in range(sz.half_j):
            place = side * sz.half_j + jj
            rows = jnp.concatenate(
                [sv[h * jk + jj * kk_count : h * jk + (jj + 1) * kk_count] for h in range(groups)], axis=0
            )
            left_ref[place] = jnp.transpose(rows).astype(bf16)
        for lg in range(sz.lgs):
            flat = nn(to_blocks(sz, su, lg).astype(bf16), chan_lanes(sz))
            for at in range(jk):
                place = side * sz.half_j + at // kk_count
                right_ref[place, at % kk_count, lg * 8 : (lg + 1) * 8, :] = flat[at * 8 : (at + 1) * 8]

    @pl.when(step == 0)
    def _():
        prepare(0, mine_ref[0], mine_ref[1])

    @pl.when(step == 1)
    def _():
        prepare(1, theirs_ref[0], theirs_ref[1])

    dims = (groups * kk_count, groups * kk_count * 128)
    spread_lanes = (iota(dims, 0) == iota(dims, 1) // 128).astype(bf16)
    each = out_ref.shape[1]
    for sub in range(each):
        columns = nn(left_ref[step * each + sub], spread_lanes)
        for kk in range(kk_count):
            for ll in range(sz.modes_y):
                row = right_ref[step * each + sub, kk, ll : ll + 1, :]
                for h in range(groups):
                    at = (h * kk_count + kk) * 128
                    part = columns[ll * sz.cpl : (ll + 1) * sz.cpl, at : at + sz.chans] * row
                    out_ref[0, sub, kk, ll, h * sz.cpl : (h + 1) * sz.cpl, :] = part


def outer_call(sz, mine, theirs):
    each = max(1, sz.half_j // 2)
    wide = sz.modes_y * sz.cpl
    return pl.pallas_call(
        lambda *refs: outer_kernel(sz, *refs),
        grid=(sz.blk_j // each,),
        out_shape=pltpu.HBM((1, sz.blk_j, sz.blk_k, sz.modes_y, sz.chans, sz.chans), f32),
        in_specs=[vmem] * 2,
        out_specs=pl.BlockSpec((1, each, sz.blk_k, sz.modes_y, sz.chans, sz.chans), lambda i: (0, i, 0, 0, 0, 0)),
        scratch_shapes=[
            pltpu.VMEM((sz.blk_j, wide, sz.groups * sz.blk_k), bf16),
            pltpu.VMEM((sz.blk_j, sz.blk_k, sz.modes_y, sz.chans), f32),
        ],
        compiler_params=pltpu.CompilerParams(vmem_limit_bytes=limit),
        cost_estimate=pl.CostEstimate(flops=0, transcendentals=0, bytes_accessed=20000000),
        name="outer",
    )(near(mine), theirs)


def exchange(block):
    return lax.all_to_all(block, AXES, split_axis=0, concat_axis=0, tiled=True)


def swap(block):
    return lax.ppermute(block, "section", [(0, 1), (1, 0)])


def swap_near(sz, block):
    return lax.ppermute(block, "gx", [(i, i ^ 1) for i in range(sz.n_gx)])


def local(ends, spectral_weight, point_weight, point_bias):
    sz = Sizes(ends, spectral_weight)
    section = lax.axis_index("section")
    first = section == 0
    s = section.astype(jnp.int32).reshape(1)

    def half(field, which):
        part = lax.dynamic_slice_in_dim(field, which * sz.len_y, sz.len_y, axis=2)
        return jnp.swapaxes(part, 1, 2).reshape(sz.rows, sz.cells)

    bx, bz, by = [jnp.asarray(t.astype(ml_dtypes.bfloat16)) for t in mode_tables(sz)]
    send = half(ends[0], 1 - section)
    send, later = lax.optimization_barrier((send, ends[0]))
    recv = swap(send)
    keep = half(later, section)
    gx = lax.axis_index("gx").astype(jnp.int32)
    gx = jnp.stack([gx, gx + 1 - 2 * (gx % 2)])
    bb = tables_call(sz, gx, bx, bz)
    own_small = jnp.concatenate([point_weight[0], jnp.broadcast_to(point_bias, (16, sz.chans))], axis=0)
    other_small = swap(own_small)
    mine_v, send_v, raw_g, out, high = first_call(sz, s, gx, keep, recv, bb, spectral_weight)
    high = swap(high)
    next_v = swap_near(sz, send_v)
    r = exchange(out)
    mine_g, send_g = split_call(sz, gx, raw_g, mine_v)
    next_g = swap_near(sz, send_g)
    low, ya = pack_call(sz, mine_v, spectral_weight, 0, by)
    bb = wide_call(sz, gx, bx, bz, mine_v)
    sv0, out, ya = mix_call(sz, 0, False, s, r, ya, (low, high), (other_small, bb, next_v))
    v1, slope0, bb, out, w1 = forward_call(sz, s, mine_v, next_v, exchange(out), bb, own_small, other_small, low, high)
    sv1, out = mix_call(sz, 1, False, s, exchange(out), ya, w1)
    out = gate_call(sz, out, next_g)
    d1, sums, out = turn_call(sz, s, mine_g, next_g, v1, exchange(out), bb, own_small, other_small)
    su1, out = mix_call(sz, 1, True, s, exchange(out), ya, w1)
    parts, out = back_call(sz, s, mine_v, next_v, d1, slope0, exchange(out), bb, sums, own_small, other_small)
    r, parts = lax.optimization_barrier((exchange(out), parts))
    mine, send = spec_call(sz, s, r, sv0, sv1, su1, ya)
    theirs = swap(send)
    parts = lax.all_to_all(parts, AXES, split_axis=0, concat_axis=0, tiled=True)
    spectral_grad = outer_call(sz, mine, theirs)
    point_grad, bias_grad = finish_call(sz, parts, spectral_grad)
    return (spectral_grad, point_grad, bias_grad)


def solution(mesh):
    return jax.shard_map(
        local,
        mesh=mesh,
        in_specs=(
            P("section", None, "gx", "gy", None),
            P("section", "gy", "gx", None, None, None),
            P("section", None, None),
            P("section", None),
        ),
        out_specs=(
            P("section", "gy", "gx", None, None, None),
            P("section", None, None),
            P("section", None),
        ),
        check_vma=False,
    )
```
